128 devices in a mesh: dp: 16 (over z, y), tensor: 8 (over x, core).
Axes of the slice: x: 4, y: 4, z: 4, core: 2. Of those that a mesh axis runs over, the one named last changes fastest.
Arguments:
- dense: bfloat16 [3072, 2048], P('dp'), may hold values from -8 to 8
- bottom_weight: bfloat16 [2048, 16384], P(None, 'tensor'), may hold values from -0.125 to 0.125
- bottom_bias: float32 [16384], P('tensor'), may hold values from -3 to 3
- cross_blocks: bfloat16 [80, 512, 512], P('tensor', 'dp'), may hold values from -0.25 to 0.25
- cross_bias: float32 [16384], P('tensor'), may hold values from -3 to 3
- cotangent: bfloat16 [3072, 16384], P('dp', 'tensor'), may hold values from -6 to 6
- in_blocks: int32 [8, 10], replicated, may hold values from 0 to 31, as said below
- out_blocks: int32 [8, 10], replicated, may hold values from 0 to 31, as said below
- live_slots: int32 [8], replicated, may hold values from 2 to 10, as said below
Outputs:
- cross_out: bfloat16 [3072, 16384], P('dp', 'tensor')
- grad_bottom: float32 [2048, 16384], P('dp', 'tensor')
- grad_bias_bottom: float32 [16384], P('tensor')
- grad_blocks: float32 [80, 512, 512], P('tensor', 'dp')
- grad_bias: float32 [16384], P('tensor')
The draws below stay inside these ranges and needn't reach their ends.
Inputs may be any that keep to these rules, and one draw needn't show every extreme that they name: `in_blocks`: among the live slots of one tensor device, at most 2 have input blocks held by any one tensor device (blocks s * 16384 / (512 * 8) onward for device s), and this most is reached in every draw. `out_blocks`: among the live slots of one tensor device, at most 2 have output blocks held by any one tensor device, and this most is reached in every draw. `live_slots`: some tensor device has all 10 slots live.
All inputs are finite; a program needn't handle non-finite values.
Results may differ from the reference program's by a relative error of at most 0.014.
Values may be sent and summed in bfloat16 or wider, within the bound.
A program may use at most 128 MiB of HBM per device.

```python
import jax
import jax.numpy as jnp
from jax import lax

DENSE = 2048
WIDTH = 16384
BLK = 512
B_DEV = 192
SLOTS = 10
SLOTS_ALL = 80
BATCH = 3072
N_DP = 16
N_TENSOR = 8


def slot_tables(key):
    per_device = WIDTH // BLK // N_TENSOR
    subkeys = jax.random.split(jax.random.fold_in(key, 7), 6)
    perm_out = jax.vmap(lambda subkey: jax.random.permutation(subkey, N_TENSOR))(jax.random.split(subkeys[0], N_TENSOR))
    perm_in = jax.vmap(lambda subkey: jax.random.permutation(subkey, N_TENSOR))(jax.random.split(subkeys[1], N_TENSOR))
    position = jnp.arange(SLOTS)
    owner_out = perm_out[:, position % N_TENSOR]
    offsets = jax.random.randint(subkeys[2], (N_TENSOR, 1), 0, per_device)
    local_out = (offsets + position[None, :] // N_TENSOR) % per_device
    owner_in = perm_in[:, position % N_TENSOR]
    local_in = jax.random.randint(subkeys[3], (N_TENSOR, SLOTS), 0, per_device)
    counts = jax.random.randint(subkeys[4], (N_TENSOR,), 2, SLOTS + 1)
    busiest = jax.random.randint(subkeys[5], (), 0, N_TENSOR)
    counts = jnp.where(jnp.arange(N_TENSOR) == busiest, SLOTS, counts)
    inputs = (owner_in * per_device + local_in).astype(jnp.int32)
    outputs = (owner_out * per_device + local_out).astype(jnp.int32)
    return (inputs, outputs, counts.astype(jnp.int32))


def draw_in_blocks(key, part):
    return slot_tables(key)[0]


def draw_out_blocks(key, part):
    return slot_tables(key)[1]


def draw_live_slots(key, part):
    return slot_tables(key)[2]


def spiked(array, rng, source, target, shards_of, factor):
    def block_of(dim):
        return (jnp.arange(array.shape[dim]) // (array.shape[dim] // shards_of)).reshape((-1,) + (1,) * (array.ndim - 1 - dim))

    near = jax.random.permutation(rng, shards_of)[block_of(target)]
    far = (block_of(target) + shards_of // 2) % shards_of
    return jnp.where((block_of(source) == near) | (block_of(source) == far), factor * array, array)


def steps_of(rng, shape, pieces, low, largest):
    factor_of, own = 1.0, jax.random.fold_in(rng, 6)
    for dim, parts in pieces:
        steps = jnp.exp(jax.random.uniform(jax.random.fold_in(own, dim), (parts,), jnp.float32, low / len(pieces), largest / len(pieces)))
        factor_of = factor_of * jnp.repeat(steps, shape[dim] // parts).reshape([-1 if axis == dim else 1 for axis in range(len(shape))])
    return factor_of


def bell_draw(stream_key, shape, spread, limit, cuts=(), kind=jnp.bfloat16):
    entries = jax.random.normal(stream_key, shape, jnp.float32) * spread
    if len(cuts) > 0:
        entries = steps_of(stream_key, shape, cuts, -0.22, 0.18) * entries
    return jnp.clip(entries, min=-limit, max=limit).astype(kind)


def gaussian_with(stream_key, extent, deviation, bound, pieces, heavy, dtype=jnp.bfloat16):
    values = deviation * jax.random.normal(stream_key, extent, jnp.float32)
    if pieces:
        values = values * steps_of(stream_key, extent, pieces, -0.22, 0.18)
    return jnp.clip(spiked(values, jax.random.fold_in(stream_key, 3), *heavy), -bound, bound).astype(dtype)


def setup_inputs(seed: int = 0) -> dict:
    splits = jax.random.split(jax.random.key(seed), 10)
    dense = gaussian_with(splits[0], (BATCH, DENSE), 1.0, 8.0, ((0, 16),), (0, 1, 16, 2.0))
    bottom_weight = bell_draw(splits[1], (DENSE, WIDTH), DENSE ** -0.5, 0.125, ((1, 8),))
    bottom_bias = bell_draw(splits[2], (WIDTH,), 0.5, 3.0, ((0, 8),), jnp.float32)
    cross_blocks = bell_draw(splits[3], (SLOTS_ALL, BLK, BLK), BLK ** -0.5, 0.25, ((0, 8), (1, 16)))
    cross_bias = bell_draw(splits[4], (WIDTH,), 0.5, 3.0, ((0, 8),), jnp.float32)
    cotangent = bell_draw(splits[5], (BATCH, WIDTH), 1.0, 6.0, ((0, 16), (1, 8)))
    in_blocks = draw_in_blocks(jax.random.fold_in(splits[9], 71), 0)
    out_blocks = draw_out_blocks(jax.random.fold_in(splits[9], 71), 0)
    live_slots = draw_live_slots(jax.random.fold_in(splits[9], 71), 0)
    return {"dense": dense, "bottom_weight": bottom_weight, "bottom_bias": bottom_bias, "cross_blocks": cross_blocks, "cross_bias": cross_bias, "cotangent": cotangent, "in_blocks": in_blocks, "out_blocks": out_blocks, "live_slots": live_slots}


def reference(dense, bottom_weight, bottom_bias, cross_blocks, cross_bias, cotangent, in_blocks, out_blocks, live_slots):
    preact = jnp.dot(dense, bottom_weight, preferred_element_type=jnp.float32) + bottom_bias
    start = jax.nn.silu(preact).astype(jnp.bfloat16)
    start_wide = start.astype(jnp.float32)
    inputs_all = in_blocks.reshape(-1).astype(jnp.int32)
    outputs_all = out_blocks.reshape(-1).astype(jnp.int32)
    alive = (jnp.arange(SLOTS)[None, :] < live_slots[:, None]).reshape(-1).astype(jnp.float32)

    def forward_slot(mixed, item):
        column, target, switch, weight_block = item
        taken = lax.dynamic_slice_in_dim(start, column * BLK, BLK, 1)
        product = jnp.dot(taken, weight_block, preferred_element_type=jnp.float32).astype(jnp.bfloat16)
        product = lax.optimization_barrier(product)
        product = product.astype(jnp.float32) * switch
        current = lax.dynamic_slice_in_dim(mixed, target * BLK, BLK, 1)
        mixed = lax.dynamic_update_slice_in_dim(mixed, current + product, target * BLK, 1)
        return mixed, None

    mixed, unused = lax.scan(forward_slot, jnp.zeros((BATCH, WIDTH), jnp.float32), (inputs_all, outputs_all, alive, cross_blocks))
    mixed = mixed + cross_bias
    cross_out = (start_wide * mixed + start_wide).astype(jnp.bfloat16)
    cot_wide = cotangent.astype(jnp.float32)
    grad_mixed = cot_wide * start_wide
    grad_mixed_low = grad_mixed.astype(jnp.bfloat16)
    grad_bias = jnp.sum(grad_mixed, axis=0)

    def backward_slot(grad_start, item):
        column, target, switch, weight_block = item
        taken = lax.dynamic_slice_in_dim(start, column * BLK, BLK, 1)
        upstream = lax.dynamic_slice_in_dim(grad_mixed_low, target * BLK, BLK, 1)
        back = jnp.dot(upstream, weight_block.T, preferred_element_type=jnp.float32).astype(jnp.bfloat16)
        back = lax.optimization_barrier(back)
        back = back.astype(jnp.float32) * switch
        current = lax.dynamic_slice_in_dim(grad_start, column * BLK, BLK, 1)
        grad_start = lax.dynamic_update_slice_in_dim(grad_start, current + back, column * BLK, 1)
        taken_groups = taken.astype(jnp.float32).reshape(N_DP, B_DEV, BLK)
        upstream_groups = upstream.astype(jnp.float32).reshape(N_DP, B_DEV, BLK)
        partial_grads = jnp.einsum("nbi,nbj->nij", taken_groups, upstream_groups, precision=lax.Precision.HIGHEST).astype(jnp.bfloat16)
        partial_grads = lax.optimization_barrier(partial_grads)
        block_grad = jnp.sum(partial_grads.astype(jnp.float32), axis=0) * switch
        return grad_start, block_grad

    grad_start, grad_blocks = lax.scan(backward_slot, jnp.zeros((BATCH, WIDTH), jnp.float32), (inputs_all, outputs_all, alive, cross_blocks))
    grad_start = grad_start + cot_wide * mixed + cot_wide
    sigma = jax.nn.sigmoid(preact)
    grad_pre = grad_start * sigma * (1.0 + preact * (1.0 - sigma))
    grad_pre_low = grad_pre.astype(jnp.bfloat16)
    grad_bias_bottom = jnp.sum(grad_pre, axis=0)

    def bottom_group(total, item):
        dense_group, grad_group = item
        partial_grad = jnp.dot(dense_group.T, grad_group, preferred_element_type=jnp.float32).astype(jnp.bfloat16)
        partial_grad = lax.optimization_barrier(partial_grad)
        return total + partial_grad.astype(jnp.float32), None

    grad_bottom, unused = lax.scan(bottom_group, jnp.zeros((DENSE, WIDTH), jnp.float32), (dense.reshape(N_DP, B_DEV, DENSE), grad_pre_low.reshape(N_DP, B_DEV, WIDTH)))
    return cross_out, grad_bottom, grad_bias_bottom, grad_blocks, grad_bias
```

```python
import jax
import jax.numpy as jnp
from jax import lax
from jax.sharding import PartitionSpec as P

BLK = 512
SLOTS = 10
CAP = 2


def slot_ranks(owner, alive):
    order = jnp.arange(owner.shape[1])
    earlier = order[None, :] < order[:, None]
    same = (owner[:, :, None] == owner[:, None, :]) & alive[:, None, :] & earlier[None, :, :]
    return jnp.sum(same.astype(jnp.int32), axis=2)


def send_table(owner, rank, alive, me, capacity):
    match = (
        (owner == me)[:, None, :]
        & alive[:, None, :]
        & (rank[:, None, :] == jnp.arange(capacity)[None, :, None])
    )
    chosen = jnp.sum(match.astype(jnp.int32) * jnp.arange(owner.shape[1])[None, None, :], axis=2)
    filled = jnp.any(match, axis=2)
    return chosen, filled


def pack_local(local_blocks, table_local, filled):
    rows = local_blocks.shape[0]
    picked = jnp.take(local_blocks, table_local.reshape(-1), axis=1)
    picked = picked * filled.reshape(-1)[None, :, None].astype(picked.dtype)
    return picked.reshape(rows, table_local.shape[0], table_local.shape[1] * BLK)


def pack_parts(parts, chosen, filled):
    picked = jnp.take(parts, chosen.reshape(-1), axis=1) * filled.reshape(-1)[None, :, None].astype(
        parts.dtype
    )
    return picked.reshape(parts.shape[0], chosen.shape[0], chosen.shape[1] * parts.shape[2])


def collect_parts(received, owner, local, rank, alive, target, capacity, per_device):
    row_count, groups, span_width = received.shape
    block_width = span_width // capacity
    match = ((owner == target) & alive)[:, :, None] & (
        rank[:, :, None] == jnp.arange(capacity)[None, None, :]
    )
    matches = match[:, :, :, None] & (
        local[:, :, None, None] == jnp.arange(per_device)[None, None, None, :]
    )
    onehot = (
        jnp.sum(matches.astype(jnp.int32), axis=1)
        .reshape(groups * capacity, per_device)
        .astype(jnp.bfloat16)
    )
    flattened = received.reshape(row_count, groups * capacity, block_width)
    summed = jnp.einsum("rib,il->rlb", flattened, onehot, preferred_element_type=jnp.float32)
    return summed.reshape(row_count, per_device * block_width)


def post_table(owner_mine, rank_mine, alive_mine, groups, capacity):
    match = (
        (owner_mine[None, None, :] == jnp.arange(groups)[:, None, None])
        & (rank_mine[None, None, :] == jnp.arange(capacity)[None, :, None])
        & alive_mine[None, None, :]
    )
    chosen = jnp.sum(match.astype(jnp.int32) * jnp.arange(owner_mine.shape[0])[None, None, :], axis=2)
    filled = jnp.any(match, axis=2)
    return (chosen, filled)


def on_device(
    dense,
    bottom_weight,
    bottom_bias,
    cross_blocks,
    cross_bias,
    cotangent,
    in_blocks,
    out_blocks,
    live_slots,
):
    groups = lax.axis_size("tensor")
    mine = lax.axis_index("tensor")
    row_count = dense.shape[0]
    local_width = bottom_weight.shape[1]
    per_device = local_width // BLK
    capacity = CAP
    weights = lax.all_gather(cross_blocks, "dp", axis=1, tiled=True)
    preact = jnp.dot(dense, bottom_weight, preferred_element_type=jnp.float32) + bottom_bias
    start = jax.nn.silu(preact).astype(jnp.bfloat16)
    start_wide = start.astype(jnp.float32)
    cot_wide = cotangent.astype(jnp.float32)
    grad_mixed = cot_wide * start_wide
    grad_mixed_low = grad_mixed.astype(jnp.bfloat16)
    grad_bias = lax.psum(jnp.sum(grad_mixed, axis=0), "dp")
    alive = jnp.arange(SLOTS)[None, :] < live_slots[:, None]
    alive_mine = alive[mine]
    switch = alive_mine.astype(jnp.bfloat16)[None, :, None]
    in_owner = in_blocks // per_device
    in_local = in_blocks % per_device
    out_owner = out_blocks // per_device
    out_local = out_blocks % per_device
    in_rank = slot_ranks(in_owner, alive)
    out_rank = slot_ranks(out_owner, alive)
    in_chosen, in_filled = send_table(in_owner, in_rank, alive, mine, capacity)
    out_chosen, out_filled = send_table(out_owner, out_rank, alive, mine, capacity)
    in_pick = jnp.take_along_axis(in_local, in_chosen.reshape(groups, -1), axis=1)
    out_pick = jnp.take_along_axis(out_local, out_chosen.reshape(groups, -1), axis=1)
    outgoing = jnp.concatenate(
        [
            pack_local(start.reshape(row_count, per_device, BLK), in_pick, in_filled),
            pack_local(grad_mixed_low.reshape(row_count, per_device, BLK), out_pick, out_filled),
        ],
        axis=2,
    )
    arrived = lax.all_to_all(outgoing, "tensor", split_axis=1, concat_axis=1, tiled=True)
    arrived = arrived.reshape(row_count, groups * 2 * capacity, BLK)
    in_index = in_owner[mine] * (2 * capacity) + jnp.minimum(in_rank[mine], capacity - 1)
    out_index = out_owner[mine] * (2 * capacity) + capacity + jnp.minimum(out_rank[mine], capacity - 1)
    fetched = jnp.take(arrived, in_index, axis=1) * switch
    upstream = jnp.take(arrived, out_index, axis=1) * switch
    block_terms = jnp.einsum("rki,rkj->kij", fetched, upstream, preferred_element_type=jnp.float32)
    grad_blocks = lax.psum_scatter(
        block_terms.astype(jnp.bfloat16), "dp", scatter_dimension=1, tiled=True
    ).astype(jnp.float32)
    product = jnp.einsum("rki,kij->rkj", fetched, weights, preferred_element_type=jnp.float32)
    parts = product.astype(jnp.bfloat16) * switch
    backward = jnp.einsum("rkj,kij->rki", upstream, weights, preferred_element_type=jnp.float32)
    back_parts = backward.astype(jnp.bfloat16) * switch
    chosen_out, filled_out = post_table(out_owner[mine], out_rank[mine], alive_mine, groups, capacity)
    chosen_in, filled_in = post_table(in_owner[mine], in_rank[mine], alive_mine, groups, capacity)
    returned = lax.all_to_all(
        jnp.concatenate(
            [
                pack_parts(parts, chosen_out, filled_out),
                pack_parts(back_parts, chosen_in, filled_in),
            ],
            axis=2,
        ),
        "tensor",
        split_axis=1,
        concat_axis=1,
        tiled=True,
    )
    arrived_parts = returned[:, :, : capacity * BLK]
    arrived_back = returned[:, :, capacity * BLK :]
    mixed = (
        collect_parts(arrived_parts, out_owner, out_local, out_rank, alive, mine, capacity, per_device)
        + cross_bias
    )
    cross_out = (start_wide * mixed + start_wide).astype(jnp.bfloat16)
    grad_start = collect_parts(
        arrived_back, in_owner, in_local, in_rank, alive, mine, capacity, per_device
    )
    grad_start = grad_start + cot_wide * mixed + cot_wide
    sigma = jax.nn.sigmoid(preact)
    grad_pre = grad_start * sigma * (1.0 + preact * (1.0 - sigma))
    grad_pre_low = grad_pre.astype(jnp.bfloat16)
    grad_bottom = lax.psum_scatter(
        lax.dot_general(
            dense, grad_pre_low, (((0,), (0,)), ((), ())), preferred_element_type=jnp.float32
        ).astype(jnp.bfloat16),
        "dp",
        scatter_dimension=0,
        tiled=True,
    ).astype(jnp.float32)
    grad_bias_bottom = lax.psum(jnp.sum(grad_pre, axis=0), "dp")
    return (cross_out, grad_bottom, grad_bias_bottom, grad_blocks, grad_bias)


def solution(mesh):
    return jax.shard_map(
        on_device,
        mesh=mesh,
        in_specs=(
            P("dp", None),
            P(None, "tensor"),
            P("tensor"),
            P("tensor", "dp", None),
            P("tensor"),
            P("dp", "tensor"),
            P(),
            P(),
            P(),
        ),
        out_specs=(
            P("dp", "tensor"),
            P("dp", "tensor"),
            P("tensor"),
            P("tensor", "dp", None),
            P("tensor"),
        ),
        check_vma=False,
    )
```

```python
import jax
import jax.numpy as jnp
from jax import lax
from jax.sharding import PartitionSpec as P

BLK = 512
SLOTS = 10


def slot_ranks(owner, alive):
    order = jnp.arange(owner.shape[1])
    earlier = order[None, :] < order[:, None]
    same = (owner[:, :, None] == owner[:, None, :]) & alive[:, None, :] & earlier[None, :, :]
    return jnp.sum(same.astype(jnp.int32), axis=2)


def post_table(owner_mine, rank_mine, alive_mine, groups, capacity):
    slot_count = owner_mine.shape[0]
    match = (
        (owner_mine[None, None, :] == jnp.arange(groups)[:, None, None])
        & (rank_mine[None, None, :] == jnp.arange(capacity)[None, :, None])
        & alive_mine[None, None, :]
    )
    chosen = jnp.sum(match.astype(jnp.int32) * jnp.arange(slot_count)[None, None, :], axis=2)
    filled = jnp.any(match, axis=2)
    return (chosen, filled)


def pack_parts(parts, chosen, filled):
    picked = jnp.take(parts, chosen.reshape(-1), axis=1) * filled.reshape(-1)[None, :, None].astype(
        parts.dtype
    )
    return picked.reshape(parts.shape[0], chosen.shape[0], chosen.shape[1] * parts.shape[2])


def collect_parts(received, owner, local, rank, alive, target, capacity, per_device):
    row_count, groups, span_width = received.shape
    block_width = span_width // capacity
    match = ((owner == target) & alive)[:, :, None] & (
        rank[:, :, None] == jnp.arange(capacity)[None, None, :]
    )
    matches = match[:, :, :, None] & (
        local[:, :, None, None] == jnp.arange(per_device)[None, None, None, :]
    )
    onehot = (
        jnp.sum(matches.astype(jnp.int32), axis=1)
        .reshape(groups * capacity, per_device)
        .astype(jnp.bfloat16)
    )
    flattened = received.reshape(row_count, groups * capacity, block_width)
    summed = jnp.einsum("rib,il->rlb", flattened, onehot, preferred_element_type=jnp.float32)
    return summed.reshape(row_count, per_device * block_width)


def ring_gather(x, axis, n):
    half = x.shape[0] // 2
    right = [(i, (i + 1) % n) for i in range(n)]
    left = [(i, (i - 1) % n) for i in range(n)]
    cur_a, cur_b = x[:half], x[half:]
    outs_a, outs_b = [cur_a], [cur_b]
    for _ in range(1, n):
        cur_a = lax.ppermute(cur_a, axis, right)
        cur_b = lax.ppermute(cur_b, axis, left)
        outs_a.append(cur_a)
        outs_b.append(cur_b)
    return jnp.stack(outs_a), jnp.stack(outs_b)


def take_blocks(stack_a, stack_b, owner, local, me, n):
    steps, half, width = stack_a.shape
    blocks_a = stack_a.reshape(steps, half, width // BLK, BLK)
    blocks_b = stack_b.reshape(steps, half, width // BLK, BLK)
    step_a = (me - owner) % n
    step_b = (owner - me) % n
    top = blocks_a[step_a, :, local, :]
    bottom = blocks_b[step_b, :, local, :]
    return jnp.transpose(jnp.concatenate([top, bottom], axis=1), (1, 0, 2))


def on_device(
    dense,
    bottom_weight,
    bottom_bias,
    cross_blocks,
    cross_bias,
    cotangent,
    in_blocks,
    out_blocks,
    live_slots,
):
    groups = lax.axis_size("tensor")
    mine = lax.axis_index("tensor")
    row_count = dense.shape[0]
    local_width = bottom_weight.shape[1]
    per_device = local_width // BLK
    capacity = -(-SLOTS // groups)
    preact = jnp.dot(dense, bottom_weight, preferred_element_type=jnp.float32) + bottom_bias
    start = jax.nn.silu(preact).astype(jnp.bfloat16)
    start_wide = start.astype(jnp.float32)
    cot_wide = cotangent.astype(jnp.float32)
    grad_mixed = cot_wide * start_wide
    grad_mixed_low = grad_mixed.astype(jnp.bfloat16)
    alive = jnp.arange(SLOTS)[None, :] < live_slots[:, None]
    alive_mine = alive[mine]
    switch = alive_mine.astype(jnp.bfloat16)[None, :, None]
    in_owner = in_blocks // per_device
    in_local = in_blocks % per_device
    out_owner = out_blocks // per_device
    out_local = out_blocks % per_device
    in_rank = slot_ranks(in_owner, alive)
    out_rank = slot_ranks(out_owner, alive)
    combo = jnp.concatenate([start, grad_mixed_low], axis=1)
    stack_a, stack_b = ring_gather(combo, "tensor", groups)
    fetched = take_blocks(stack_a, stack_b, in_owner[mine], in_local[mine], mine, groups)
    taken = fetched
    product = jnp.einsum(
        "rki,kij->rkj",
        taken,
        lax.all_gather(cross_blocks, "dp", axis=1, tiled=True),
        preferred_element_type=jnp.float32,
    )
    parts = product.astype(jnp.bfloat16) * switch
    chosen_out, filled_out = post_table(
        out_owner[mine], out_rank[mine], alive_mine, groups, capacity
    )
    arrived_parts = lax.all_to_all(
        pack_parts(parts, chosen_out, filled_out), "tensor", split_axis=1, concat_axis=1, tiled=True
    )
    mixed = (
        collect_parts(
            arrived_parts, out_owner, out_local, out_rank, alive, mine, capacity, per_device
        )
        + cross_bias
    )
    cross_out = (start_wide * mixed + start_wide).astype(jnp.bfloat16)
    upstream = take_blocks(
        stack_a, stack_b, out_owner[mine], out_local[mine] + per_device, mine, groups
    )
    upstream = upstream * switch
    backward = jnp.einsum(
        "rkj,kij->rki",
        upstream,
        lax.all_gather(cross_blocks, "dp", axis=1, tiled=True),
        preferred_element_type=jnp.float32,
    )
    back_parts = backward.astype(jnp.bfloat16)
    chosen_in, filled_in = post_table(in_owner[mine], in_rank[mine], alive_mine, groups, capacity)
    arrived_back = lax.all_to_all(
        pack_parts(back_parts, chosen_in, filled_in),
        "tensor",
        split_axis=1,
        concat_axis=1,
        tiled=True,
    )
    grad_start = collect_parts(
        arrived_back, in_owner, in_local, in_rank, alive, mine, capacity, per_device
    )
    block_terms = jnp.einsum("rki,rkj->kij", fetched, upstream, preferred_element_type=jnp.float32)
    grad_blocks = lax.psum_scatter(
        block_terms.astype(jnp.bfloat16), "dp", scatter_dimension=1, tiled=True
    ).astype(jnp.float32)
    grad_start = grad_start + cot_wide * mixed + cot_wide
    sigma = jax.nn.sigmoid(preact)
    grad_pre = grad_start * sigma * (1.0 + preact * (1.0 - sigma))
    grad_pre_low = grad_pre.astype(jnp.bfloat16)
    taken = dense
    grad_bottom = lax.psum_scatter(
        lax.dot_general(
            taken, grad_pre_low, (((0,), (0,)), ((), ())), preferred_element_type=jnp.float32
        ).astype(jnp.bfloat16),
        "dp",
        scatter_dimension=0,
        tiled=True,
    ).astype(jnp.float32)
    bias_sums = lax.psum((jnp.sum(grad_pre, axis=0), jnp.sum(grad_mixed, axis=0)), "dp")
    return (cross_out, grad_bottom, bias_sums[0], grad_blocks, bias_sums[1])


def solution(mesh):
    return jax.shard_map(
        on_device,
        mesh=mesh,
        in_specs=(
            P("dp", None),
            P(None, "tensor"),
            P("tensor"),
            P("tensor", "dp", None),
            P("tensor"),
            P("dp", "tensor"),
            P(),
            P(),
            P(),
        ),
        out_specs=(
            P("dp", "tensor"),
            P("dp", "tensor"),
            P("tensor"),
            P("tensor", "dp", None),
            P("tensor"),
        ),
        check_vma=False,
    )
```

```python
import jax
import jax.numpy as jnp
from jax import lax
from jax.sharding import PartitionSpec as P

BLK = 512
SLOTS = 10


def slot_ranks(owner, alive):
    order = jnp.arange(owner.shape[1])
    earlier = order[None, :] < order[:, None]
    same = (owner[:, :, None] == owner[:, None, :]) & alive[:, None, :] & earlier[None, :, :]
    return jnp.sum(same.astype(jnp.int32), axis=2)


def post_table(owner_mine, rank_mine, alive_mine, groups, capacity):
    slot_count = owner_mine.shape[0]
    match = (
        (owner_mine[None, None, :] == jnp.arange(groups)[:, None, None])
        & (rank_mine[None, None, :] == jnp.arange(capacity)[None, :, None])
        & alive_mine[None, None, :]
    )
    chosen = jnp.sum(match.astype(jnp.int32) * jnp.arange(slot_count)[None, None, :], axis=2)
    filled = jnp.any(match, axis=2)
    return (chosen, filled)


def pack_parts(parts, chosen, filled):
    picked = jnp.take(parts, chosen.reshape(-1), axis=0) * filled.reshape(-1)[:, None, None].astype(
        parts.dtype
    )
    return picked.reshape(chosen.shape[0], chosen.shape[1] * parts.shape[1], parts.shape[2])


def collect_parts(received, owner, local, rank, alive, target, capacity, per_device):
    groups, span_rows, block_width = received.shape
    row_count = span_rows // capacity
    match = ((owner == target) & alive)[:, :, None] & (
        rank[:, :, None] == jnp.arange(capacity)[None, None, :]
    )
    matches = match[:, :, :, None] & (
        local[:, :, None, None] == jnp.arange(per_device)[None, None, None, :]
    )
    onehot = (
        jnp.sum(matches.astype(jnp.int32), axis=1)
        .reshape(groups * capacity, per_device)
        .astype(jnp.bfloat16)
    )
    flattened = received.reshape(groups * capacity, row_count, block_width)
    summed = jnp.einsum("irb,il->rlb", flattened, onehot, preferred_element_type=jnp.float32)
    return summed.reshape(row_count, per_device * block_width)


def ring_gather(x, axis, n):
    half = x.shape[0] // 2
    right = [(i, (i + 1) % n) for i in range(n)]
    left = [(i, (i - 1) % n) for i in range(n)]
    cur_a, cur_b = x[:half], x[half:]
    outs_a, outs_b = [cur_a], [cur_b]
    for _ in range(1, n):
        cur_a = lax.ppermute(cur_a, axis, right)
        cur_b = lax.ppermute(cur_b, axis, left)
        outs_a.append(cur_a)
        outs_b.append(cur_b)
    return jnp.stack(outs_a), jnp.stack(outs_b)


def take_blocks(stack_a, stack_b, owner, local, me, n):
    steps, half, width = stack_a.shape
    blocks_a = stack_a.reshape(steps, half, width // BLK, BLK)
    blocks_b = stack_b.reshape(steps, half, width // BLK, BLK)
    step_a = (me - owner) % n
    step_b = (owner - me) % n
    top = blocks_a[step_a, :, local, :]
    bottom = blocks_b[step_b, :, local, :]
    return jnp.concatenate([top, bottom], axis=1)


def on_device(
    dense,
    bottom_weight,
    bottom_bias,
    cross_blocks,
    cross_bias,
    cotangent,
    in_blocks,
    out_blocks,
    live_slots,
):
    groups = lax.axis_size("tensor")
    mine = lax.axis_index("tensor")
    row_count = dense.shape[0]
    local_width = bottom_weight.shape[1]
    per_device = local_width // BLK
    capacity = -(-SLOTS // groups)
    preact = jnp.dot(dense, bottom_weight, preferred_element_type=jnp.float32) + bottom_bias
    start = jax.nn.silu(preact).astype(jnp.bfloat16)
    start_wide = start.astype(jnp.float32)
    cot_wide = cotangent.astype(jnp.float32)
    grad_mixed = cot_wide * start_wide
    grad_mixed_low = grad_mixed.astype(jnp.bfloat16)
    alive = jnp.arange(SLOTS)[None, :] < live_slots[:, None]
    alive_mine = alive[mine]
    switch = alive_mine.astype(jnp.bfloat16)[:, None, None]
    in_owner = in_blocks // per_device
    in_local = in_blocks % per_device
    out_owner = out_blocks // per_device
    out_local = out_blocks % per_device
    in_rank = slot_ranks(in_owner, alive)
    out_rank = slot_ranks(out_owner, alive)
    combo = jnp.concatenate([start, grad_mixed_low], axis=1)
    stack_a, stack_b = ring_gather(combo, "tensor", groups)
    fetched = take_blocks(stack_a, stack_b, in_owner[mine], in_local[mine], mine, groups)
    taken = fetched
    product = jnp.einsum(
        "kri,kij->krj",
        taken,
        lax.all_gather(cross_blocks, "dp", axis=1, tiled=True),
        preferred_element_type=jnp.float32,
    )
    parts = product.astype(jnp.bfloat16) * switch
    chosen_out, filled_out = post_table(
        out_owner[mine], out_rank[mine], alive_mine, groups, capacity
    )
    arrived_parts = lax.all_to_all(
        pack_parts(parts, chosen_out, filled_out), "tensor", split_axis=0, concat_axis=0, tiled=True
    )
    mixed = (
        collect_parts(
            arrived_parts, out_owner, out_local, out_rank, alive, mine, capacity, per_device
        )
        + cross_bias
    )
    cross_out = (start_wide * mixed + start_wide).astype(jnp.bfloat16)
    upstream = take_blocks(
        stack_a, stack_b, out_owner[mine], out_local[mine] + per_device, mine, groups
    )
    upstream = upstream * switch
    backward = jnp.einsum(
        "krj,kij->kri",
        upstream,
        lax.all_gather(cross_blocks, "dp", axis=1, tiled=True),
        preferred_element_type=jnp.float32,
    )
    back_parts = backward.astype(jnp.bfloat16)
    chosen_in, filled_in = post_table(in_owner[mine], in_rank[mine], alive_mine, groups, capacity)
    arrived_back = lax.all_to_all(
        pack_parts(back_parts, chosen_in, filled_in),
        "tensor",
        split_axis=0,
        concat_axis=0,
        tiled=True,
    )
    grad_start = collect_parts(
        arrived_back, in_owner, in_local, in_rank, alive, mine, capacity, per_device
    )
    block_terms = jnp.einsum("kri,krj->kij", fetched, upstream, preferred_element_type=jnp.float32)
    grad_blocks = lax.psum_scatter(
        block_terms.astype(jnp.bfloat16), "dp", scatter_dimension=1, tiled=True
    ).astype(jnp.float32)
    grad_start = grad_start + cot_wide * mixed + cot_wide
    sigma = jax.nn.sigmoid(preact)
    grad_pre = grad_start * sigma * (1.0 + preact * (1.0 - sigma))
    grad_pre_low = grad_pre.astype(jnp.bfloat16)
    taken = dense
    grad_bottom = lax.psum_scatter(
        lax.dot_general(
            taken, grad_pre_low, (((0,), (0,)), ((), ())), preferred_element_type=jnp.float32
        ).astype(jnp.bfloat16),
        "dp",
        scatter_dimension=0,
        tiled=True,
    ).astype(jnp.float32)
    bias_sums = lax.psum((jnp.sum(grad_pre, axis=0), jnp.sum(grad_mixed, axis=0)), "dp")
    return (cross_out, grad_bottom, bias_sums[0], grad_blocks, bias_sums[1])


def solution(mesh):
    return jax.shard_map(
        on_device,
        mesh=mesh,
        in_specs=(
            P("dp", None),
            P(None, "tensor"),
            P("tensor"),
            P("tensor", "dp", None),
            P("tensor"),
            P("dp", "tensor"),
            P(),
            P(),
            P(),
        ),
        out_specs=(
            P("dp", "tensor"),
            P("dp", "tensor"),
            P("tensor"),
            P("tensor", "dp", None),
            P("tensor"),
        ),
        check_vma=False,
    )
```

```python
import jax
import jax.numpy as jnp
from jax import lax
from jax.sharding import PartitionSpec as P

BLK = 512
SLOTS = 10


def slot_ranks(owner, alive):
    order = jnp.arange(owner.shape[1])
    earlier = order[None, :] < order[:, None]
    same = (owner[:, :, None] == owner[:, None, :]) & alive[:, None, :] & earlier[None, :, :]
    return jnp.sum(same.astype(jnp.int32), axis=2)


def post_table(owner_mine, rank_mine, alive_mine, groups, capacity):
    slot_count = owner_mine.shape[0]
    match = (
        (owner_mine[None, None, :] == jnp.arange(groups)[:, None, None])
        & (rank_mine[None, None, :] == jnp.arange(capacity)[None, :, None])
        & alive_mine[None, None, :]
    )
    chosen = jnp.sum(match.astype(jnp.int32) * jnp.arange(slot_count)[None, None, :], axis=2)
    filled = jnp.any(match, axis=2)
    return (chosen, filled)


def pack_parts(parts, chosen, filled):
    picked = jnp.take(parts, chosen.reshape(-1), axis=0) * filled.reshape(-1)[:, None, None].astype(
        parts.dtype
    )
    return picked.reshape(chosen.shape[0], chosen.shape[1] * parts.shape[1], parts.shape[2])


def collect_parts(received, owner, local, rank, alive, target, capacity, per_device):
    groups, span_rows, block_width = received.shape
    row_count = span_rows // capacity
    match = ((owner == target) & alive)[:, :, None] & (
        rank[:, :, None] == jnp.arange(capacity)[None, None, :]
    )
    matches = match[:, :, :, None] & (
        local[:, :, None, None] == jnp.arange(per_device)[None, None, None, :]
    )
    onehot = (
        jnp.sum(matches.astype(jnp.int32), axis=1)
        .reshape(groups * capacity, per_device)
        .astype(jnp.bfloat16)
    )
    flattened = received.reshape(groups * capacity, row_count, block_width)
    summed = jnp.einsum("irb,il->rlb", flattened, onehot, preferred_element_type=jnp.float32)
    return summed.reshape(row_count, per_device * block_width)


def ring_gather(x, axis, n):
    half = x.shape[0] // 2
    right = [(i, (i + 1) % n) for i in range(n)]
    left = [(i, (i - 1) % n) for i in range(n)]
    cur_a, cur_b = x[:half], x[half:]
    outs_a, outs_b = [cur_a], [cur_b]
    for _ in range(1, n):
        cur_a = lax.ppermute(cur_a, axis, right)
        cur_b = lax.ppermute(cur_b, axis, left)
        outs_a.append(cur_a)
        outs_b.append(cur_b)
    return jnp.stack(outs_a), jnp.stack(outs_b)


def take_blocks(stack_a, stack_b, owner, local, me, n):
    steps, half, width = stack_a.shape
    blocks_a = stack_a.reshape(steps, half, width // BLK, BLK)
    blocks_b = stack_b.reshape(steps, half, width // BLK, BLK)
    step_a = (me - owner) % n
    step_b = (owner - me) % n
    top = blocks_a[step_a, :, local, :]
    bottom = blocks_b[step_b, :, local, :]
    return jnp.concatenate([top, bottom], axis=1)


def on_device(
    dense,
    bottom_weight,
    bottom_bias,
    cross_blocks,
    cross_bias,
    cotangent,
    in_blocks,
    out_blocks,
    live_slots,
):
    groups = lax.axis_size("tensor")
    mine = lax.axis_index("tensor")
    row_count = dense.shape[0]
    local_width = bottom_weight.shape[1]
    per_device = local_width // BLK
    capacity = -(-SLOTS // groups)
    preact = jnp.dot(dense, bottom_weight, preferred_element_type=jnp.float32) + bottom_bias
    start = jax.nn.silu(preact).astype(jnp.bfloat16)
    start_wide = start.astype(jnp.float32)
    cot_wide = cotangent.astype(jnp.float32)
    grad_mixed = cot_wide * start_wide
    grad_mixed_low = grad_mixed.astype(jnp.bfloat16)
    alive = jnp.arange(SLOTS)[None, :] < live_slots[:, None]
    alive_mine = alive[mine]
    switch = alive_mine.astype(jnp.bfloat16)[:, None, None]
    in_owner = in_blocks // per_device
    in_local = in_blocks % per_device
    out_owner = out_blocks // per_device
    out_local = out_blocks % per_device
    in_rank = slot_ranks(in_owner, alive)
    out_rank = slot_ranks(out_owner, alive)
    combo = jnp.concatenate([start, grad_mixed_low], axis=1)
    stack_a, stack_b = ring_gather(combo, "tensor", groups)
    fetched = take_blocks(stack_a, stack_b, in_owner[mine], in_local[mine], mine, groups)
    taken = fetched
    product = jnp.einsum(
        "kri,kij->krj",
        taken,
        lax.all_gather(cross_blocks, "dp", axis=1, tiled=True),
        preferred_element_type=jnp.float32,
    )
    parts = product.astype(jnp.bfloat16) * switch
    chosen_out, filled_out = post_table(
        out_owner[mine], out_rank[mine], alive_mine, groups, capacity
    )
    arrived_parts = lax.all_to_all(
        pack_parts(parts, chosen_out, filled_out), "tensor", split_axis=0, concat_axis=0, tiled=True
    )
    mixed = (
        collect_parts(
            arrived_parts, out_owner, out_local, out_rank, alive, mine, capacity, per_device
        )
        + cross_bias
    )
    cross_out = (start_wide * mixed + start_wide).astype(jnp.bfloat16)
    upstream = take_blocks(
        stack_a, stack_b, out_owner[mine], out_local[mine] + per_device, mine, groups
    )
    upstream = upstream * switch
    backward = jnp.einsum(
        "krj,kij->kri",
        upstream,
        lax.all_gather(cross_blocks, "dp", axis=1, tiled=True),
        preferred_element_type=jnp.float32,
    )
    back_parts = backward.astype(jnp.bfloat16)
    chosen_in, filled_in = post_table(in_owner[mine], in_rank[mine], alive_mine, groups, capacity)
    arrived_back = lax.all_to_all(
        pack_parts(back_parts, chosen_in, filled_in),
        "tensor",
        split_axis=0,
        concat_axis=0,
        tiled=True,
    )
    grad_start = collect_parts(
        arrived_back, in_owner, in_local, in_rank, alive, mine, capacity, per_device
    )
    block_terms = jnp.einsum("kri,krj->kij", fetched, upstream, preferred_element_type=jnp.float32)
    grad_blocks = lax.psum_scatter(
        block_terms.astype(jnp.bfloat16), "dp", scatter_dimension=1, tiled=True
    ).astype(jnp.float32)
    grad_start = grad_start + cot_wide * mixed + cot_wide
    sigma = jax.nn.sigmoid(preact)
    grad_pre = grad_start * sigma * (1.0 + preact * (1.0 - sigma))
    grad_pre_low = grad_pre.astype(jnp.bfloat16)
    dp_size = lax.axis_size("dp")
    split = local_width // 2
    lead = lax.dot_general(
        grad_pre_low[:, :split], dense, (((0,), (0,)), ((), ())), preferred_element_type=jnp.float32
    ).astype(jnp.bfloat16)
    lead = lax.psum_scatter(lead, "dp", scatter_dimension=1, tiled=True).astype(jnp.float32).T
    rest = lax.dot_general(
        dense, grad_pre_low[:, split:], (((0,), (0,)), ((), ())), preferred_element_type=jnp.float32
    ).astype(jnp.bfloat16)
    rest = rest.reshape(dp_size, rest.shape[0] // dp_size, rest.shape[1])
    rest = lax.all_to_all(rest, "dp", split_axis=0, concat_axis=0, tiled=True)
    rest = jnp.sum(rest.astype(jnp.float32), axis=0)
    grad_bottom = jnp.concatenate([lead, rest], axis=1)
    bias_sums = lax.psum((jnp.sum(grad_pre, axis=0), jnp.sum(grad_mixed, axis=0)), "dp")
    return (cross_out, grad_bottom, bias_sums[0], grad_blocks, bias_sums[1])


def solution(mesh):
    return jax.shard_map(
        on_device,
        mesh=mesh,
        in_specs=(
            P("dp", None),
            P(None, "tensor"),
            P("tensor"),
            P("tensor", "dp", None),
            P("tensor"),
            P("dp", "tensor"),
            P(),
            P(),
            P(),
        ),
        out_specs=(
            P("dp", "tensor"),
            P("dp", "tensor"),
            P("tensor"),
            P("tensor", "dp", None),
            P("tensor"),
        ),
        check_vma=False,
    )
```

```python
import jax
import jax.numpy as jnp
from jax import lax
from jax.sharding import PartitionSpec as P

BLK = 512
SLOTS = 10


def slot_ranks(owner, alive):
    order = jnp.arange(owner.shape[1])
    earlier = order[None, :] < order[:, None]
    same = (owner[:, :, None] == owner[:, None, :]) & alive[:, None, :] & earlier[None, :, :]
    return jnp.sum(same.astype(jnp.int32), axis=2)


def post_table(owner_mine, rank_mine, alive_mine, groups, capacity):
    slot_count = owner_mine.shape[0]
    match = (
        (owner_mine[None, None, :] == jnp.arange(groups)[:, None, None])
        & (rank_mine[None, None, :] == jnp.arange(capacity)[None, :, None])
        & alive_mine[None, None, :]
    )
    chosen = jnp.sum(match.astype(jnp.int32) * jnp.arange(slot_count)[None, None, :], axis=2)
    filled = jnp.any(match, axis=2)
    return (chosen, filled)


def pack_parts(parts, chosen, filled):
    picked = jnp.take(parts, chosen.reshape(-1), axis=0) * filled.reshape(-1)[:, None, None].astype(
        parts.dtype
    )
    return picked.reshape(chosen.shape[0], chosen.shape[1] * parts.shape[1], parts.shape[2])


def collect_parts(received, owner, local, rank, alive, target, capacity, per_device):
    groups, span_rows, block_width = received.shape
    row_count = span_rows // capacity
    match = ((owner == target) & alive)[:, :, None] & (
        rank[:, :, None] == jnp.arange(capacity)[None, None, :]
    )
    matches = match[:, :, :, None] & (
        local[:, :, None, None] == jnp.arange(per_device)[None, None, None, :]
    )
    onehot = (
        jnp.sum(matches.astype(jnp.int32), axis=1)
        .reshape(groups * capacity, per_device)
        .astype(jnp.bfloat16)
    )
    flattened = received.reshape(groups * capacity, row_count, block_width)
    summed = jnp.einsum("irb,il->rlb", flattened, onehot, preferred_element_type=jnp.float32)
    return summed.reshape(row_count, per_device * block_width)


def chip_gather(x, axis, n):
    me = lax.axis_index(axis)
    core = me % 2
    half = x.shape[0] // 2
    swap = [(i, i ^ 1) for i in range(n)]
    ring = [(i, (i + 2) % n) if i % 2 == 0 else (i, (i - 2) % n) for i in range(n)]
    partner = lax.ppermute(x, axis, swap)
    both = jnp.stack([x, partner])
    pair = jnp.take(both, jnp.stack([core, 1 - core]), axis=0)
    cur = lax.dynamic_slice_in_dim(pair, core * half, half, axis=1)
    other = lax.dynamic_slice_in_dim(pair, (1 - core) * half, half, axis=1)
    mine_steps, other_steps = [cur], [other]
    for _ in range(1, n // 2):
        cur = lax.ppermute(cur, axis, ring)
        mine_steps.append(cur)
        other_steps.append(lax.ppermute(cur, axis, swap))
    return jnp.stack([jnp.stack(mine_steps), jnp.stack(other_steps)])


def take_blocks(stacks, owner, local, me, n):
    sides, chips, cores, half, width = stacks.shape
    blocks = stacks.reshape(sides, chips, cores, half, width // BLK, BLK)
    core = me % 2
    chip = me // 2
    owner_chip = owner // 2
    owner_core = owner % 2
    top = blocks[core, (chip - owner_chip) % chips, owner_core, :, local, :]
    bottom = blocks[1 - core, (owner_chip - chip) % chips, owner_core, :, local, :]
    return jnp.concatenate([top, bottom], axis=1)

def on_device(
    dense,
    bottom_weight,
    bottom_bias,
    cross_blocks,
    cross_bias,
    cotangent,
    in_blocks,
    out_blocks,
    live_slots,
):
    groups = lax.axis_size("tensor")
    mine = lax.axis_index("tensor")
    row_count = dense.shape[0]
    local_width = bottom_weight.shape[1]
    per_device = local_width // BLK
    capacity = -(-SLOTS // groups)
    preact = jnp.dot(dense, bottom_weight, preferred_element_type=jnp.float32) + bottom_bias
    start = jax.nn.silu(preact).astype(jnp.bfloat16)
    start_wide = start.astype(jnp.float32)
    cot_wide = cotangent.astype(jnp.float32)
    grad_mixed = cot_wide * start_wide
    grad_mixed_low = grad_mixed.astype(jnp.bfloat16)
    alive = jnp.arange(SLOTS)[None, :] < live_slots[:, None]
    alive_mine = alive[mine]
    switch = alive_mine.astype(jnp.bfloat16)[:, None, None]
    in_owner = in_blocks // per_device
    in_local = in_blocks % per_device
    out_owner = out_blocks // per_device
    out_local = out_blocks % per_device
    in_rank = slot_ranks(in_owner, alive)
    out_rank = slot_ranks(out_owner, alive)
    combo = jnp.concatenate([start, grad_mixed_low], axis=1)
    stacks = chip_gather(combo, "tensor", groups)
    fetched = take_blocks(stacks, in_owner[mine], in_local[mine], mine, groups)
    taken = fetched
    product = jnp.einsum(
        "kri,kij->krj",
        taken,
        lax.all_gather(cross_blocks, "dp", axis=1, tiled=True),
        preferred_element_type=jnp.float32,
    )
    parts = product.astype(jnp.bfloat16) * switch
    chosen_out, filled_out = post_table(
        out_owner[mine], out_rank[mine], alive_mine, groups, capacity
    )
    arrived_parts = lax.all_to_all(
        pack_parts(parts, chosen_out, filled_out), "tensor", split_axis=0, concat_axis=0, tiled=True
    )
    mixed = (
        collect_parts(
            arrived_parts, out_owner, out_local, out_rank, alive, mine, capacity, per_device
        )
        + cross_bias
    )
    cross_out = (start_wide * mixed + start_wide).astype(jnp.bfloat16)
    upstream = take_blocks(stacks, out_owner[mine], out_local[mine] + per_device, mine, groups)
    upstream = upstream * switch
    backward = jnp.einsum(
        "krj,kij->kri",
        upstream,
        lax.all_gather(cross_blocks, "dp", axis=1, tiled=True),
        preferred_element_type=jnp.float32,
    )
    back_parts = backward.astype(jnp.bfloat16)
    chosen_in, filled_in = post_table(in_owner[mine], in_rank[mine], alive_mine, groups, capacity)
    arrived_back = lax.all_to_all(
        pack_parts(back_parts, chosen_in, filled_in),
        "tensor",
        split_axis=0,
        concat_axis=0,
        tiled=True,
    )
    grad_start = collect_parts(
        arrived_back, in_owner, in_local, in_rank, alive, mine, capacity, per_device
    )
    block_terms = jnp.einsum("kri,krj->kij", fetched, upstream, preferred_element_type=jnp.float32)
    grad_blocks = lax.psum_scatter(
        block_terms.astype(jnp.bfloat16), "dp", scatter_dimension=1, tiled=True
    ).astype(jnp.float32)
    grad_start = grad_start + cot_wide * mixed + cot_wide
    sigma = jax.nn.sigmoid(preact)
    grad_pre = grad_start * sigma * (1.0 + preact * (1.0 - sigma))
    grad_pre_low = grad_pre.astype(jnp.bfloat16)
    taken = dense
    grad_bottom = lax.psum_scatter(
        lax.dot_general(
            taken, grad_pre_low, (((0,), (0,)), ((), ())), preferred_element_type=jnp.float32
        ).astype(jnp.bfloat16),
        "dp",
        scatter_dimension=0,
        tiled=True,
    ).astype(jnp.float32)
    bias_sums = lax.psum((jnp.sum(grad_pre, axis=0), jnp.sum(grad_mixed, axis=0)), "dp")
    return (cross_out, grad_bottom, bias_sums[0], grad_blocks, bias_sums[1])


def solution(mesh):
    return jax.shard_map(
        on_device,
        mesh=mesh,
        in_specs=(
            P("dp", None),
            P(None, "tensor"),
            P("tensor"),
            P("tensor", "dp", None),
            P("tensor"),
            P("dp", "tensor"),
            P(),
            P(),
            P(),
        ),
        out_specs=(
            P("dp", "tensor"),
            P("dp", "tensor"),
            P("tensor"),
            P("tensor", "dp", None),
            P("tensor"),
        ),
        check_vma=False,
    )
```

```python
import jax
import jax.numpy as jnp
from jax import lax
from jax.sharding import PartitionSpec as P
from jax.experimental import pallas as pl
from jax.experimental.pallas import tpu as pltpu

BLK = 512
SLOTS = 10


def slot_ranks(owner, alive):
    order = jnp.arange(owner.shape[1])
    earlier = order[None, :] < order[:, None]
    same = (owner[:, :, None] == owner[:, None, :]) & alive[:, None, :] & earlier[None, :, :]
    return jnp.sum(same.astype(jnp.int32), axis=2)


def post_table(owner_mine, rank_mine, alive_mine, groups, capacity):
    slot_count = owner_mine.shape[0]
    match = (
        (owner_mine[None, None, :] == jnp.arange(groups)[:, None, None])
        & (rank_mine[None, None, :] == jnp.arange(capacity)[None, :, None])
        & alive_mine[None, None, :]
    )
    chosen = jnp.sum(match.astype(jnp.int32) * jnp.arange(slot_count)[None, None, :], axis=2)
    filled = jnp.any(match, axis=2)
    return (chosen, filled)


def pack_parts(parts, chosen, filled):
    picked = jnp.take(parts, chosen.reshape(-1), axis=0) * filled.reshape(-1)[:, None, None].astype(
        parts.dtype
    )
    return picked.reshape(chosen.shape[0], chosen.shape[1] * parts.shape[1], parts.shape[2])


def collect_parts(received, owner, local, rank, alive, target, capacity, per_device):
    groups, span_rows, block_width = received.shape
    row_count = span_rows // capacity
    match = ((owner == target) & alive)[:, :, None] & (
        rank[:, :, None] == jnp.arange(capacity)[None, None, :]
    )
    matches = match[:, :, :, None] & (
        local[:, :, None, None] == jnp.arange(per_device)[None, None, None, :]
    )
    onehot = (
        jnp.sum(matches.astype(jnp.int32), axis=1)
        .reshape(groups * capacity, per_device)
        .astype(jnp.bfloat16)
    )
    flattened = received.reshape(groups * capacity, row_count, block_width)
    summed = jnp.einsum("irb,il->rlb", flattened, onehot, preferred_element_type=jnp.float32)
    return summed.reshape(row_count, per_device * block_width)


def ring_gather(x, axis, n):
    half = x.shape[0] // 2
    right = [(i, (i + 1) % n) for i in range(n)]
    left = [(i, (i - 1) % n) for i in range(n)]
    cur_a, cur_b = x[:half], x[half:]
    outs_a, outs_b = [cur_a], [cur_b]
    for _ in range(1, n):
        cur_a = lax.ppermute(cur_a, axis, right)
        cur_b = lax.ppermute(cur_b, axis, left)
        outs_a.append(cur_a)
        outs_b.append(cur_b)
    return jnp.stack(outs_a), jnp.stack(outs_b)


def take_blocks(stack_a, stack_b, owner, local, me, n):
    steps, half, width = stack_a.shape
    blocks_a = stack_a.reshape(steps, half, width // BLK, BLK)
    blocks_b = stack_b.reshape(steps, half, width // BLK, BLK)
    step_a = (me - owner) % n
    step_b = (owner - me) % n
    top = blocks_a[step_a, :, local, :]
    bottom = blocks_b[step_b, :, local, :]
    return jnp.concatenate([top, bottom], axis=1)


def slot_kernel(sa_i, sb_i, bi, sa_o, sb_o, bo, live, fa, fb, ua, ub, w, part_ref, back_ref, term_ref):
    k = pl.program_id(0)
    on = live[k] > 0
    half = fa.shape[1]
    wk = w[0]
    top_in, bottom_in = fa[0], fb[0]
    top_up, bottom_up = ua[0], ub[0]
    nt = (((1,), (1,)), ((), ()))
    tn = (((0,), (0,)), ((), ()))
    for rows, src in ((slice(0, half), top_in), (slice(half, 2 * half), bottom_in)):
        value = jnp.dot(src, wk, preferred_element_type=jnp.float32)
        part_ref[0, rows, :] = jnp.where(on, value, 0.0).astype(part_ref.dtype)
    for rows, src in ((slice(0, half), top_up), (slice(half, 2 * half), bottom_up)):
        value = lax.dot_general(src, wk, nt, preferred_element_type=jnp.float32)
        back_ref[0, rows, :] = jnp.where(on, value, 0.0).astype(back_ref.dtype)
    term = lax.dot_general(top_in, top_up, tn, preferred_element_type=jnp.float32)
    term = term + lax.dot_general(bottom_in, bottom_up, tn, preferred_element_type=jnp.float32)
    term_ref[0] = jnp.where(on, term, 0.0).astype(term_ref.dtype)


def slot_products(stack_a, stack_b, weights, tables):
    slots, size, _ = weights.shape
    steps, half, width = stack_a.shape
    rows = 2 * half

    def block(step_ref, blk_ref):
        return pl.BlockSpec(
            (1, half, BLK), lambda k, *t: (t[step_ref][k], 0, t[blk_ref][k])
        )

    grid_spec = pltpu.PrefetchScalarGridSpec(
        num_scalar_prefetch=len(tables),
        grid=(slots,),
        in_specs=[
            block(0, 2),
            block(1, 2),
            block(3, 5),
            block(4, 5),
            pl.BlockSpec((1, size, size), lambda k, *t: (k, 0, 0)),
        ],
        out_specs=[
            pl.BlockSpec((1, rows, BLK), lambda k, *t: (k, 0, 0)),
            pl.BlockSpec((1, rows, BLK), lambda k, *t: (k, 0, 0)),
            pl.BlockSpec((1, size, size), lambda k, *t: (k, 0, 0)),
        ],
    )
    return pl.pallas_call(
        slot_kernel,
        grid_spec=grid_spec,
        out_shape=[
            jax.ShapeDtypeStruct((slots, rows, BLK), jnp.bfloat16),
            jax.ShapeDtypeStruct((slots, rows, BLK), jnp.bfloat16),
            jax.ShapeDtypeStruct((slots, size, size), jnp.bfloat16),
        ],
        cost_estimate=pl.CostEstimate(
            flops=6 * slots * rows * size * size,
            bytes_accessed=slots * (4 * rows * BLK + 2 * size * size) * 2,
            transcendentals=0,
        ),
    )(*tables, stack_a, stack_b, stack_a, stack_b, weights)


def on_device(
    dense,
    bottom_weight,
    bottom_bias,
    cross_blocks,
    cross_bias,
    cotangent,
    in_blocks,
    out_blocks,
    live_slots,
):
    groups = lax.axis_size("tensor")
    mine = lax.axis_index("tensor")
    row_count = dense.shape[0]
    local_width = bottom_weight.shape[1]
    per_device = local_width // BLK
    capacity = -(-SLOTS // groups)
    preact = jnp.dot(dense, bottom_weight, preferred_element_type=jnp.float32) + bottom_bias
    start = jax.nn.silu(preact).astype(jnp.bfloat16)
    start_wide = start.astype(jnp.float32)
    cot_wide = cotangent.astype(jnp.float32)
    grad_mixed = cot_wide * start_wide
    grad_mixed_low = grad_mixed.astype(jnp.bfloat16)
    alive = jnp.arange(SLOTS)[None, :] < live_slots[:, None]
    alive_mine = alive[mine]
    in_owner = in_blocks // per_device
    in_local = in_blocks % per_device
    out_owner = out_blocks // per_device
    out_local = out_blocks % per_device
    in_rank = slot_ranks(in_owner, alive)
    out_rank = slot_ranks(out_owner, alive)
    combo = jnp.concatenate([start, grad_mixed_low], axis=1)
    stack_a, stack_b = ring_gather(combo, "tensor", groups)
    step_a = lambda owner: (mine - owner) % groups
    step_b = lambda owner: (owner - mine) % groups
    tables = (
        step_a(in_owner[mine]),
        step_b(in_owner[mine]),
        in_local[mine],
        step_a(out_owner[mine]),
        step_b(out_owner[mine]),
        out_local[mine] + per_device,
        alive_mine.astype(jnp.int32),
    )
    weights = lax.all_gather(cross_blocks, "dp", axis=1, tiled=True)
    parts, back_parts, block_terms = slot_products(
        stack_a.reshape(groups, -1, 2 * local_width),
        stack_b.reshape(groups, -1, 2 * local_width),
        weights,
        tuple(t.astype(jnp.int32) for t in tables),
    )
    chosen_out, filled_out = post_table(
        out_owner[mine], out_rank[mine], alive_mine, groups, capacity
    )
    arrived_parts = lax.all_to_all(
        pack_parts(parts, chosen_out, filled_out), "tensor", split_axis=0, concat_axis=0, tiled=True
    )
    mixed = (
        collect_parts(
            arrived_parts, out_owner, out_local, out_rank, alive, mine, capacity, per_device
        )
        + cross_bias
    )
    cross_out = (start_wide * mixed + start_wide).astype(jnp.bfloat16)
    chosen_in, filled_in = post_table(in_owner[mine], in_rank[mine], alive_mine, groups, capacity)
    arrived_back = lax.all_to_all(
        pack_parts(back_parts, chosen_in, filled_in),
        "tensor",
        split_axis=0,
        concat_axis=0,
        tiled=True,
    )
    grad_start = collect_parts(
        arrived_back, in_owner, in_local, in_rank, alive, mine, capacity, per_device
    )
    grad_blocks = lax.psum_scatter(block_terms, "dp", scatter_dimension=1, tiled=True).astype(
        jnp.float32
    )
    grad_start = grad_start + cot_wide * mixed + cot_wide
    sigma = jax.nn.sigmoid(preact)
    grad_pre = grad_start * sigma * (1.0 + preact * (1.0 - sigma))
    grad_pre_low = grad_pre.astype(jnp.bfloat16)
    taken = dense
    grad_bottom = lax.psum_scatter(
        lax.dot_general(
            taken, grad_pre_low, (((0,), (0,)), ((), ())), preferred_element_type=jnp.float32
        ).astype(jnp.bfloat16),
        "dp",
        scatter_dimension=0,
        tiled=True,
    ).astype(jnp.float32)
    bias_sums = lax.psum((jnp.sum(grad_pre, axis=0), jnp.sum(grad_mixed, axis=0)), "dp")
    return (cross_out, grad_bottom, bias_sums[0], grad_blocks, bias_sums[1])


def solution(mesh):
    return jax.shard_map(
        on_device,
        mesh=mesh,
        in_specs=(
            P("dp", None),
            P(None, "tensor"),
            P("tensor"),
            P("tensor", "dp", None),
            P("tensor"),
            P("dp", "tensor"),
            P(),
            P(),
            P(),
        ),
        out_specs=(
            P("dp", "tensor"),
            P("dp", "tensor"),
            P("tensor"),
            P("tensor", "dp", None),
            P("tensor"),
        ),
        check_vma=False,
    )
```

```python
import jax
import jax.numpy as jnp
from jax import lax
from jax.sharding import PartitionSpec as P
from jax.experimental import pallas as pl
from jax.experimental.pallas import tpu as pltpu

BLK = 512
SLOTS = 10


def slot_ranks(owner, alive):
    order = jnp.arange(owner.shape[1])
    earlier = order[None, :] < order[:, None]
    same = (owner[:, :, None] == owner[:, None, :]) & alive[:, None, :] & earlier[None, :, :]
    return jnp.sum(same.astype(jnp.int32), axis=2)


def post_table(owner_mine, rank_mine, alive_mine, groups, capacity):
    slot_count = owner_mine.shape[0]
    match = (
        (owner_mine[None, None, :] == jnp.arange(groups)[:, None, None])
        & (rank_mine[None, None, :] == jnp.arange(capacity)[None, :, None])
        & alive_mine[None, None, :]
    )
    chosen = jnp.sum(match.astype(jnp.int32) * jnp.arange(slot_count)[None, None, :], axis=2)
    filled = jnp.any(match, axis=2)
    return (chosen, filled)


def pack_parts(parts, chosen, filled):
    picked = jnp.take(parts, chosen.reshape(-1), axis=0) * filled.reshape(-1)[:, None, None].astype(
        parts.dtype
    )
    return picked.reshape(chosen.shape[0], chosen.shape[1] * parts.shape[1], parts.shape[2])


def collect_parts(received, owner, local, rank, alive, target, capacity, per_device):
    groups, span_rows, block_width = received.shape
    row_count = span_rows // capacity
    match = ((owner == target) & alive)[:, :, None] & (
        rank[:, :, None] == jnp.arange(capacity)[None, None, :]
    )
    matches = match[:, :, :, None] & (
        local[:, :, None, None] == jnp.arange(per_device)[None, None, None, :]
    )
    onehot = (
        jnp.sum(matches.astype(jnp.int32), axis=1)
        .reshape(groups * capacity, per_device)
        .astype(jnp.bfloat16)
    )
    flattened = received.reshape(groups * capacity, row_count, block_width)
    summed = jnp.einsum("irb,il->rlb", flattened, onehot, preferred_element_type=jnp.float32)
    return summed.reshape(row_count, per_device * block_width)


def ring_gather(x, axis, n):
    half = x.shape[0] // 2
    right = [(i, (i + 1) % n) for i in range(n)]
    left = [(i, (i - 1) % n) for i in range(n)]
    cur_a, cur_b = x[:half], x[half:]
    outs_a, outs_b = [cur_a], [cur_b]
    for _ in range(1, n):
        cur_a = lax.ppermute(cur_a, axis, right)
        cur_b = lax.ppermute(cur_b, axis, left)
        outs_a.append(cur_a)
        outs_b.append(cur_b)
    return jnp.stack(outs_a), jnp.stack(outs_b)


def take_blocks(stack_a, stack_b, owner, local, me, n):
    steps, half, width = stack_a.shape
    blocks_a = stack_a.reshape(steps, half, width // BLK, BLK)
    blocks_b = stack_b.reshape(steps, half, width // BLK, BLK)
    step_a = (me - owner) % n
    step_b = (owner - me) % n
    top = blocks_a[step_a, :, local, :]
    bottom = blocks_b[step_b, :, local, :]
    return jnp.concatenate([top, bottom], axis=1)


def slot_kernel(sa_i, sb_i, bi, sa_o, sb_o, bo, live, fa, fb, ua, ub, w, part_ref, back_ref, term_ref):
    k = pl.program_id(0)
    on = live[k] > 0
    half = fa.shape[1]
    wk = w[0]
    top_in, bottom_in = fa[0], fb[0]
    top_up, bottom_up = ua[0], ub[0]
    nt = (((1,), (1,)), ((), ()))
    tn = (((0,), (0,)), ((), ()))
    for rows, src in ((slice(0, half), top_in), (slice(half, 2 * half), bottom_in)):
        value = jnp.dot(src, wk, preferred_element_type=jnp.float32)
        part_ref[0, rows, :] = jnp.where(on, value, 0.0).astype(part_ref.dtype)
    for rows, src in ((slice(0, half), top_up), (slice(half, 2 * half), bottom_up)):
        value = lax.dot_general(src, wk, nt, preferred_element_type=jnp.float32)
        back_ref[0, rows, :] = jnp.where(on, value, 0.0).astype(back_ref.dtype)
    term = lax.dot_general(top_in, top_up, tn, preferred_element_type=jnp.float32)
    term = term + lax.dot_general(bottom_in, bottom_up, tn, preferred_element_type=jnp.float32)
    term_ref[0] = jnp.where(on, term, 0.0).astype(term_ref.dtype)


def slot_products(stack_a, stack_b, weights, tables):
    slots, size, _ = weights.shape
    steps, half, width = stack_a.shape
    rows = 2 * half

    def block(step_ref, blk_ref):
        return pl.BlockSpec(
            (1, half, BLK), lambda k, *t: (t[step_ref][k], 0, t[blk_ref][k])
        )

    grid_spec = pltpu.PrefetchScalarGridSpec(
        num_scalar_prefetch=len(tables),
        grid=(slots,),
        in_specs=[
            block(0, 2),
            block(1, 2),
            block(3, 5),
            block(4, 5),
            pl.BlockSpec((1, size, size), lambda k, *t: (k, 0, 0)),
        ],
        out_specs=[
            pl.BlockSpec((1, rows, BLK), lambda k, *t: (k, 0, 0)),
            pl.BlockSpec((1, rows, BLK), lambda k, *t: (k, 0, 0)),
            pl.BlockSpec((1, size, size), lambda k, *t: (k, 0, 0)),
        ],
    )
    return pl.pallas_call(
        slot_kernel,
        grid_spec=grid_spec,
        out_shape=[
            jax.ShapeDtypeStruct((slots, rows, BLK), jnp.bfloat16),
            jax.ShapeDtypeStruct((slots, rows, BLK), jnp.bfloat16),
            jax.ShapeDtypeStruct((slots, size, size), jnp.bfloat16),
        ],
        cost_estimate=pl.CostEstimate(
            flops=6 * slots * rows * size * size,
            bytes_accessed=slots * (4 * rows * BLK + 2 * size * size) * 2,
            transcendentals=0,
        ),
    )(*tables, stack_a, stack_b, stack_a, stack_b, weights)


def outer_kernel(left, right, out):
    out[...] = lax.dot_general(
        left[...], right[...], (((0,), (0,)), ((), ())), preferred_element_type=jnp.float32
    ).astype(out.dtype)


def group_outer(left, right, tile_m=512, tile_n=1024):
    rows, m = left.shape
    n = right.shape[1]
    return pl.pallas_call(
        outer_kernel,
        grid=(m // tile_m, n // tile_n),
        in_specs=[
            pl.BlockSpec((rows, tile_m), lambda i, j: (0, i)),
            pl.BlockSpec((rows, tile_n), lambda i, j: (0, j)),
        ],
        out_specs=pl.BlockSpec((tile_m, tile_n), lambda i, j: (i, j)),
        out_shape=jax.ShapeDtypeStruct((m, n), jnp.bfloat16),
        cost_estimate=pl.CostEstimate(
            flops=2 * rows * m * n, bytes_accessed=2 * (rows * (m + n) + m * n), transcendentals=0
        ),
    )(left, right)


def on_device(
    dense,
    bottom_weight,
    bottom_bias,
    cross_blocks,
    cross_bias,
    cotangent,
    in_blocks,
    out_blocks,
    live_slots,
):
    groups = lax.axis_size("tensor")
    mine = lax.axis_index("tensor")
    row_count = dense.shape[0]
    local_width = bottom_weight.shape[1]
    per_device = local_width // BLK
    capacity = -(-SLOTS // groups)
    preact = jnp.dot(dense, bottom_weight, preferred_element_type=jnp.float32) + bottom_bias
    start = jax.nn.silu(preact).astype(jnp.bfloat16)
    start_wide = start.astype(jnp.float32)
    cot_wide = cotangent.astype(jnp.float32)
    grad_mixed = cot_wide * start_wide
    grad_mixed_low = grad_mixed.astype(jnp.bfloat16)
    alive = jnp.arange(SLOTS)[None, :] < live_slots[:, None]
    alive_mine = alive[mine]
    in_owner = in_blocks // per_device
    in_local = in_blocks % per_device
    out_owner = out_blocks // per_device
    out_local = out_blocks % per_device
    in_rank = slot_ranks(in_owner, alive)
    out_rank = slot_ranks(out_owner, alive)
    combo = jnp.concatenate([start, grad_mixed_low], axis=1)
    stack_a, stack_b = ring_gather(combo, "tensor", groups)
    step_a = lambda owner: (mine - owner) % groups
    step_b = lambda owner: (owner - mine) % groups
    tables = (
        step_a(in_owner[mine]),
        step_b(in_owner[mine]),
        in_local[mine],
        step_a(out_owner[mine]),
        step_b(out_owner[mine]),
        out_local[mine] + per_device,
        alive_mine.astype(jnp.int32),
    )
    weights = lax.all_gather(cross_blocks, "dp", axis=1, tiled=True)
    parts, back_parts, block_terms = slot_products(
        stack_a.reshape(groups, -1, 2 * local_width),
        stack_b.reshape(groups, -1, 2 * local_width),
        weights,
        tuple(t.astype(jnp.int32) for t in tables),
    )
    chosen_out, filled_out = post_table(
        out_owner[mine], out_rank[mine], alive_mine, groups, capacity
    )
    arrived_parts = lax.all_to_all(
        pack_parts(parts, chosen_out, filled_out), "tensor", split_axis=0, concat_axis=0, tiled=True
    )
    mixed = (
        collect_parts(
            arrived_parts, out_owner, out_local, out_rank, alive, mine, capacity, per_device
        )
        + cross_bias
    )
    cross_out = (start_wide * mixed + start_wide).astype(jnp.bfloat16)
    chosen_in, filled_in = post_table(in_owner[mine], in_rank[mine], alive_mine, groups, capacity)
    arrived_back = lax.all_to_all(
        pack_parts(back_parts, chosen_in, filled_in),
        "tensor",
        split_axis=0,
        concat_axis=0,
        tiled=True,
    )
    grad_start = collect_parts(
        arrived_back, in_owner, in_local, in_rank, alive, mine, capacity, per_device
    )
    grad_blocks = lax.psum_scatter(block_terms, "dp", scatter_dimension=1, tiled=True).astype(
        jnp.float32
    )
    grad_start = grad_start + cot_wide * mixed + cot_wide
    sigma = jax.nn.sigmoid(preact)
    grad_pre = grad_start * sigma * (1.0 + preact * (1.0 - sigma))
    grad_pre_low = grad_pre.astype(jnp.bfloat16)
    taken = dense
    grad_bottom = lax.psum_scatter(
        group_outer(taken, grad_pre_low),
        "dp",
        scatter_dimension=0,
        tiled=True,
    ).astype(jnp.float32)
    bias_sums = lax.psum((jnp.sum(grad_pre, axis=0), jnp.sum(grad_mixed, axis=0)), "dp")
    return (cross_out, grad_bottom, bias_sums[0], grad_blocks, bias_sums[1])


def solution(mesh):
    return jax.shard_map(
        on_device,
        mesh=mesh,
        in_specs=(
            P("dp", None),
            P(None, "tensor"),
            P("tensor"),
            P("tensor", "dp", None),
            P("tensor"),
            P("dp", "tensor"),
            P(),
            P(),
            P(),
        ),
        out_specs=(
            P("dp", "tensor"),
            P("dp", "tensor"),
            P("tensor"),
            P("tensor", "dp", None),
            P("tensor"),
        ),
        check_vma=False,
    )
```

```python
import functools

import jax
import jax.numpy as jnp
from jax import lax
from jax.sharding import PartitionSpec as P
from jax.experimental import pallas as pl
from jax.experimental.pallas import tpu as pltpu

BLK = 512
SLOTS = 10


def slot_ranks(owner, alive):
    order = jnp.arange(owner.shape[1])
    earlier = order[None, :] < order[:, None]
    same = (owner[:, :, None] == owner[:, None, :]) & alive[:, None, :] & earlier[None, :, :]
    return jnp.sum(same.astype(jnp.int32), axis=2)


def post_table(owner_mine, rank_mine, alive_mine, groups, capacity):
    slot_count = owner_mine.shape[0]
    match = (
        (owner_mine[None, None, :] == jnp.arange(groups)[:, None, None])
        & (rank_mine[None, None, :] == jnp.arange(capacity)[None, :, None])
        & alive_mine[None, None, :]
    )
    chosen = jnp.sum(match.astype(jnp.int32) * jnp.arange(slot_count)[None, None, :], axis=2)
    filled = jnp.any(match, axis=2)
    return (chosen, filled)


def pack_parts(parts, chosen, filled):
    picked = jnp.take(parts, chosen.reshape(-1), axis=0) * filled.reshape(-1)[:, None, None].astype(
        parts.dtype
    )
    return picked.reshape(chosen.shape[0], chosen.shape[1] * parts.shape[1], parts.shape[2])


def collect_parts(received, owner, local, rank, alive, target, capacity, per_device):
    groups, span_rows, block_width = received.shape
    row_count = span_rows // capacity
    match = ((owner == target) & alive)[:, :, None] & (
        rank[:, :, None] == jnp.arange(capacity)[None, None, :]
    )
    matches = match[:, :, :, None] & (
        local[:, :, None, None] == jnp.arange(per_device)[None, None, None, :]
    )
    onehot = (
        jnp.sum(matches.astype(jnp.int32), axis=1)
        .reshape(groups * capacity, per_device)
        .astype(jnp.bfloat16)
    )
    flattened = received.reshape(groups * capacity, row_count, block_width)
    summed = jnp.einsum("irb,il->rlb", flattened, onehot, preferred_element_type=jnp.float32)
    return summed.reshape(row_count, per_device * block_width)

def ring_kernel(n, top, bottom, out_a, out_b, own_sem, send_sem, recv_sem):
    me = lax.axis_index("tensor")
    row = lax.axis_index("dp")
    right = lax.rem(me + 1, n)
    left = lax.rem(me + n - 1, n)
    mesh_ids = pl.DeviceIdType.MESH
    barrier = pltpu.get_barrier_semaphore()
    for neighbour in (left, right):
        pl.semaphore_signal(barrier, inc=1, device_id=(row, neighbour), device_id_type=mesh_ids)
    pl.semaphore_wait(barrier, 2)
    own_a = pltpu.make_async_copy(top, out_a.at[0], own_sem.at[0])
    own_b = pltpu.make_async_copy(bottom, out_b.at[0], own_sem.at[1])
    own_a.start()
    own_b.start()

    def link(out, side, step, target, src=None):
        return pltpu.make_async_remote_copy(
            src_ref=out.at[step] if src is None else src,
            dst_ref=out.at[step],
            send_sem=send_sem.at[side, step],
            recv_sem=recv_sem.at[side, step],
            device_id=(row, target),
            device_id_type=mesh_ids,
        )

    sends = []
    for step in range(1, n):
        if step == 1:
            src_a, src_b = top, bottom
        else:
            link(out_a, 0, step - 1, right).wait_recv()
            link(out_b, 1, step - 1, left).wait_recv()
            src_a, src_b = out_a.at[step - 1], out_b.at[step - 1]
        copy_a = link(out_a, 0, step, right, src_a)
        copy_b = link(out_b, 1, step, left, src_b)
        copy_a.start()
        copy_b.start()
        sends += [copy_a, copy_b]
    link(out_a, 0, n - 1, right).wait_recv()
    link(out_b, 1, n - 1, left).wait_recv()
    for copy in sends:
        copy.wait_send()
    own_a.wait()
    own_b.wait()


def ring_gather(x, axis, n):
    half = x.shape[0] // 2
    shape = jax.ShapeDtypeStruct((n, half, x.shape[1]), x.dtype)
    anywhere = pl.BlockSpec(memory_space=pl.ANY)
    return pl.pallas_call(
        functools.partial(ring_kernel, n),
        out_shape=[shape, shape],
        in_specs=[anywhere, anywhere],
        out_specs=[anywhere, anywhere],
        scratch_shapes=[
            pltpu.SemaphoreType.DMA((2,)),
            pltpu.SemaphoreType.DMA((2, n)),
            pltpu.SemaphoreType.DMA((2, n)),
        ],
        compiler_params=pltpu.CompilerParams(collective_id=0, has_side_effects=True),
    )(x[:half], x[half:])


def take_blocks(stack_a, stack_b, owner, local, me, n):
    steps, half, width = stack_a.shape
    blocks_a = stack_a.reshape(steps, half, width // BLK, BLK)
    blocks_b = stack_b.reshape(steps, half, width // BLK, BLK)
    step_a = (me - owner) % n
    step_b = (owner - me) % n
    top = blocks_a[step_a, :, local, :]
    bottom = blocks_b[step_b, :, local, :]
    return jnp.concatenate([top, bottom], axis=1)


def slot_kernel(sa_i, sb_i, bi, sa_o, sb_o, bo, live, fa, fb, ua, ub, w, part_ref, back_ref, term_ref):
    k = pl.program_id(0)
    on = live[k] > 0
    half = fa.shape[1]
    wk = w[0]
    top_in, bottom_in = fa[0], fb[0]
    top_up, bottom_up = ua[0], ub[0]
    nt = (((1,), (1,)), ((), ()))
    tn = (((0,), (0,)), ((), ()))
    for rows, src in ((slice(0, half), top_in), (slice(half, 2 * half), bottom_in)):
        value = jnp.dot(src, wk, preferred_element_type=jnp.float32)
        part_ref[0, rows, :] = jnp.where(on, value, 0.0).astype(part_ref.dtype)
    for rows, src in ((slice(0, half), top_up), (slice(half, 2 * half), bottom_up)):
        value = lax.dot_general(src, wk, nt, preferred_element_type=jnp.float32)
        back_ref[0, rows, :] = jnp.where(on, value, 0.0).astype(back_ref.dtype)
    term = lax.dot_general(top_in, top_up, tn, preferred_element_type=jnp.float32)
    term = term + lax.dot_general(bottom_in, bottom_up, tn, preferred_element_type=jnp.float32)
    term_ref[0] = jnp.where(on, term, 0.0).astype(term_ref.dtype)


def slot_products(stack_a, stack_b, weights, tables):
    slots, size, _ = weights.shape
    steps, half, width = stack_a.shape
    rows = 2 * half

    def block(step_ref, blk_ref):
        return pl.BlockSpec(
            (1, half, BLK), lambda k, *t: (t[step_ref][k], 0, t[blk_ref][k])
        )

    grid_spec = pltpu.PrefetchScalarGridSpec(
        num_scalar_prefetch=len(tables),
        grid=(slots,),
        in_specs=[
            block(0, 2),
            block(1, 2),
            block(3, 5),
            block(4, 5),
            pl.BlockSpec((1, size, size), lambda k, *t: (k, 0, 0)),
        ],
        out_specs=[
            pl.BlockSpec((1, rows, BLK), lambda k, *t: (k, 0, 0)),
            pl.BlockSpec((1, rows, BLK), lambda k, *t: (k, 0, 0)),
            pl.BlockSpec((1, size, size), lambda k, *t: (k, 0, 0)),
        ],
    )
    return pl.pallas_call(
        slot_kernel,
        grid_spec=grid_spec,
        out_shape=[
            jax.ShapeDtypeStruct((slots, rows, BLK), jnp.bfloat16),
            jax.ShapeDtypeStruct((slots, rows, BLK), jnp.bfloat16),
            jax.ShapeDtypeStruct((slots, size, size), jnp.bfloat16),
        ],
        cost_estimate=pl.CostEstimate(
            flops=6 * slots * rows * size * size,
            bytes_accessed=slots * (4 * rows * BLK + 2 * size * size) * 2,
            transcendentals=0,
        ),
    )(*tables, stack_a, stack_b, stack_a, stack_b, weights)


def outer_kernel(left, right, out):
    out[...] = lax.dot_general(
        left[...], right[...], (((0,), (0,)), ((), ())), preferred_element_type=jnp.float32
    ).astype(out.dtype)


def group_outer(left, right, tile_m=512, tile_n=1024):
    rows, m = left.shape
    n = right.shape[1]
    return pl.pallas_call(
        outer_kernel,
        grid=(m // tile_m, n // tile_n),
        in_specs=[
            pl.BlockSpec((rows, tile_m), lambda i, j: (0, i)),
            pl.BlockSpec((rows, tile_n), lambda i, j: (0, j)),
        ],
        out_specs=pl.BlockSpec((tile_m, tile_n), lambda i, j: (i, j)),
        out_shape=jax.ShapeDtypeStruct((m, n), jnp.bfloat16),
        cost_estimate=pl.CostEstimate(
            flops=2 * rows * m * n, bytes_accessed=2 * (rows * (m + n) + m * n), transcendentals=0
        ),
    )(left, right)


def on_device(
    dense,
    bottom_weight,
    bottom_bias,
    cross_blocks,
    cross_bias,
    cotangent,
    in_blocks,
    out_blocks,
    live_slots,
):
    groups = lax.axis_size("tensor")
    mine = lax.axis_index("tensor")
    row_count = dense.shape[0]
    local_width = bottom_weight.shape[1]
    per_device = local_width // BLK
    capacity = -(-SLOTS // groups)
    preact = jnp.dot(dense, bottom_weight, preferred_element_type=jnp.float32) + bottom_bias
    start = jax.nn.silu(preact).astype(jnp.bfloat16)
    start_wide = start.astype(jnp.float32)
    cot_wide = cotangent.astype(jnp.float32)
    grad_mixed = cot_wide * start_wide
    grad_mixed_low = grad_mixed.astype(jnp.bfloat16)
    alive = jnp.arange(SLOTS)[None, :] < live_slots[:, None]
    alive_mine = alive[mine]
    in_owner = in_blocks // per_device
    in_local = in_blocks % per_device
    out_owner = out_blocks // per_device
    out_local = out_blocks % per_device
    in_rank = slot_ranks(in_owner, alive)
    out_rank = slot_ranks(out_owner, alive)
    combo = jnp.concatenate([start, grad_mixed_low], axis=1)
    stack_a, stack_b = ring_gather(combo, "tensor", groups)
    step_a = lambda owner: (mine - owner) % groups
    step_b = lambda owner: (owner - mine) % groups
    tables = (
        step_a(in_owner[mine]),
        step_b(in_owner[mine]),
        in_local[mine],
        step_a(out_owner[mine]),
        step_b(out_owner[mine]),
        out_local[mine] + per_device,
        alive_mine.astype(jnp.int32),
    )
    weights = lax.all_gather(cross_blocks, "dp", axis=1, tiled=True)
    parts, back_parts, block_terms = slot_products(
        stack_a.reshape(groups, -1, 2 * local_width),
        stack_b.reshape(groups, -1, 2 * local_width),
        weights,
        tuple(t.astype(jnp.int32) for t in tables),
    )
    chosen_out, filled_out = post_table(
        out_owner[mine], out_rank[mine], alive_mine, groups, capacity
    )
    arrived_parts = lax.all_to_all(
        pack_parts(parts, chosen_out, filled_out), "tensor", split_axis=0, concat_axis=0, tiled=True
    )
    mixed = (
        collect_parts(
            arrived_parts, out_owner, out_local, out_rank, alive, mine, capacity, per_device
        )
        + cross_bias
    )
    cross_out = (start_wide * mixed + start_wide).astype(jnp.bfloat16)
    chosen_in, filled_in = post_table(in_owner[mine], in_rank[mine], alive_mine, groups, capacity)
    arrived_back = lax.all_to_all(
        pack_parts(back_parts, chosen_in, filled_in),
        "tensor",
        split_axis=0,
        concat_axis=0,
        tiled=True,
    )
    grad_start = collect_parts(
        arrived_back, in_owner, in_local, in_rank, alive, mine, capacity, per_device
    )
    grad_blocks = lax.psum_scatter(block_terms, "dp", scatter_dimension=1, tiled=True).astype(
        jnp.float32
    )
    grad_start = grad_start + cot_wide * mixed + cot_wide
    sigma = jax.nn.sigmoid(preact)
    grad_pre = grad_start * sigma * (1.0 + preact * (1.0 - sigma))
    grad_pre_low = grad_pre.astype(jnp.bfloat16)
    taken = dense
    grad_bottom = lax.psum_scatter(
        group_outer(taken, grad_pre_low),
        "dp",
        scatter_dimension=0,
        tiled=True,
    ).astype(jnp.float32)
    bias_sums = lax.psum((jnp.sum(grad_pre, axis=0), jnp.sum(grad_mixed, axis=0)), "dp")
    return (cross_out, grad_bottom, bias_sums[0], grad_blocks, bias_sums[1])


def solution(mesh):
    return jax.shard_map(
        on_device,
        mesh=mesh,
        in_specs=(
            P("dp", None),
            P(None, "tensor"),
            P("tensor"),
            P("tensor", "dp", None),
            P("tensor"),
            P("dp", "tensor"),
            P(),
            P(),
            P(),
        ),
        out_specs=(
            P("dp", "tensor"),
            P("dp", "tensor"),
            P("tensor"),
            P("tensor", "dp", None),
            P("tensor"),
        ),
        check_vma=False,
    )
```

```python
import functools

import jax
import jax.numpy as jnp
from jax import lax
from jax.sharding import PartitionSpec as P
from jax.experimental import pallas as pl
from jax.experimental.pallas import tpu as pltpu

BLK = 512
SLOTS = 10
RING_CHUNKS = 4


def slot_ranks(owner, alive):
    order = jnp.arange(owner.shape[1])
    earlier = order[None, :] < order[:, None]
    same = (owner[:, :, None] == owner[:, None, :]) & alive[:, None, :] & earlier[None, :, :]
    return jnp.sum(same.astype(jnp.int32), axis=2)


def post_table(owner_mine, rank_mine, alive_mine, groups, capacity):
    slot_count = owner_mine.shape[0]
    match = (
        (owner_mine[None, None, :] == jnp.arange(groups)[:, None, None])
        & (rank_mine[None, None, :] == jnp.arange(capacity)[None, :, None])
        & alive_mine[None, None, :]
    )
    chosen = jnp.sum(match.astype(jnp.int32) * jnp.arange(slot_count)[None, None, :], axis=2)
    filled = jnp.any(match, axis=2)
    return (chosen, filled)


def pack_parts(parts, chosen, filled):
    picked = jnp.take(parts, chosen.reshape(-1), axis=0) * filled.reshape(-1)[:, None, None].astype(
        parts.dtype
    )
    return picked.reshape(chosen.shape[0], chosen.shape[1] * parts.shape[1], parts.shape[2])


def collect_parts(received, owner, local, rank, alive, target, capacity, per_device):
    groups, span_rows, block_width = received.shape
    row_count = span_rows // capacity
    match = ((owner == target) & alive)[:, :, None] & (
        rank[:, :, None] == jnp.arange(capacity)[None, None, :]
    )
    matches = match[:, :, :, None] & (
        local[:, :, None, None] == jnp.arange(per_device)[None, None, None, :]
    )
    onehot = (
        jnp.sum(matches.astype(jnp.int32), axis=1)
        .reshape(groups * capacity, per_device)
        .astype(jnp.bfloat16)
    )
    flattened = received.reshape(groups * capacity, row_count, block_width)
    summed = jnp.einsum("irb,il->rlb", flattened, onehot, preferred_element_type=jnp.float32)
    return summed.reshape(row_count, per_device * block_width)

def ring_kernel(n, top, bottom, out_a, out_b, own_sem, send_sem, recv_sem):
    me = lax.axis_index("tensor")
    row = lax.axis_index("dp")
    right = lax.rem(me + 1, n)
    left = lax.rem(me + n - 1, n)
    mesh_ids = pl.DeviceIdType.MESH
    barrier = pltpu.get_barrier_semaphore()
    for neighbour in (left, right):
        pl.semaphore_signal(barrier, inc=1, device_id=(row, neighbour), device_id_type=mesh_ids)
    pl.semaphore_wait(barrier, 2)
    own_a = pltpu.make_async_copy(top, out_a.at[0], own_sem.at[0])
    own_b = pltpu.make_async_copy(bottom, out_b.at[0], own_sem.at[1])
    own_a.start()
    own_b.start()

    chunks = send_sem.shape[2]
    rows = top.shape[0] // chunks

    def piece(ref, c):
        return ref.at[pl.ds(c * rows, rows)]

    def link(out, side, step, c, target, src=None):
        return pltpu.make_async_remote_copy(
            src_ref=piece(out.at[step] if src is None else src, c),
            dst_ref=piece(out.at[step], c),
            send_sem=send_sem.at[side, step, c],
            recv_sem=recv_sem.at[side, step, c],
            device_id=(row, target),
            device_id_type=mesh_ids,
        )

    sends = []
    for step in range(1, n):
        for c in range(chunks):
            if step == 1:
                src_a, src_b = top, bottom
            else:
                link(out_a, 0, step - 1, c, right).wait_recv()
                link(out_b, 1, step - 1, c, left).wait_recv()
                src_a, src_b = out_a.at[step - 1], out_b.at[step - 1]
            copy_a = link(out_a, 0, step, c, right, src_a)
            copy_b = link(out_b, 1, step, c, left, src_b)
            copy_a.start()
            copy_b.start()
            sends += [copy_a, copy_b]
    for c in range(chunks):
        link(out_a, 0, n - 1, c, right).wait_recv()
        link(out_b, 1, n - 1, c, left).wait_recv()
    for copy in sends:
        copy.wait_send()
    own_a.wait()
    own_b.wait()


def ring_gather(x, axis, n):
    half = x.shape[0] // 2
    shape = jax.ShapeDtypeStruct((n, half, x.shape[1]), x.dtype)
    anywhere = pl.BlockSpec(memory_space=pl.ANY)
    return pl.pallas_call(
        functools.partial(ring_kernel, n),
        out_shape=[shape, shape],
        in_specs=[anywhere, anywhere],
        out_specs=[anywhere, anywhere],
        scratch_shapes=[
            pltpu.SemaphoreType.DMA((2,)),
            pltpu.SemaphoreType.DMA((2, n, RING_CHUNKS)),
            pltpu.SemaphoreType.DMA((2, n, RING_CHUNKS)),
        ],
        compiler_params=pltpu.CompilerParams(collective_id=0, has_side_effects=True),
    )(x[:half], x[half:])


def take_blocks(stack_a, stack_b, owner, local, me, n):
    steps, half, width = stack_a.shape
    blocks_a = stack_a.reshape(steps, half, width // BLK, BLK)
    blocks_b = stack_b.reshape(steps, half, width // BLK, BLK)
    step_a = (me - owner) % n
    step_b = (owner - me) % n
    top = blocks_a[step_a, :, local, :]
    bottom = blocks_b[step_b, :, local, :]
    return jnp.concatenate([top, bottom], axis=1)


def slot_kernel(sa_i, sb_i, bi, sa_o, sb_o, bo, live, fa, fb, ua, ub, w, part_ref, back_ref, term_ref):
    k = pl.program_id(0)
    on = live[k] > 0
    half = fa.shape[1]
    wk = w[0]
    top_in, bottom_in = fa[0], fb[0]
    top_up, bottom_up = ua[0], ub[0]
    nt = (((1,), (1,)), ((), ()))
    tn = (((0,), (0,)), ((), ()))
    for rows, src in ((slice(0, half), top_in), (slice(half, 2 * half), bottom_in)):
        value = jnp.dot(src, wk, preferred_element_type=jnp.float32)
        part_ref[0, rows, :] = jnp.where(on, value, 0.0).astype(part_ref.dtype)
    for rows, src in ((slice(0, half), top_up), (slice(half, 2 * half), bottom_up)):
        value = lax.dot_general(src, wk, nt, preferred_element_type=jnp.float32)
        back_ref[0, rows, :] = jnp.where(on, value, 0.0).astype(back_ref.dtype)
    term = lax.dot_general(top_in, top_up, tn, preferred_element_type=jnp.float32)
    term = term + lax.dot_general(bottom_in, bottom_up, tn, preferred_element_type=jnp.float32)
    term_ref[0] = jnp.where(on, term, 0.0).astype(term_ref.dtype)


def slot_products(stack_a, stack_b, weights, tables):
    slots, size, _ = weights.shape
    steps, half, width = stack_a.shape
    rows = 2 * half

    def block(step_ref, blk_ref):
        return pl.BlockSpec(
            (1, half, BLK), lambda k, *t: (t[step_ref][k], 0, t[blk_ref][k])
        )

    grid_spec = pltpu.PrefetchScalarGridSpec(
        num_scalar_prefetch=len(tables),
        grid=(slots,),
        in_specs=[
            block(0, 2),
            block(1, 2),
            block(3, 5),
            block(4, 5),
            pl.BlockSpec((1, size, size), lambda k, *t: (k, 0, 0)),
        ],
        out_specs=[
            pl.BlockSpec((1, rows, BLK), lambda k, *t: (k, 0, 0)),
            pl.BlockSpec((1, rows, BLK), lambda k, *t: (k, 0, 0)),
            pl.BlockSpec((1, size, size), lambda k, *t: (k, 0, 0)),
        ],
    )
    return pl.pallas_call(
        slot_kernel,
        grid_spec=grid_spec,
        out_shape=[
            jax.ShapeDtypeStruct((slots, rows, BLK), jnp.bfloat16),
            jax.ShapeDtypeStruct((slots, rows, BLK), jnp.bfloat16),
            jax.ShapeDtypeStruct((slots, size, size), jnp.bfloat16),
        ],
        cost_estimate=pl.CostEstimate(
            flops=6 * slots * rows * size * size,
            bytes_accessed=slots * (4 * rows * BLK + 2 * size * size) * 2,
            transcendentals=0,
        ),
    )(*tables, stack_a, stack_b, stack_a, stack_b, weights)


def outer_kernel(left, right, out):
    out[...] = lax.dot_general(
        left[...], right[...], (((0,), (0,)), ((), ())), preferred_element_type=jnp.float32
    ).astype(out.dtype)


def group_outer(left, right, tile_m=512, tile_n=1024):
    rows, m = left.shape
    n = right.shape[1]
    return pl.pallas_call(
        outer_kernel,
        grid=(m // tile_m, n // tile_n),
        in_specs=[
            pl.BlockSpec((rows, tile_m), lambda i, j: (0, i)),
            pl.BlockSpec((rows, tile_n), lambda i, j: (0, j)),
        ],
        out_specs=pl.BlockSpec((tile_m, tile_n), lambda i, j: (i, j)),
        out_shape=jax.ShapeDtypeStruct((m, n), jnp.bfloat16),
        cost_estimate=pl.CostEstimate(
            flops=2 * rows * m * n, bytes_accessed=2 * (rows * (m + n) + m * n), transcendentals=0
        ),
    )(left, right)


def on_device(
    dense,
    bottom_weight,
    bottom_bias,
    cross_blocks,
    cross_bias,
    cotangent,
    in_blocks,
    out_blocks,
    live_slots,
):
    groups = lax.axis_size("tensor")
    mine = lax.axis_index("tensor")
    row_count = dense.shape[0]
    local_width = bottom_weight.shape[1]
    per_device = local_width // BLK
    capacity = -(-SLOTS // groups)
    preact = jnp.dot(dense, bottom_weight, preferred_element_type=jnp.float32) + bottom_bias
    start = jax.nn.silu(preact).astype(jnp.bfloat16)
    start_wide = start.astype(jnp.float32)
    cot_wide = cotangent.astype(jnp.float32)
    grad_mixed = cot_wide * start_wide
    grad_mixed_low = grad_mixed.astype(jnp.bfloat16)
    alive = jnp.arange(SLOTS)[None, :] < live_slots[:, None]
    alive_mine = alive[mine]
    in_owner = in_blocks // per_device
    in_local = in_blocks % per_device
    out_owner = out_blocks // per_device
    out_local = out_blocks % per_device
    in_rank = slot_ranks(in_owner, alive)
    out_rank = slot_ranks(out_owner, alive)
    combo = jnp.concatenate([start, grad_mixed_low], axis=1)
    stack_a, stack_b = ring_gather(combo, "tensor", groups)
    step_a = lambda owner: (mine - owner) % groups
    step_b = lambda owner: (owner - mine) % groups
    tables = (
        step_a(in_owner[mine]),
        step_b(in_owner[mine]),
        in_local[mine],
        step_a(out_owner[mine]),
        step_b(out_owner[mine]),
        out_local[mine] + per_device,
        alive_mine.astype(jnp.int32),
    )
    weights = lax.all_gather(cross_blocks, "dp", axis=1, tiled=True)
    parts, back_parts, block_terms = slot_products(
        stack_a.reshape(groups, -1, 2 * local_width),
        stack_b.reshape(groups, -1, 2 * local_width),
        weights,
        tuple(t.astype(jnp.int32) for t in tables),
    )
    chosen_out, filled_out = post_table(
        out_owner[mine], out_rank[mine], alive_mine, groups, capacity
    )
    arrived_parts = lax.all_to_all(
        pack_parts(parts, chosen_out, filled_out), "tensor", split_axis=0, concat_axis=0, tiled=True
    )
    mixed = (
        collect_parts(
            arrived_parts, out_owner, out_local, out_rank, alive, mine, capacity, per_device
        )
        + cross_bias
    )
    cross_out = (start_wide * mixed + start_wide).astype(jnp.bfloat16)
    chosen_in, filled_in = post_table(in_owner[mine], in_rank[mine], alive_mine, groups, capacity)
    arrived_back = lax.all_to_all(
        pack_parts(back_parts, chosen_in, filled_in),
        "tensor",
        split_axis=0,
        concat_axis=0,
        tiled=True,
    )
    grad_start = collect_parts(
        arrived_back, in_owner, in_local, in_rank, alive, mine, capacity, per_device
    )
    grad_blocks = lax.psum_scatter(block_terms, "dp", scatter_dimension=1, tiled=True).astype(
        jnp.float32
    )
    grad_start = grad_start + cot_wide * mixed + cot_wide
    sigma = jax.nn.sigmoid(preact)
    grad_pre = grad_start * sigma * (1.0 + preact * (1.0 - sigma))
    grad_pre_low = grad_pre.astype(jnp.bfloat16)
    taken = dense
    grad_bottom = lax.psum_scatter(
        group_outer(taken, grad_pre_low),
        "dp",
        scatter_dimension=0,
        tiled=True,
    ).astype(jnp.float32)
    bias_sums = lax.psum((jnp.sum(grad_pre, axis=0), jnp.sum(grad_mixed, axis=0)), "dp")
    return (cross_out, grad_bottom, bias_sums[0], grad_blocks, bias_sums[1])


def solution(mesh):
    return jax.shard_map(
        on_device,
        mesh=mesh,
        in_specs=(
            P("dp", None),
            P(None, "tensor"),
            P("tensor"),
            P("tensor", "dp", None),
            P("tensor"),
            P("dp", "tensor"),
            P(),
            P(),
            P(),
        ),
        out_specs=(
            P("dp", "tensor"),
            P("dp", "tensor"),
            P("tensor"),
            P("tensor", "dp", None),
            P("tensor"),
        ),
        check_vma=False,
    )
```

```python
import functools

import jax
import jax.numpy as jnp
from jax import lax
from jax.sharding import PartitionSpec as P
from jax.experimental import pallas as pl
from jax.experimental.pallas import tpu as pltpu

BLK = 512
SLOTS = 10
RING_CHUNKS = 4


def slot_ranks(owner, alive):
    order = jnp.arange(owner.shape[1])
    earlier = order[None, :] < order[:, None]
    same = (owner[:, :, None] == owner[:, None, :]) & alive[:, None, :] & earlier[None, :, :]
    return jnp.sum(same.astype(jnp.int32), axis=2)


def post_table(owner_mine, rank_mine, alive_mine, groups, capacity):
    slot_count = owner_mine.shape[0]
    match = (
        (owner_mine[None, None, :] == jnp.arange(groups)[:, None, None])
        & (rank_mine[None, None, :] == jnp.arange(capacity)[None, :, None])
        & alive_mine[None, None, :]
    )
    chosen = jnp.sum(match.astype(jnp.int32) * jnp.arange(slot_count)[None, None, :], axis=2)
    filled = jnp.any(match, axis=2)
    return (chosen, filled)


def pack_parts(parts, chosen, filled):
    picked = jnp.take(parts, chosen.reshape(-1), axis=0) * filled.reshape(-1)[:, None, None].astype(
        parts.dtype
    )
    return picked.reshape(chosen.shape[0], chosen.shape[1] * parts.shape[1], parts.shape[2])


def collect_parts(received, owner, local, rank, alive, target, capacity, per_device):
    groups, span_rows, block_width = received.shape
    row_count = span_rows // capacity
    match = ((owner == target) & alive)[:, :, None] & (
        rank[:, :, None] == jnp.arange(capacity)[None, None, :]
    )
    matches = match[:, :, :, None] & (
        local[:, :, None, None] == jnp.arange(per_device)[None, None, None, :]
    )
    onehot = (
        jnp.sum(matches.astype(jnp.int32), axis=1)
        .reshape(groups * capacity, per_device)
        .astype(jnp.bfloat16)
    )
    flattened = received.reshape(groups * capacity, row_count, block_width)
    summed = jnp.einsum("irb,il->rlb", flattened, onehot, preferred_element_type=jnp.float32)
    return summed.reshape(row_count, per_device * block_width)

def ring_kernel(n, top, bottom, out_a, out_b, own_sem, send_sem, recv_sem):
    me = lax.axis_index("tensor")
    row = lax.axis_index("dp")
    right = lax.rem(me + 1, n)
    left = lax.rem(me + n - 1, n)
    mesh_ids = pl.DeviceIdType.MESH
    barrier = pltpu.get_barrier_semaphore()
    for neighbour in (left, right):
        pl.semaphore_signal(barrier, inc=1, device_id=(row, neighbour), device_id_type=mesh_ids)
    pl.semaphore_wait(barrier, 2)
    own_a = pltpu.make_async_copy(top, out_a.at[0], own_sem.at[0])
    own_b = pltpu.make_async_copy(bottom, out_b.at[0], own_sem.at[1])
    own_a.start()
    own_b.start()

    chunks = send_sem.shape[2]
    rows = top.shape[0] // chunks

    def piece(ref, c):
        return ref.at[pl.ds(c * rows, rows)]

    def link(out, side, step, c, target, src=None):
        return pltpu.make_async_remote_copy(
            src_ref=piece(out.at[step] if src is None else src, c),
            dst_ref=piece(out.at[step], c),
            send_sem=send_sem.at[side, step, c],
            recv_sem=recv_sem.at[side, step, c],
            device_id=(row, target),
            device_id_type=mesh_ids,
        )

    sends = []
    for step in range(1, n):
        for c in range(chunks):
            if step == 1:
                src_a, src_b = top, bottom
            else:
                link(out_a, 0, step - 1, c, right).wait_recv()
                link(out_b, 1, step - 1, c, left).wait_recv()
                src_a, src_b = out_a.at[step - 1], out_b.at[step - 1]
            copy_a = link(out_a, 0, step, c, right, src_a)
            copy_b = link(out_b, 1, step, c, left, src_b)
            copy_a.start()
            copy_b.start()
            sends += [copy_a, copy_b]
    for c in range(chunks):
        link(out_a, 0, n - 1, c, right).wait_recv()
        link(out_b, 1, n - 1, c, left).wait_recv()
    for copy in sends:
        copy.wait_send()
    own_a.wait()
    own_b.wait()


def ring_gather(x, axis, n):
    half = x.shape[0] // 2
    shape = jax.ShapeDtypeStruct((n, half, x.shape[1]), x.dtype)
    anywhere = pl.BlockSpec(memory_space=pl.ANY)
    return pl.pallas_call(
        functools.partial(ring_kernel, n),
        out_shape=[shape, shape],
        in_specs=[anywhere, anywhere],
        out_specs=[anywhere, anywhere],
        scratch_shapes=[
            pltpu.SemaphoreType.DMA((2,)),
            pltpu.SemaphoreType.DMA((2, n, RING_CHUNKS)),
            pltpu.SemaphoreType.DMA((2, n, RING_CHUNKS)),
        ],
        compiler_params=pltpu.CompilerParams(collective_id=0, has_side_effects=True),
    )(x[:half], x[half:])


def exchange_kernel(n, first, second, out_first, out_second, own_sem, send_sem, recv_sem):
    me = lax.axis_index("tensor")
    row = lax.axis_index("dp")
    mesh_ids = pl.DeviceIdType.MESH
    barrier = pltpu.get_barrier_semaphore()
    for offset in range(1, n):
        peer = lax.rem(me + offset, n)
        pl.semaphore_signal(barrier, inc=1, device_id=(row, peer), device_id_type=mesh_ids)
    pl.semaphore_wait(barrier, n - 1)
    pairs = ((first, out_first), (second, out_second))
    own = [
        pltpu.make_async_copy(src.at[me], dst.at[me], own_sem.at[side])
        for side, (src, dst) in enumerate(pairs)
    ]
    for copy in own:
        copy.start()

    def link(side, peer, slot):
        src, dst = pairs[side]
        return pltpu.make_async_remote_copy(
            src_ref=src.at[peer],
            dst_ref=dst.at[slot],
            send_sem=send_sem.at[side, peer],
            recv_sem=recv_sem.at[side, slot],
            device_id=(row, peer),
            device_id_type=mesh_ids,
        )

    sends = []
    for offset in (1, n - 1, 2, n - 2, 3, n - 3, 4)[: n - 1]:
        peer = lax.rem(me + offset, n)
        for side in range(2):
            copy = link(side, peer, me)
            copy.start()
            sends.append(copy)
    for offset in range(1, n):
        source = lax.rem(me + offset, n)
        for side in range(2):
            link(side, source, source).wait_recv()
    for copy in sends:
        copy.wait_send()
    for copy in own:
        copy.wait()


def exchange(first, second, n):
    anywhere = pl.BlockSpec(memory_space=pl.ANY)
    return pl.pallas_call(
        functools.partial(exchange_kernel, n),
        out_shape=[
            jax.ShapeDtypeStruct(first.shape, first.dtype),
            jax.ShapeDtypeStruct(second.shape, second.dtype),
        ],
        in_specs=[anywhere, anywhere],
        out_specs=[anywhere, anywhere],
        scratch_shapes=[
            pltpu.SemaphoreType.DMA((2,)),
            pltpu.SemaphoreType.DMA((2, n)),
            pltpu.SemaphoreType.DMA((2, n)),
        ],
        compiler_params=pltpu.CompilerParams(collective_id=1, has_side_effects=True),
    )(first, second)


def take_blocks(stack_a, stack_b, owner, local, me, n):
    steps, half, width = stack_a.shape
    blocks_a = stack_a.reshape(steps, half, width // BLK, BLK)
    blocks_b = stack_b.reshape(steps, half, width // BLK, BLK)
    step_a = (me - owner) % n
    step_b = (owner - me) % n
    top = blocks_a[step_a, :, local, :]
    bottom = blocks_b[step_b, :, local, :]
    return jnp.concatenate([top, bottom], axis=1)


def slot_kernel(sa_i, sb_i, bi, sa_o, sb_o, bo, live, fa, fb, ua, ub, w, part_ref, back_ref, term_ref):
    k = pl.program_id(0)
    on = live[k] > 0
    half = fa.shape[1]
    wk = w[0]
    top_in, bottom_in = fa[0], fb[0]
    top_up, bottom_up = ua[0], ub[0]
    nt = (((1,), (1,)), ((), ()))
    tn = (((0,), (0,)), ((), ()))
    for rows, src in ((slice(0, half), top_in), (slice(half, 2 * half), bottom_in)):
        value = jnp.dot(src, wk, preferred_element_type=jnp.float32)
        part_ref[0, rows, :] = jnp.where(on, value, 0.0).astype(part_ref.dtype)
    for rows, src in ((slice(0, half), top_up), (slice(half, 2 * half), bottom_up)):
        value = lax.dot_general(src, wk, nt, preferred_element_type=jnp.float32)
        back_ref[0, rows, :] = jnp.where(on, value, 0.0).astype(back_ref.dtype)
    term = lax.dot_general(top_in, top_up, tn, preferred_element_type=jnp.float32)
    term = term + lax.dot_general(bottom_in, bottom_up, tn, preferred_element_type=jnp.float32)
    term_ref[0] = jnp.where(on, term, 0.0).astype(term_ref.dtype)


def slot_products(stack_a, stack_b, weights, tables):
    slots, size, _ = weights.shape
    steps, half, width = stack_a.shape
    rows = 2 * half

    def block(step_ref, blk_ref):
        return pl.BlockSpec(
            (1, half, BLK), lambda k, *t: (t[step_ref][k], 0, t[blk_ref][k])
        )

    grid_spec = pltpu.PrefetchScalarGridSpec(
        num_scalar_prefetch=len(tables),
        grid=(slots,),
        in_specs=[
            block(0, 2),
            block(1, 2),
            block(3, 5),
            block(4, 5),
            pl.BlockSpec((1, size, size), lambda k, *t: (k, 0, 0)),
        ],
        out_specs=[
            pl.BlockSpec((1, rows, BLK), lambda k, *t: (k, 0, 0)),
            pl.BlockSpec((1, rows, BLK), lambda k, *t: (k, 0, 0)),
            pl.BlockSpec((1, size, size), lambda k, *t: (k, 0, 0)),
        ],
    )
    return pl.pallas_call(
        slot_kernel,
        grid_spec=grid_spec,
        out_shape=[
            jax.ShapeDtypeStruct((slots, rows, BLK), jnp.bfloat16),
            jax.ShapeDtypeStruct((slots, rows, BLK), jnp.bfloat16),
            jax.ShapeDtypeStruct((slots, size, size), jnp.bfloat16),
        ],
        cost_estimate=pl.CostEstimate(
            flops=6 * slots * rows * size * size,
            bytes_accessed=slots * (4 * rows * BLK + 2 * size * size) * 2,
            transcendentals=0,
        ),
    )(*tables, stack_a, stack_b, stack_a, stack_b, weights)


def outer_kernel(left, right, out):
    out[...] = lax.dot_general(
        left[...], right[...], (((0,), (0,)), ((), ())), preferred_element_type=jnp.float32
    ).astype(out.dtype)


def group_outer(left, right, tile_m=512, tile_n=1024):
    rows, m = left.shape
    n = right.shape[1]
    return pl.pallas_call(
        outer_kernel,
        grid=(m // tile_m, n // tile_n),
        in_specs=[
            pl.BlockSpec((rows, tile_m), lambda i, j: (0, i)),
            pl.BlockSpec((rows, tile_n), lambda i, j: (0, j)),
        ],
        out_specs=pl.BlockSpec((tile_m, tile_n), lambda i, j: (i, j)),
        out_shape=jax.ShapeDtypeStruct((m, n), jnp.bfloat16),
        cost_estimate=pl.CostEstimate(
            flops=2 * rows * m * n, bytes_accessed=2 * (rows * (m + n) + m * n), transcendentals=0
        ),
    )(left, right)


def on_device(
    dense,
    bottom_weight,
    bottom_bias,
    cross_blocks,
    cross_bias,
    cotangent,
    in_blocks,
    out_blocks,
    live_slots,
):
    groups = lax.axis_size("tensor")
    mine = lax.axis_index("tensor")
    row_count = dense.shape[0]
    local_width = bottom_weight.shape[1]
    per_device = local_width // BLK
    capacity = -(-SLOTS // groups)
    preact = jnp.dot(dense, bottom_weight, preferred_element_type=jnp.float32) + bottom_bias
    start = jax.nn.silu(preact).astype(jnp.bfloat16)
    start_wide = start.astype(jnp.float32)
    cot_wide = cotangent.astype(jnp.float32)
    grad_mixed = cot_wide * start_wide
    grad_mixed_low = grad_mixed.astype(jnp.bfloat16)
    alive = jnp.arange(SLOTS)[None, :] < live_slots[:, None]
    alive_mine = alive[mine]
    in_owner = in_blocks // per_device
    in_local = in_blocks % per_device
    out_owner = out_blocks // per_device
    out_local = out_blocks % per_device
    in_rank = slot_ranks(in_owner, alive)
    out_rank = slot_ranks(out_owner, alive)
    combo = jnp.concatenate([start, grad_mixed_low], axis=1)
    stack_a, stack_b = ring_gather(combo, "tensor", groups)
    step_a = lambda owner: (mine - owner) % groups
    step_b = lambda owner: (owner - mine) % groups
    tables = (
        step_a(in_owner[mine]),
        step_b(in_owner[mine]),
        in_local[mine],
        step_a(out_owner[mine]),
        step_b(out_owner[mine]),
        out_local[mine] + per_device,
        alive_mine.astype(jnp.int32),
    )
    weights = lax.all_gather(cross_blocks, "dp", axis=1, tiled=True)
    parts, back_parts, block_terms = slot_products(
        stack_a.reshape(groups, -1, 2 * local_width),
        stack_b.reshape(groups, -1, 2 * local_width),
        weights,
        tuple(t.astype(jnp.int32) for t in tables),
    )
    chosen_out, filled_out = post_table(
        out_owner[mine], out_rank[mine], alive_mine, groups, capacity
    )
    chosen_in, filled_in = post_table(in_owner[mine], in_rank[mine], alive_mine, groups, capacity)
    arrived_parts, arrived_back = exchange(
        pack_parts(parts, chosen_out, filled_out),
        pack_parts(back_parts, chosen_in, filled_in),
        groups,
    )
    mixed = (
        collect_parts(
            arrived_parts, out_owner, out_local, out_rank, alive, mine, capacity, per_device
        )
        + cross_bias
    )
    cross_out = (start_wide * mixed + start_wide).astype(jnp.bfloat16)
    grad_start = collect_parts(
        arrived_back, in_owner, in_local, in_rank, alive, mine, capacity, per_device
    )
    grad_blocks = lax.psum_scatter(block_terms, "dp", scatter_dimension=1, tiled=True).astype(
        jnp.float32
    )
    grad_start = grad_start + cot_wide * mixed + cot_wide
    sigma = jax.nn.sigmoid(preact)
    grad_pre = grad_start * sigma * (1.0 + preact * (1.0 - sigma))
    grad_pre_low = grad_pre.astype(jnp.bfloat16)
    taken = dense
    grad_bottom = lax.psum_scatter(
        group_outer(taken, grad_pre_low),
        "dp",
        scatter_dimension=0,
        tiled=True,
    ).astype(jnp.float32)
    bias_sums = lax.psum((jnp.sum(grad_pre, axis=0), jnp.sum(grad_mixed, axis=0)), "dp")
    return (cross_out, grad_bottom, bias_sums[0], grad_blocks, bias_sums[1])


def solution(mesh):
    return jax.shard_map(
        on_device,
        mesh=mesh,
        in_specs=(
            P("dp", None),
            P(None, "tensor"),
            P("tensor"),
            P("tensor", "dp", None),
            P("tensor"),
            P("dp", "tensor"),
            P(),
            P(),
            P(),
        ),
        out_specs=(
            P("dp", "tensor"),
            P("dp", "tensor"),
            P("tensor"),
            P("tensor", "dp", None),
            P("tensor"),
        ),
        check_vma=False,
    )
```

```python
import functools

import jax
import jax.numpy as jnp
from jax import lax
from jax.sharding import PartitionSpec as P
from jax.experimental import pallas as pl
from jax.experimental.pallas import tpu as pltpu

BLK = 512
SLOTS = 10
RING_CHUNKS = 4


def slot_ranks(owner, alive):
    order = jnp.arange(owner.shape[1])
    earlier = order[None, :] < order[:, None]
    same = (owner[:, :, None] == owner[:, None, :]) & alive[:, None, :] & earlier[None, :, :]
    return jnp.sum(same.astype(jnp.int32), axis=2)


def post_table(owner_mine, rank_mine, alive_mine, groups, capacity):
    slot_count = owner_mine.shape[0]
    match = (
        (owner_mine[None, None, :] == jnp.arange(groups)[:, None, None])
        & (rank_mine[None, None, :] == jnp.arange(capacity)[None, :, None])
        & alive_mine[None, None, :]
    )
    chosen = jnp.sum(match.astype(jnp.int32) * jnp.arange(slot_count)[None, None, :], axis=2)
    filled = jnp.any(match, axis=2)
    return (chosen, filled)


def pack_parts(parts, chosen, filled):
    picked = jnp.take(parts, chosen.reshape(-1), axis=0) * filled.reshape(-1)[:, None, None].astype(
        parts.dtype
    )
    return picked.reshape(chosen.shape[0], chosen.shape[1] * parts.shape[1], parts.shape[2])


def collect_parts(received, owner, local, rank, alive, target, capacity, per_device):
    groups, span_rows, block_width = received.shape
    row_count = span_rows // capacity
    match = ((owner == target) & alive)[:, :, None] & (
        rank[:, :, None] == jnp.arange(capacity)[None, None, :]
    )
    matches = match[:, :, :, None] & (
        local[:, :, None, None] == jnp.arange(per_device)[None, None, None, :]
    )
    onehot = (
        jnp.sum(matches.astype(jnp.int32), axis=1)
        .reshape(groups * capacity, per_device)
        .astype(jnp.bfloat16)
    )
    flattened = received.reshape(groups * capacity, row_count, block_width)
    summed = jnp.einsum("irb,il->rlb", flattened, onehot, preferred_element_type=jnp.float32)
    return summed.reshape(row_count, per_device * block_width)

def ring_kernel(n, top, bottom, out_a, out_b, own_sem, send_sem, recv_sem):
    me = lax.axis_index("tensor")
    row = lax.axis_index("dp")
    right = lax.rem(me + 1, n)
    left = lax.rem(me + n - 1, n)
    mesh_ids = pl.DeviceIdType.MESH
    barrier = pltpu.get_barrier_semaphore()
    for neighbour in (left, right):
        pl.semaphore_signal(barrier, inc=1, device_id=(row, neighbour), device_id_type=mesh_ids)
    pl.semaphore_wait(barrier, 2)
    own_a = pltpu.make_async_copy(top, out_a.at[0], own_sem.at[0])
    own_b = pltpu.make_async_copy(bottom, out_b.at[0], own_sem.at[1])
    own_a.start()
    own_b.start()

    chunks = send_sem.shape[2]
    rows = top.shape[0] // chunks

    def piece(ref, c):
        return ref.at[pl.ds(c * rows, rows)]

    def link(out, side, step, c, target, src=None):
        return pltpu.make_async_remote_copy(
            src_ref=piece(out.at[step] if src is None else src, c),
            dst_ref=piece(out.at[step], c),
            send_sem=send_sem.at[side, step, c],
            recv_sem=recv_sem.at[side, step, c],
            device_id=(row, target),
            device_id_type=mesh_ids,
        )

    sends = []
    for step in range(1, n):
        for c in range(chunks):
            if step == 1:
                src_a, src_b = top, bottom
            else:
                link(out_a, 0, step - 1, c, right).wait_recv()
                link(out_b, 1, step - 1, c, left).wait_recv()
                src_a, src_b = out_a.at[step - 1], out_b.at[step - 1]
            copy_a = link(out_a, 0, step, c, right, src_a)
            copy_b = link(out_b, 1, step, c, left, src_b)
            copy_a.start()
            copy_b.start()
            sends += [copy_a, copy_b]
    for c in range(chunks):
        link(out_a, 0, n - 1, c, right).wait_recv()
        link(out_b, 1, n - 1, c, left).wait_recv()
    for copy in sends:
        copy.wait_send()
    own_a.wait()
    own_b.wait()


def ring_gather(x, axis, n):
    half = x.shape[0] // 2
    shape = jax.ShapeDtypeStruct((n, half, x.shape[1]), x.dtype)
    anywhere = pl.BlockSpec(memory_space=pl.ANY)
    return pl.pallas_call(
        functools.partial(ring_kernel, n),
        out_shape=[shape, shape],
        in_specs=[anywhere, anywhere],
        out_specs=[anywhere, anywhere],
        scratch_shapes=[
            pltpu.SemaphoreType.DMA((2,)),
            pltpu.SemaphoreType.DMA((2, n, RING_CHUNKS)),
            pltpu.SemaphoreType.DMA((2, n, RING_CHUNKS)),
        ],
        compiler_params=pltpu.CompilerParams(collective_id=0, has_side_effects=True),
    )(x[:half], x[half:])


def exchange_kernel(n, first, second, out_first, out_second, own_sem, send_sem, recv_sem):
    me = lax.axis_index("tensor")
    row = lax.axis_index("dp")
    mesh_ids = pl.DeviceIdType.MESH
    barrier = pltpu.get_barrier_semaphore()
    for offset in range(1, n):
        peer = lax.rem(me + offset, n)
        pl.semaphore_signal(barrier, inc=1, device_id=(row, peer), device_id_type=mesh_ids)
    pl.semaphore_wait(barrier, n - 1)
    pairs = ((first, out_first), (second, out_second))
    own = [
        pltpu.make_async_copy(src.at[me], dst.at[me], own_sem.at[side])
        for side, (src, dst) in enumerate(pairs)
    ]
    for copy in own:
        copy.start()

    def link(side, peer, slot):
        src, dst = pairs[side]
        return pltpu.make_async_remote_copy(
            src_ref=src.at[peer],
            dst_ref=dst.at[slot],
            send_sem=send_sem.at[side, peer],
            recv_sem=recv_sem.at[side, slot],
            device_id=(row, peer),
            device_id_type=mesh_ids,
        )

    sends = []
    for offset in (1, n - 1, 2, n - 2, 3, n - 3, 4)[: n - 1]:
        peer = lax.rem(me + offset, n)
        for side in range(2):
            copy = link(side, peer, me)
            copy.start()
            sends.append(copy)
    for offset in range(1, n):
        source = lax.rem(me + offset, n)
        for side in range(2):
            link(side, source, source).wait_recv()
    for copy in sends:
        copy.wait_send()
    for copy in own:
        copy.wait()


def exchange(first, second, n):
    anywhere = pl.BlockSpec(memory_space=pl.ANY)
    return pl.pallas_call(
        functools.partial(exchange_kernel, n),
        out_shape=[
            jax.ShapeDtypeStruct(first.shape, first.dtype),
            jax.ShapeDtypeStruct(second.shape, second.dtype),
        ],
        in_specs=[anywhere, anywhere],
        out_specs=[anywhere, anywhere],
        scratch_shapes=[
            pltpu.SemaphoreType.DMA((2,)),
            pltpu.SemaphoreType.DMA((2, n)),
            pltpu.SemaphoreType.DMA((2, n)),
        ],
        compiler_params=pltpu.CompilerParams(collective_id=1, has_side_effects=True),
    )(first, second)


def take_blocks(stack_a, stack_b, owner, local, me, n):
    steps, half, width = stack_a.shape
    blocks_a = stack_a.reshape(steps, half, width // BLK, BLK)
    blocks_b = stack_b.reshape(steps, half, width // BLK, BLK)
    step_a = (me - owner) % n
    step_b = (owner - me) % n
    top = blocks_a[step_a, :, local, :]
    bottom = blocks_b[step_b, :, local, :]
    return jnp.concatenate([top, bottom], axis=1)


def slot_kernel(sa_i, sb_i, bi, sa_o, sb_o, bo, live, fa, fb, ua, ub, w, part_ref, back_ref, term_ref):
    k = pl.program_id(0)
    on = live[k] > 0
    half = fa.shape[1]
    wk = w[0]
    top_in, bottom_in = fa[0], fb[0]
    top_up, bottom_up = ua[0], ub[0]
    nt = (((1,), (1,)), ((), ()))
    tn = (((0,), (0,)), ((), ()))
    for rows, src in ((slice(0, half), top_in), (slice(half, 2 * half), bottom_in)):
        value = jnp.dot(src, wk, preferred_element_type=jnp.float32)
        part_ref[0, rows, :] = jnp.where(on, value, 0.0).astype(part_ref.dtype)
    for rows, src in ((slice(0, half), top_up), (slice(half, 2 * half), bottom_up)):
        value = lax.dot_general(src, wk, nt, preferred_element_type=jnp.float32)
        back_ref[0, rows, :] = jnp.where(on, value, 0.0).astype(back_ref.dtype)
    term = lax.dot_general(top_in, top_up, tn, preferred_element_type=jnp.float32)
    term = term + lax.dot_general(bottom_in, bottom_up, tn, preferred_element_type=jnp.float32)
    term_ref[0] = jnp.where(on, term, 0.0).astype(term_ref.dtype)


def slot_products(stack_a, stack_b, weights, tables):
    slots, size, _ = weights.shape
    steps, half, width = stack_a.shape
    rows = 2 * half

    def block(step_ref, blk_ref):
        return pl.BlockSpec(
            (1, half, BLK), lambda k, *t: (t[step_ref][k], 0, t[blk_ref][k])
        )

    grid_spec = pltpu.PrefetchScalarGridSpec(
        num_scalar_prefetch=len(tables),
        grid=(slots,),
        in_specs=[
            block(0, 2),
            block(1, 2),
            block(3, 5),
            block(4, 5),
            pl.BlockSpec((1, size, size), lambda k, *t: (k, 0, 0)),
        ],
        out_specs=[
            pl.BlockSpec((1, rows, BLK), lambda k, *t: (k, 0, 0)),
            pl.BlockSpec((1, rows, BLK), lambda k, *t: (k, 0, 0)),
            pl.BlockSpec((1, size, size), lambda k, *t: (k, 0, 0)),
        ],
    )
    return pl.pallas_call(
        slot_kernel,
        grid_spec=grid_spec,
        out_shape=[
            jax.ShapeDtypeStruct((slots, rows, BLK), jnp.bfloat16),
            jax.ShapeDtypeStruct((slots, rows, BLK), jnp.bfloat16),
            jax.ShapeDtypeStruct((slots, size, size), jnp.bfloat16),
        ],
        cost_estimate=pl.CostEstimate(
            flops=6 * slots * rows * size * size,
            bytes_accessed=slots * (4 * rows * BLK + 2 * size * size) * 2,
            transcendentals=0,
        ),
    )(*tables, stack_a, stack_b, stack_a, stack_b, weights)


def outer_kernel(left, right, out):
    out[...] = lax.dot_general(
        left[...], right[...], (((0,), (0,)), ((), ())), preferred_element_type=jnp.float32
    ).astype(out.dtype)


def group_outer(left, right, core, tile_m=128, tile_n=1024):
    rows, m = left.shape
    n = right.shape[1]

    def place(i, j, c):
        return ((1 - c[0]) * i + c[0] * ((i % 4) * 4 + i // 4), j)

    grid_spec = pltpu.PrefetchScalarGridSpec(
        num_scalar_prefetch=1,
        grid=(m // tile_m, n // tile_n),
        in_specs=[
            pl.BlockSpec((rows, tile_m), lambda i, j, c: (0, i)),
            pl.BlockSpec((rows, tile_n), lambda i, j, c: (0, j)),
        ],
        out_specs=pl.BlockSpec((tile_m, tile_n), place),
    )
    return pl.pallas_call(
        lambda c, left_ref, right_ref, out_ref: outer_kernel(left_ref, right_ref, out_ref),
        grid_spec=grid_spec,
        out_shape=jax.ShapeDtypeStruct((m, n), jnp.bfloat16),
        cost_estimate=pl.CostEstimate(
            flops=2 * rows * m * n, bytes_accessed=2 * (rows * (m + n) + m * n), transcendentals=0
        ),
    )(core.reshape(1), left, right)


def reduce_kernel(side, part, out, send1, recv1, acc1, send2, recv2, sems1, sems2):
    core = lax.axis_index("tensor") % 2
    me = lax.axis_index("dp")
    column = lax.axis_index("tensor")
    hi, lo = me // side, me % side
    p1 = (1 - core) * hi + core * lo
    p2 = (1 - core) * lo + core * hi
    mesh_ids = pl.DeviceIdType.MESH
    half = part.shape[2] // 2
    halves = (pl.ds(0, half), pl.ds(half, half))

    def device(q1, q2):
        q1, q2 = q1 % side, q2 % side
        return (1 - core) * (q1 * side + q2) + core * (q2 * side + q1)

    ring1 = (device(p1 + 1, p2), device(p1 - 1, p2))
    ring2 = (device(p1, p2 + 1), device(p1, p2 - 1))
    barrier = pltpu.get_barrier_semaphore()
    for target in ring1 + ring2:
        pl.semaphore_signal(barrier, inc=1, device_id=(target, column), device_id_type=mesh_ids)
    pl.semaphore_wait(barrier, 4)

    def link(send, recv, sems, d, step, target):
        return pltpu.make_async_remote_copy(
            src_ref=send.at[d, step],
            dst_ref=recv.at[d, step],
            send_sem=sems.at[0, d, step],
            recv_sem=sems.at[1, d, step],
            device_id=(target, column),
            device_id_type=mesh_ids,
        )

    def own1(k, d):
        return part[pl.ds(k * side, side), :, halves[d]].astype(jnp.float32)

    def own2(k, d):
        return acc1[k, :, halves[d]]

    sends = []
    for stage, (send, recv, sems, ring, pos, own) in enumerate(
        ((send1, recv1, sems1, ring1, p1, own1), (send2, recv2, sems2, ring2, p2, own2))
    ):
        for step in range(side - 1):
            for d, sign in ((0, 1), (1, -1)):
                k = (pos - sign * (1 + step)) % side
                value = own(k, d)
                if step > 0:
                    link(send, recv, sems, d, step - 1, ring[d]).wait_recv()
                    value = value + recv[d, step - 1].astype(jnp.float32)
                send[d, step] = value.astype(send.dtype)
                copy = link(send, recv, sems, d, step, ring[d])
                copy.start()
                sends.append(copy)
        for d in range(2):
            link(send, recv, sems, d, side - 2, ring[d]).wait_recv()
            total = own(pos, d) + recv[d, side - 2].astype(jnp.float32)
            if stage == 0:
                acc1[:, :, halves[d]] = total
            else:
                out[:, halves[d]] = total
    for copy in sends:
        copy.wait_send()


def reduce_rows(part, side):
    chunk, width = part.shape[0] // (side * side), part.shape[1]
    part = part.reshape(side * side, chunk, width)
    vmem = pl.BlockSpec(memory_space=pltpu.VMEM)
    return pl.pallas_call(
        functools.partial(reduce_kernel, side),
        out_shape=jax.ShapeDtypeStruct((chunk, width), jnp.float32),
        in_specs=[vmem],
        out_specs=vmem,
        scratch_shapes=[
            pltpu.VMEM((2, side - 1, side, chunk, width // 2), jnp.bfloat16),
            pltpu.VMEM((2, side - 1, side, chunk, width // 2), jnp.bfloat16),
            pltpu.VMEM((side, chunk, width), jnp.float32),
            pltpu.VMEM((2, side - 1, chunk, width // 2), jnp.bfloat16),
            pltpu.VMEM((2, side - 1, chunk, width // 2), jnp.bfloat16),
            pltpu.SemaphoreType.DMA((2, 2, side - 1)),
            pltpu.SemaphoreType.DMA((2, 2, side - 1)),
        ],
        compiler_params=pltpu.CompilerParams(
            collective_id=2, has_side_effects=True, vmem_limit_bytes=60 * 1024 * 1024
        ),
    )(part)

def on_device(
    dense,
    bottom_weight,
    bottom_bias,
    cross_blocks,
    cross_bias,
    cotangent,
    in_blocks,
    out_blocks,
    live_slots,
):
    groups = lax.axis_size("tensor")
    mine = lax.axis_index("tensor")
    row_count = dense.shape[0]
    local_width = bottom_weight.shape[1]
    per_device = local_width // BLK
    capacity = -(-SLOTS // groups)
    preact = jnp.dot(dense, bottom_weight, preferred_element_type=jnp.float32) + bottom_bias
    start = jax.nn.silu(preact).astype(jnp.bfloat16)
    start_wide = start.astype(jnp.float32)
    cot_wide = cotangent.astype(jnp.float32)
    grad_mixed = cot_wide * start_wide
    grad_mixed_low = grad_mixed.astype(jnp.bfloat16)
    alive = jnp.arange(SLOTS)[None, :] < live_slots[:, None]
    alive_mine = alive[mine]
    in_owner = in_blocks // per_device
    in_local = in_blocks % per_device
    out_owner = out_blocks // per_device
    out_local = out_blocks % per_device
    in_rank = slot_ranks(in_owner, alive)
    out_rank = slot_ranks(out_owner, alive)
    combo = jnp.concatenate([start, grad_mixed_low], axis=1)
    stack_a, stack_b = ring_gather(combo, "tensor", groups)
    step_a = lambda owner: (mine - owner) % groups
    step_b = lambda owner: (owner - mine) % groups
    tables = (
        step_a(in_owner[mine]),
        step_b(in_owner[mine]),
        in_local[mine],
        step_a(out_owner[mine]),
        step_b(out_owner[mine]),
        out_local[mine] + per_device,
        alive_mine.astype(jnp.int32),
    )
    weights = lax.all_gather(cross_blocks, "dp", axis=1, tiled=True)
    parts, back_parts, block_terms = slot_products(
        stack_a.reshape(groups, -1, 2 * local_width),
        stack_b.reshape(groups, -1, 2 * local_width),
        weights,
        tuple(t.astype(jnp.int32) for t in tables),
    )
    chosen_out, filled_out = post_table(
        out_owner[mine], out_rank[mine], alive_mine, groups, capacity
    )
    chosen_in, filled_in = post_table(in_owner[mine], in_rank[mine], alive_mine, groups, capacity)
    arrived_parts, arrived_back = exchange(
        pack_parts(parts, chosen_out, filled_out),
        pack_parts(back_parts, chosen_in, filled_in),
        groups,
    )
    mixed = (
        collect_parts(
            arrived_parts, out_owner, out_local, out_rank, alive, mine, capacity, per_device
        )
        + cross_bias
    )
    cross_out = (start_wide * mixed + start_wide).astype(jnp.bfloat16)
    grad_start = collect_parts(
        arrived_back, in_owner, in_local, in_rank, alive, mine, capacity, per_device
    )
    grad_blocks = lax.psum_scatter(block_terms, "dp", scatter_dimension=1, tiled=True).astype(
        jnp.float32
    )
    grad_start = grad_start + cot_wide * mixed + cot_wide
    sigma = jax.nn.sigmoid(preact)
    grad_pre = grad_start * sigma * (1.0 + preact * (1.0 - sigma))
    grad_pre_low = grad_pre.astype(jnp.bfloat16)
    taken = dense
    side = int(round(lax.axis_size("dp") ** 0.5))
    grad_bottom = reduce_rows(group_outer(taken, grad_pre_low, (mine % 2).astype(jnp.int32)), side)
    bias_sums = lax.psum((jnp.sum(grad_pre, axis=0), jnp.sum(grad_mixed, axis=0)), "dp")
    return (cross_out, grad_bottom, bias_sums[0], grad_blocks, bias_sums[1])


def solution(mesh):
    return jax.shard_map(
        on_device,
        mesh=mesh,
        in_specs=(
            P("dp", None),
            P(None, "tensor"),
            P("tensor"),
            P("tensor", "dp", None),
            P("tensor"),
            P("dp", "tensor"),
            P(),
            P(),
            P(),
        ),
        out_specs=(
            P("dp", "tensor"),
            P("dp", "tensor"),
            P("tensor"),
            P("tensor", "dp", None),
            P("tensor"),
        ),
        check_vma=False,
    )
```

```python
import functools

import jax
import jax.numpy as jnp
from jax import lax
from jax.sharding import PartitionSpec as P
from jax.experimental import pallas as pl
from jax.experimental.pallas import tpu as pltpu

BLK = 512
SLOTS = 10
RING_CHUNKS = 4


def slot_ranks(owner, alive):
    order = jnp.arange(owner.shape[1])
    earlier = order[None, :] < order[:, None]
    same = (owner[:, :, None] == owner[:, None, :]) & alive[:, None, :] & earlier[None, :, :]
    return jnp.sum(same.astype(jnp.int32), axis=2)


def post_table(owner_mine, rank_mine, alive_mine, groups, capacity):
    slot_count = owner_mine.shape[0]
    match = (
        (owner_mine[None, None, :] == jnp.arange(groups)[:, None, None])
        & (rank_mine[None, None, :] == jnp.arange(capacity)[None, :, None])
        & alive_mine[None, None, :]
    )
    chosen = jnp.sum(match.astype(jnp.int32) * jnp.arange(slot_count)[None, None, :], axis=2)
    filled = jnp.any(match, axis=2)
    return (chosen, filled)


def pack_parts(parts, chosen, filled):
    picked = jnp.take(parts, chosen.reshape(-1), axis=0) * filled.reshape(-1)[:, None, None].astype(
        parts.dtype
    )
    return picked.reshape(chosen.shape[0], chosen.shape[1] * parts.shape[1], parts.shape[2])


def collect_parts(received, owner, local, rank, alive, target, capacity, per_device):
    groups, span_rows, block_width = received.shape
    row_count = span_rows // capacity
    match = ((owner == target) & alive)[:, :, None] & (
        rank[:, :, None] == jnp.arange(capacity)[None, None, :]
    )
    matches = match[:, :, :, None] & (
        local[:, :, None, None] == jnp.arange(per_device)[None, None, None, :]
    )
    onehot = (
        jnp.sum(matches.astype(jnp.int32), axis=1)
        .reshape(groups * capacity, per_device)
        .astype(jnp.bfloat16)
    )
    flattened = received.reshape(groups * capacity, row_count, block_width)
    summed = jnp.einsum("irb,il->rlb", flattened, onehot, preferred_element_type=jnp.float32)
    return summed.reshape(row_count, per_device * block_width)

def ring_kernel(n, top, bottom, out_a, out_b, own_sem, send_sem, recv_sem):
    me = lax.axis_index("tensor")
    row = lax.axis_index("dp")
    right = lax.rem(me + 1, n)
    left = lax.rem(me + n - 1, n)
    mesh_ids = pl.DeviceIdType.MESH
    barrier = pltpu.get_barrier_semaphore()
    for neighbour in (left, right):
        pl.semaphore_signal(barrier, inc=1, device_id=(row, neighbour), device_id_type=mesh_ids)
    pl.semaphore_wait(barrier, 2)
    own_a = pltpu.make_async_copy(top, out_a.at[0], own_sem.at[0])
    own_b = pltpu.make_async_copy(bottom, out_b.at[0], own_sem.at[1])
    own_a.start()
    own_b.start()

    chunks = send_sem.shape[2]
    rows = top.shape[0] // chunks

    def piece(ref, c):
        return ref.at[pl.ds(c * rows, rows)]

    def link(out, side, step, c, target, src=None):
        return pltpu.make_async_remote_copy(
            src_ref=piece(out.at[step] if src is None else src, c),
            dst_ref=piece(out.at[step], c),
            send_sem=send_sem.at[side, step, c],
            recv_sem=recv_sem.at[side, step, c],
            device_id=(row, target),
            device_id_type=mesh_ids,
        )

    sends = []
    for step in range(1, n):
        for c in range(chunks):
            if step == 1:
                src_a, src_b = top, bottom
            else:
                link(out_a, 0, step - 1, c, right).wait_recv()
                link(out_b, 1, step - 1, c, left).wait_recv()
                src_a, src_b = out_a.at[step - 1], out_b.at[step - 1]
            copy_a = link(out_a, 0, step, c, right, src_a)
            copy_b = link(out_b, 1, step, c, left, src_b)
            copy_a.start()
            copy_b.start()
            sends += [copy_a, copy_b]
    for c in range(chunks):
        link(out_a, 0, n - 1, c, right).wait_recv()
        link(out_b, 1, n - 1, c, left).wait_recv()
    for copy in sends:
        copy.wait_send()
    own_a.wait()
    own_b.wait()


def ring_gather(x, axis, n):
    half = x.shape[0] // 2
    shape = jax.ShapeDtypeStruct((n, half, x.shape[1]), x.dtype)
    anywhere = pl.BlockSpec(memory_space=pl.ANY)
    return pl.pallas_call(
        functools.partial(ring_kernel, n),
        out_shape=[shape, shape],
        in_specs=[anywhere, anywhere],
        out_specs=[anywhere, anywhere],
        scratch_shapes=[
            pltpu.SemaphoreType.DMA((2,)),
            pltpu.SemaphoreType.DMA((2, n, RING_CHUNKS)),
            pltpu.SemaphoreType.DMA((2, n, RING_CHUNKS)),
        ],
        compiler_params=pltpu.CompilerParams(collective_id=0, has_side_effects=True),
    )(x[:half], x[half:])


def exchange_kernel(n, first, second, out_first, out_second, own_sem, send_sem, recv_sem):
    me = lax.axis_index("tensor")
    row = lax.axis_index("dp")
    mesh_ids = pl.DeviceIdType.MESH
    barrier = pltpu.get_barrier_semaphore()
    for offset in range(1, n):
        peer = lax.rem(me + offset, n)
        pl.semaphore_signal(barrier, inc=1, device_id=(row, peer), device_id_type=mesh_ids)
    pl.semaphore_wait(barrier, n - 1)
    pairs = ((first, out_first), (second, out_second))
    own = [
        pltpu.make_async_copy(src.at[me], dst.at[me], own_sem.at[side])
        for side, (src, dst) in enumerate(pairs)
    ]
    for copy in own:
        copy.start()

    def link(side, peer, slot):
        src, dst = pairs[side]
        return pltpu.make_async_remote_copy(
            src_ref=src.at[peer],
            dst_ref=dst.at[slot],
            send_sem=send_sem.at[side, peer],
            recv_sem=recv_sem.at[side, slot],
            device_id=(row, peer),
            device_id_type=mesh_ids,
        )

    sends = []
    for offset in (1, n - 1, 2, n - 2, 3, n - 3, 4)[: n - 1]:
        peer = lax.rem(me + offset, n)
        for side in range(2):
            copy = link(side, peer, me)
            copy.start()
            sends.append(copy)
    for offset in range(1, n):
        source = lax.rem(me + offset, n)
        for side in range(2):
            link(side, source, source).wait_recv()
    for copy in sends:
        copy.wait_send()
    for copy in own:
        copy.wait()


def exchange(first, second, n):
    anywhere = pl.BlockSpec(memory_space=pl.ANY)
    return pl.pallas_call(
        functools.partial(exchange_kernel, n),
        out_shape=[
            jax.ShapeDtypeStruct(first.shape, first.dtype),
            jax.ShapeDtypeStruct(second.shape, second.dtype),
        ],
        in_specs=[anywhere, anywhere],
        out_specs=[anywhere, anywhere],
        scratch_shapes=[
            pltpu.SemaphoreType.DMA((2,)),
            pltpu.SemaphoreType.DMA((2, n)),
            pltpu.SemaphoreType.DMA((2, n)),
        ],
        compiler_params=pltpu.CompilerParams(collective_id=1, has_side_effects=True),
    )(first, second)


def take_blocks(stack_a, stack_b, owner, local, me, n):
    steps, half, width = stack_a.shape
    blocks_a = stack_a.reshape(steps, half, width // BLK, BLK)
    blocks_b = stack_b.reshape(steps, half, width // BLK, BLK)
    step_a = (me - owner) % n
    step_b = (owner - me) % n
    top = blocks_a[step_a, :, local, :]
    bottom = blocks_b[step_b, :, local, :]
    return jnp.concatenate([top, bottom], axis=1)


def slot_kernel(sa_i, sb_i, bi, sa_o, sb_o, bo, live, fa, fb, ua, ub, w, part_ref, back_ref, term_ref):
    k = pl.program_id(0)
    on = live[k] > 0
    half = fa.shape[1]
    wk = w[0]
    top_in, bottom_in = fa[0], fb[0]
    top_up, bottom_up = ua[0], ub[0]
    nt = (((1,), (1,)), ((), ()))
    tn = (((0,), (0,)), ((), ()))
    for rows, src in ((slice(0, half), top_in), (slice(half, 2 * half), bottom_in)):
        value = jnp.dot(src, wk, preferred_element_type=jnp.float32)
        part_ref[0, rows, :] = jnp.where(on, value, 0.0).astype(part_ref.dtype)
    for rows, src in ((slice(0, half), top_up), (slice(half, 2 * half), bottom_up)):
        value = lax.dot_general(src, wk, nt, preferred_element_type=jnp.float32)
        back_ref[0, rows, :] = jnp.where(on, value, 0.0).astype(back_ref.dtype)
    term = lax.dot_general(top_in, top_up, tn, preferred_element_type=jnp.float32)
    term = term + lax.dot_general(bottom_in, bottom_up, tn, preferred_element_type=jnp.float32)
    term_ref[0] = jnp.where(on, term, 0.0).astype(term_ref.dtype)


def slot_products(stack_a, stack_b, weights, tables):
    slots, size, _ = weights.shape
    steps, half, width = stack_a.shape
    rows = 2 * half

    def block(step_ref, blk_ref):
        return pl.BlockSpec(
            (1, half, BLK), lambda k, *t: (t[step_ref][k], 0, t[blk_ref][k])
        )

    grid_spec = pltpu.PrefetchScalarGridSpec(
        num_scalar_prefetch=len(tables),
        grid=(slots,),
        in_specs=[
            block(0, 2),
            block(1, 2),
            block(3, 5),
            block(4, 5),
            pl.BlockSpec((1, size, size), lambda k, *t: (k, 0, 0)),
        ],
        out_specs=[
            pl.BlockSpec((1, rows, BLK), lambda k, *t: (k, 0, 0)),
            pl.BlockSpec((1, rows, BLK), lambda k, *t: (k, 0, 0)),
            pl.BlockSpec((1, size, size), lambda k, *t: (k, 0, 0)),
        ],
    )
    return pl.pallas_call(
        slot_kernel,
        grid_spec=grid_spec,
        out_shape=[
            jax.ShapeDtypeStruct((slots, rows, BLK), jnp.bfloat16),
            jax.ShapeDtypeStruct((slots, rows, BLK), jnp.bfloat16),
            jax.ShapeDtypeStruct((slots, size, size), jnp.bfloat16),
        ],
        cost_estimate=pl.CostEstimate(
            flops=6 * slots * rows * size * size,
            bytes_accessed=slots * (4 * rows * BLK + 2 * size * size) * 2,
            transcendentals=0,
        ),
    )(*tables, stack_a, stack_b, stack_a, stack_b, weights)


def outer_kernel(left, right, out):
    out[...] = lax.dot_general(
        left[...], right[...], (((0,), (0,)), ((), ())), preferred_element_type=jnp.float32
    ).astype(out.dtype)


def group_outer(left, right, tile_m=512, tile_n=1024):
    rows, m = left.shape
    n = right.shape[1]
    return pl.pallas_call(
        outer_kernel,
        grid=(m // tile_m, n // tile_n),
        in_specs=[
            pl.BlockSpec((rows, tile_m), lambda i, j: (0, i)),
            pl.BlockSpec((rows, tile_n), lambda i, j: (0, j)),
        ],
        out_specs=pl.BlockSpec((tile_m, tile_n), lambda i, j: (i, j)),
        out_shape=jax.ShapeDtypeStruct((m, n), jnp.bfloat16),
        cost_estimate=pl.CostEstimate(
            flops=2 * rows * m * n, bytes_accessed=2 * (rows * (m + n) + m * n), transcendentals=0
        ),
    )(left, right)


def reduce_kernel(side, part, out, send1, recv1, acc1, send2, recv2, sems1, sems2):
    core = lax.axis_index("tensor") % 2
    me = lax.axis_index("dp")
    column = lax.axis_index("tensor")
    hi, lo = me // side, me % side
    p1 = (1 - core) * hi + core * lo
    p2 = (1 - core) * lo + core * hi
    mesh_ids = pl.DeviceIdType.MESH
    half = part.shape[3] // 2
    halves = (pl.ds(0, half), pl.ds(half, half))

    def device(q1, q2):
        q1, q2 = q1 % side, q2 % side
        return (1 - core) * (q1 * side + q2) + core * (q2 * side + q1)

    ring1 = (device(p1 + 1, p2), device(p1 - 1, p2))
    ring2 = (device(p1, p2 + 1), device(p1, p2 - 1))
    barrier = pltpu.get_barrier_semaphore()
    for target in ring1 + ring2:
        pl.semaphore_signal(barrier, inc=1, device_id=(target, column), device_id_type=mesh_ids)
    pl.semaphore_wait(barrier, 4)

    def link(send, recv, sems, d, step, target):
        return pltpu.make_async_remote_copy(
            src_ref=send.at[d, step],
            dst_ref=recv.at[d, step],
            send_sem=sems.at[0, d, step],
            recv_sem=sems.at[1, d, step],
            device_id=(target, column),
            device_id_type=mesh_ids,
        )

    def own1(k, d):
        lead = part[k, :, :, halves[d]]
        cross = part[:, k, :, halves[d]]
        return jnp.where(core == 0, lead, cross).astype(jnp.float32)

    def own2(k, d):
        return acc1[k, :, halves[d]]

    sends = []
    for stage, (send, recv, sems, ring, pos, own) in enumerate(
        ((send1, recv1, sems1, ring1, p1, own1), (send2, recv2, sems2, ring2, p2, own2))
    ):
        for step in range(side - 1):
            for d, sign in ((0, 1), (1, -1)):
                k = (pos - sign * (1 + step)) % side
                value = own(k, d)
                if step > 0:
                    link(send, recv, sems, d, step - 1, ring[d]).wait_recv()
                    value = value + recv[d, step - 1].astype(jnp.float32)
                send[d, step] = value.astype(send.dtype)
                copy = link(send, recv, sems, d, step, ring[d])
                copy.start()
                sends.append(copy)
        for d in range(2):
            link(send, recv, sems, d, side - 2, ring[d]).wait_recv()
            total = own(pos, d) + recv[d, side - 2].astype(jnp.float32)
            if stage == 0:
                acc1[:, :, halves[d]] = total
            else:
                out[:, halves[d]] = total
    for copy in sends:
        copy.wait_send()


def reduce_rows(part, side):
    chunk, width = part.shape[0] // (side * side), part.shape[1]
    part = part.reshape(side, side, chunk, width)
    vmem = pl.BlockSpec(memory_space=pltpu.VMEM)
    return pl.pallas_call(
        functools.partial(reduce_kernel, side),
        out_shape=jax.ShapeDtypeStruct((chunk, width), jnp.float32),
        in_specs=[vmem],
        out_specs=vmem,
        scratch_shapes=[
            pltpu.VMEM((2, side - 1, side, chunk, width // 2), jnp.bfloat16),
            pltpu.VMEM((2, side - 1, side, chunk, width // 2), jnp.bfloat16),
            pltpu.VMEM((side, chunk, width), jnp.float32),
            pltpu.VMEM((2, side - 1, chunk, width // 2), jnp.bfloat16),
            pltpu.VMEM((2, side - 1, chunk, width // 2), jnp.bfloat16),
            pltpu.SemaphoreType.DMA((2, 2, side - 1)),
            pltpu.SemaphoreType.DMA((2, 2, side - 1)),
        ],
        compiler_params=pltpu.CompilerParams(
            collective_id=2, has_side_effects=True, vmem_limit_bytes=60 * 1024 * 1024
        ),
    )(part)

def on_device(
    dense,
    bottom_weight,
    bottom_bias,
    cross_blocks,
    cross_bias,
    cotangent,
    in_blocks,
    out_blocks,
    live_slots,
):
    groups = lax.axis_size("tensor")
    mine = lax.axis_index("tensor")
    row_count = dense.shape[0]
    local_width = bottom_weight.shape[1]
    per_device = local_width // BLK
    capacity = -(-SLOTS // groups)
    preact = jnp.dot(dense, bottom_weight, preferred_element_type=jnp.float32) + bottom_bias
    start = jax.nn.silu(preact).astype(jnp.bfloat16)
    start_wide = start.astype(jnp.float32)
    cot_wide = cotangent.astype(jnp.float32)
    grad_mixed = cot_wide * start_wide
    grad_mixed_low = grad_mixed.astype(jnp.bfloat16)
    alive = jnp.arange(SLOTS)[None, :] < live_slots[:, None]
    alive_mine = alive[mine]
    in_owner = in_blocks // per_device
    in_local = in_blocks % per_device
    out_owner = out_blocks // per_device
    out_local = out_blocks % per_device
    in_rank = slot_ranks(in_owner, alive)
    out_rank = slot_ranks(out_owner, alive)
    combo = jnp.concatenate([start, grad_mixed_low], axis=1)
    stack_a, stack_b = ring_gather(combo, "tensor", groups)
    step_a = lambda owner: (mine - owner) % groups
    step_b = lambda owner: (owner - mine) % groups
    tables = (
        step_a(in_owner[mine]),
        step_b(in_owner[mine]),
        in_local[mine],
        step_a(out_owner[mine]),
        step_b(out_owner[mine]),
        out_local[mine] + per_device,
        alive_mine.astype(jnp.int32),
    )
    weights = lax.all_gather(cross_blocks, "dp", axis=1, tiled=True)
    parts, back_parts, block_terms = slot_products(
        stack_a.reshape(groups, -1, 2 * local_width),
        stack_b.reshape(groups, -1, 2 * local_width),
        weights,
        tuple(t.astype(jnp.int32) for t in tables),
    )
    chosen_out, filled_out = post_table(
        out_owner[mine], out_rank[mine], alive_mine, groups, capacity
    )
    chosen_in, filled_in = post_table(in_owner[mine], in_rank[mine], alive_mine, groups, capacity)
    arrived_parts, arrived_back = exchange(
        pack_parts(parts, chosen_out, filled_out),
        pack_parts(back_parts, chosen_in, filled_in),
        groups,
    )
    mixed = (
        collect_parts(
            arrived_parts, out_owner, out_local, out_rank, alive, mine, capacity, per_device
        )
        + cross_bias
    )
    cross_out = (start_wide * mixed + start_wide).astype(jnp.bfloat16)
    grad_start = collect_parts(
        arrived_back, in_owner, in_local, in_rank, alive, mine, capacity, per_device
    )
    grad_blocks = lax.psum_scatter(block_terms, "dp", scatter_dimension=1, tiled=True).astype(
        jnp.float32
    )
    grad_start = grad_start + cot_wide * mixed + cot_wide
    sigma = jax.nn.sigmoid(preact)
    grad_pre = grad_start * sigma * (1.0 + preact * (1.0 - sigma))
    grad_pre_low = grad_pre.astype(jnp.bfloat16)
    taken = dense
    side = int(round(lax.axis_size("dp") ** 0.5))
    grad_bottom = reduce_rows(group_outer(taken, grad_pre_low), side)
    grad_bias_bottom = jnp.sum(lax.all_gather(jnp.sum(grad_pre, axis=0), "dp"), axis=0)
    grad_bias = jnp.sum(lax.all_gather(jnp.sum(grad_mixed, axis=0), "dp"), axis=0)
    return (cross_out, grad_bottom, grad_bias_bottom, grad_blocks, grad_bias)


def solution(mesh):
    return jax.shard_map(
        on_device,
        mesh=mesh,
        in_specs=(
            P("dp", None),
            P(None, "tensor"),
            P("tensor"),
            P("tensor", "dp", None),
            P("tensor"),
            P("dp", "tensor"),
            P(),
            P(),
            P(),
        ),
        out_specs=(
            P("dp", "tensor"),
            P("dp", "tensor"),
            P("tensor"),
            P("tensor", "dp", None),
            P("tensor"),
        ),
        check_vma=False,
    )
```

```python
import functools

import jax
import jax.numpy as jnp
from jax import lax
from jax.sharding import PartitionSpec as P
from jax.experimental import pallas as pl
from jax.experimental.pallas import tpu as pltpu

BLK = 512
SLOTS = 10
RING_CHUNKS = 4


def slot_ranks(owner, alive):
    order = jnp.arange(owner.shape[1])
    earlier = order[None, :] < order[:, None]
    same = (owner[:, :, None] == owner[:, None, :]) & alive[:, None, :] & earlier[None, :, :]
    return jnp.sum(same.astype(jnp.int32), axis=2)


def post_table(owner_mine, rank_mine, alive_mine, groups, capacity):
    slot_count = owner_mine.shape[0]
    match = (
        (owner_mine[None, None, :] == jnp.arange(groups)[:, None, None])
        & (rank_mine[None, None, :] == jnp.arange(capacity)[None, :, None])
        & alive_mine[None, None, :]
    )
    chosen = jnp.sum(match.astype(jnp.int32) * jnp.arange(slot_count)[None, None, :], axis=2)
    filled = jnp.any(match, axis=2)
    return (chosen, filled)


def pack_parts(parts, chosen, filled):
    picked = jnp.take(parts, chosen.reshape(-1), axis=0) * filled.reshape(-1)[:, None, None].astype(
        parts.dtype
    )
    return picked.reshape(chosen.shape[0], chosen.shape[1] * parts.shape[1], parts.shape[2])


def collect_parts(received, owner, local, rank, alive, target, capacity, per_device):
    groups, span_rows, block_width = received.shape
    row_count = span_rows // capacity
    match = ((owner == target) & alive)[:, :, None] & (
        rank[:, :, None] == jnp.arange(capacity)[None, None, :]
    )
    matches = match[:, :, :, None] & (
        local[:, :, None, None] == jnp.arange(per_device)[None, None, None, :]
    )
    onehot = (
        jnp.sum(matches.astype(jnp.int32), axis=1)
        .reshape(groups * capacity, per_device)
        .astype(jnp.bfloat16)
    )
    flattened = received.reshape(groups * capacity, row_count, block_width)
    summed = jnp.einsum("irb,il->rlb", flattened, onehot, preferred_element_type=jnp.float32)
    return summed.reshape(row_count, per_device * block_width)

def ring_kernel(n, top, bottom, out_a, out_b, own_sem, send_sem, recv_sem):
    me = lax.axis_index("tensor")
    row = lax.axis_index("dp")
    right = lax.rem(me + 1, n)
    left = lax.rem(me + n - 1, n)
    mesh_ids = pl.DeviceIdType.MESH
    barrier = pltpu.get_barrier_semaphore()
    for neighbour in (left, right):
        pl.semaphore_signal(barrier, inc=1, device_id=(row, neighbour), device_id_type=mesh_ids)
    pl.semaphore_wait(barrier, 2)
    own_a = pltpu.make_async_copy(top, out_a.at[0], own_sem.at[0])
    own_b = pltpu.make_async_copy(bottom, out_b.at[0], own_sem.at[1])
    own_a.start()
    own_b.start()

    chunks = send_sem.shape[2]
    rows = top.shape[0] // chunks

    def piece(ref, c):
        return ref.at[pl.ds(c * rows, rows)]

    def link(out, side, step, c, target, src=None):
        return pltpu.make_async_remote_copy(
            src_ref=piece(out.at[step] if src is None else src, c),
            dst_ref=piece(out.at[step], c),
            send_sem=send_sem.at[side, step, c],
            recv_sem=recv_sem.at[side, step, c],
            device_id=(row, target),
            device_id_type=mesh_ids,
        )

    sends = []
    for step in range(1, n):
        for c in range(chunks):
            if step == 1:
                src_a, src_b = top, bottom
            else:
                link(out_a, 0, step - 1, c, right).wait_recv()
                link(out_b, 1, step - 1, c, left).wait_recv()
                src_a, src_b = out_a.at[step - 1], out_b.at[step - 1]
            copy_a = link(out_a, 0, step, c, right, src_a)
            copy_b = link(out_b, 1, step, c, left, src_b)
            copy_a.start()
            copy_b.start()
            sends += [copy_a, copy_b]
    for c in range(chunks):
        link(out_a, 0, n - 1, c, right).wait_recv()
        link(out_b, 1, n - 1, c, left).wait_recv()
    for copy in sends:
        copy.wait_send()
    own_a.wait()
    own_b.wait()


def ring_gather(x, axis, n):
    half = x.shape[0] // 2
    shape = jax.ShapeDtypeStruct((n, half, x.shape[1]), x.dtype)
    anywhere = pl.BlockSpec(memory_space=pl.ANY)
    return pl.pallas_call(
        functools.partial(ring_kernel, n),
        out_shape=[shape, shape],
        in_specs=[anywhere, anywhere],
        out_specs=[anywhere, anywhere],
        scratch_shapes=[
            pltpu.SemaphoreType.DMA((2,)),
            pltpu.SemaphoreType.DMA((2, n, RING_CHUNKS)),
            pltpu.SemaphoreType.DMA((2, n, RING_CHUNKS)),
        ],
        compiler_params=pltpu.CompilerParams(collective_id=0, has_side_effects=True),
    )(x[:half], x[half:])


def exchange_kernel(n, first, second, out_first, out_second, own_sem, send_sem, recv_sem):
    me = lax.axis_index("tensor")
    row = lax.axis_index("dp")
    mesh_ids = pl.DeviceIdType.MESH
    barrier = pltpu.get_barrier_semaphore()
    for offset in range(1, n):
        peer = lax.rem(me + offset, n)
        pl.semaphore_signal(barrier, inc=1, device_id=(row, peer), device_id_type=mesh_ids)
    pl.semaphore_wait(barrier, n - 1)
    pairs = ((first, out_first), (second, out_second))
    own = [
        pltpu.make_async_copy(src.at[me], dst.at[me], own_sem.at[side])
        for side, (src, dst) in enumerate(pairs)
    ]
    for copy in own:
        copy.start()

    def link(side, peer, slot):
        src, dst = pairs[side]
        return pltpu.make_async_remote_copy(
            src_ref=src.at[peer],
            dst_ref=dst.at[slot],
            send_sem=send_sem.at[side, peer],
            recv_sem=recv_sem.at[side, slot],
            device_id=(row, peer),
            device_id_type=mesh_ids,
        )

    sends = []
    for offset in (1, n - 1, 2, n - 2, 3, n - 3, 4)[: n - 1]:
        peer = lax.rem(me + offset, n)
        for side in range(2):
            copy = link(side, peer, me)
            copy.start()
            sends.append(copy)
    for offset in range(1, n):
        source = lax.rem(me + offset, n)
        for side in range(2):
            link(side, source, source).wait_recv()
    for copy in sends:
        copy.wait_send()
    for copy in own:
        copy.wait()


def exchange(first, second, n):
    anywhere = pl.BlockSpec(memory_space=pl.ANY)
    return pl.pallas_call(
        functools.partial(exchange_kernel, n),
        out_shape=[
            jax.ShapeDtypeStruct(first.shape, first.dtype),
            jax.ShapeDtypeStruct(second.shape, second.dtype),
        ],
        in_specs=[anywhere, anywhere],
        out_specs=[anywhere, anywhere],
        scratch_shapes=[
            pltpu.SemaphoreType.DMA((2,)),
            pltpu.SemaphoreType.DMA((2, n)),
            pltpu.SemaphoreType.DMA((2, n)),
        ],
        compiler_params=pltpu.CompilerParams(collective_id=1, has_side_effects=True),
    )(first, second)


def take_blocks(stack_a, stack_b, owner, local, me, n):
    steps, half, width = stack_a.shape
    blocks_a = stack_a.reshape(steps, half, width // BLK, BLK)
    blocks_b = stack_b.reshape(steps, half, width // BLK, BLK)
    step_a = (me - owner) % n
    step_b = (owner - me) % n
    top = blocks_a[step_a, :, local, :]
    bottom = blocks_b[step_b, :, local, :]
    return jnp.concatenate([top, bottom], axis=1)


def slot_kernel(sa_i, sb_i, bi, sa_o, sb_o, bo, live, fa, fb, ua, ub, w, part_ref, back_ref, term_ref):
    k = pl.program_id(0)
    on = live[k] > 0
    half = fa.shape[1]
    wk = w[0]
    top_in, bottom_in = fa[0], fb[0]
    top_up, bottom_up = ua[0], ub[0]
    nt = (((1,), (1,)), ((), ()))
    tn = (((0,), (0,)), ((), ()))
    for rows, src in ((slice(0, half), top_in), (slice(half, 2 * half), bottom_in)):
        value = jnp.dot(src, wk, preferred_element_type=jnp.float32)
        part_ref[0, rows, :] = jnp.where(on, value, 0.0).astype(part_ref.dtype)
    for rows, src in ((slice(0, half), top_up), (slice(half, 2 * half), bottom_up)):
        value = lax.dot_general(src, wk, nt, preferred_element_type=jnp.float32)
        back_ref[0, rows, :] = jnp.where(on, value, 0.0).astype(back_ref.dtype)
    term = lax.dot_general(top_in, top_up, tn, preferred_element_type=jnp.float32)
    term = term + lax.dot_general(bottom_in, bottom_up, tn, preferred_element_type=jnp.float32)
    term_ref[0] = jnp.where(on, term, 0.0).astype(term_ref.dtype)


def slot_products(stack_a, stack_b, weights, tables):
    slots, size, _ = weights.shape
    steps, half, width = stack_a.shape
    rows = 2 * half

    def block(step_ref, blk_ref):
        return pl.BlockSpec(
            (1, half, BLK), lambda k, *t: (t[step_ref][k], 0, t[blk_ref][k])
        )

    grid_spec = pltpu.PrefetchScalarGridSpec(
        num_scalar_prefetch=len(tables),
        grid=(slots,),
        in_specs=[
            block(0, 2),
            block(1, 2),
            block(3, 5),
            block(4, 5),
            pl.BlockSpec((1, size, size), lambda k, *t: (k, 0, 0)),
        ],
        out_specs=[
            pl.BlockSpec((1, rows, BLK), lambda k, *t: (k, 0, 0)),
            pl.BlockSpec((1, rows, BLK), lambda k, *t: (k, 0, 0)),
            pl.BlockSpec((1, size, size), lambda k, *t: (k, 0, 0)),
        ],
    )
    return pl.pallas_call(
        slot_kernel,
        grid_spec=grid_spec,
        out_shape=[
            jax.ShapeDtypeStruct((slots, rows, BLK), jnp.bfloat16),
            jax.ShapeDtypeStruct((slots, rows, BLK), jnp.bfloat16),
            jax.ShapeDtypeStruct((slots, size, size), jnp.bfloat16),
        ],
        cost_estimate=pl.CostEstimate(
            flops=6 * slots * rows * size * size,
            bytes_accessed=slots * (4 * rows * BLK + 2 * size * size) * 2,
            transcendentals=0,
        ),
    )(*tables, stack_a, stack_b, stack_a, stack_b, weights)


def outer_kernel(left, right, out):
    out[...] = lax.dot_general(
        left[...], right[...], (((0,), (0,)), ((), ())), preferred_element_type=jnp.float32
    ).astype(out.dtype)


def group_outer(left, right, tile_m=512, tile_n=1024):
    rows, m = left.shape
    n = right.shape[1]
    return pl.pallas_call(
        outer_kernel,
        grid=(m // tile_m, n // tile_n),
        in_specs=[
            pl.BlockSpec((rows, tile_m), lambda i, j: (0, i)),
            pl.BlockSpec((rows, tile_n), lambda i, j: (0, j)),
        ],
        out_specs=pl.BlockSpec((tile_m, tile_n), lambda i, j: (i, j)),
        out_shape=jax.ShapeDtypeStruct((m, n), jnp.bfloat16),
        cost_estimate=pl.CostEstimate(
            flops=2 * rows * m * n, bytes_accessed=2 * (rows * (m + n) + m * n), transcendentals=0
        ),
    )(left, right)


def reduce_kernel(side, part, bias, out, bias_out, send1, recv1, acc1, send2, recv2, sems1, sems2,
                  bsend1, brecv1, bacc1, bsend2, brecv2, bsems1, bsems2):
    core = lax.axis_index("tensor") % 2
    me = lax.axis_index("dp")
    column = lax.axis_index("tensor")
    hi, lo = me // side, me % side
    p1 = (1 - core) * hi + core * lo
    p2 = (1 - core) * lo + core * hi
    mesh_ids = pl.DeviceIdType.MESH
    half = part.shape[3] // 2
    halves = (pl.ds(0, half), pl.ds(half, half))

    def device(q1, q2):
        q1, q2 = q1 % side, q2 % side
        return (1 - core) * (q1 * side + q2) + core * (q2 * side + q1)

    ring1 = (device(p1 + 1, p2), device(p1 - 1, p2))
    ring2 = (device(p1, p2 + 1), device(p1, p2 - 1))
    barrier = pltpu.get_barrier_semaphore()
    for target in ring1 + ring2:
        pl.semaphore_signal(barrier, inc=1, device_id=(target, column), device_id_type=mesh_ids)
    pl.semaphore_wait(barrier, 4)

    def link(send, recv, sems, d, step, target):
        return pltpu.make_async_remote_copy(
            src_ref=send.at[d, step],
            dst_ref=recv.at[d, step],
            send_sem=sems.at[0, d, step],
            recv_sem=sems.at[1, d, step],
            device_id=(target, column),
            device_id_type=mesh_ids,
        )

    def own1(k, d):
        lead = part[k, :, :, halves[d]]
        cross = part[:, k, :, halves[d]]
        return jnp.where(core == 0, lead, cross).astype(jnp.float32)

    def own2(k, d):
        return acc1[k, :, halves[d]]

    def store1(total, d):
        acc1[:, :, halves[d]] = total

    def store2(total, d):
        out[:, halves[d]] = total

    def bias1(k, d):
        return bias[:, halves[d]]

    def bias2(k, d):
        return bacc1[:, halves[d]]

    def bstore1(total, d):
        bacc1[:, halves[d]] = total

    def bstore2(total, d):
        bias_out[:, halves[d]] = total

    stages = (
        (ring1, p1, ((send1, recv1, sems1, own1, store1), (bsend1, brecv1, bsems1, bias1, bstore1))),
        (ring2, p2, ((send2, recv2, sems2, own2, store2), (bsend2, brecv2, bsems2, bias2, bstore2))),
    )
    sends = []
    for ring, pos, channels in stages:
        for step in range(side - 1):
            for d, sign in ((0, 1), (1, -1)):
                k = (pos - sign * (1 + step)) % side
                for send, recv, sems, own, _ in channels:
                    value = own(k, d)
                    if step > 0:
                        link(send, recv, sems, d, step - 1, ring[d]).wait_recv()
                        value = value + recv[d, step - 1].astype(jnp.float32)
                    send[d, step] = value.astype(send.dtype)
                    copy = link(send, recv, sems, d, step, ring[d])
                    copy.start()
                    sends.append(copy)
        for d in range(2):
            for send, recv, sems, own, store in channels:
                link(send, recv, sems, d, side - 2, ring[d]).wait_recv()
                store(own(pos, d) + recv[d, side - 2].astype(jnp.float32), d)
    for copy in sends:
        copy.wait_send()


def reduce_rows(part, bias, side):
    chunk, width = part.shape[0] // (side * side), part.shape[1]
    part = part.reshape(side, side, chunk, width)
    rows = bias.shape[0]
    vmem = pl.BlockSpec(memory_space=pltpu.VMEM)
    return pl.pallas_call(
        functools.partial(reduce_kernel, side),
        out_shape=[
            jax.ShapeDtypeStruct((chunk, width), jnp.float32),
            jax.ShapeDtypeStruct((rows, width), jnp.float32),
        ],
        in_specs=[vmem, vmem],
        out_specs=[vmem, vmem],
        scratch_shapes=[
            pltpu.VMEM((2, side - 1, side, chunk, width // 2), jnp.bfloat16),
            pltpu.VMEM((2, side - 1, side, chunk, width // 2), jnp.bfloat16),
            pltpu.VMEM((side, chunk, width), jnp.float32),
            pltpu.VMEM((2, side - 1, chunk, width // 2), jnp.bfloat16),
            pltpu.VMEM((2, side - 1, chunk, width // 2), jnp.bfloat16),
            pltpu.SemaphoreType.DMA((2, 2, side - 1)),
            pltpu.SemaphoreType.DMA((2, 2, side - 1)),
            pltpu.VMEM((2, side - 1, rows, width // 2), jnp.float32),
            pltpu.VMEM((2, side - 1, rows, width // 2), jnp.float32),
            pltpu.VMEM((rows, width), jnp.float32),
            pltpu.VMEM((2, side - 1, rows, width // 2), jnp.float32),
            pltpu.VMEM((2, side - 1, rows, width // 2), jnp.float32),
            pltpu.SemaphoreType.DMA((2, 2, side - 1)),
            pltpu.SemaphoreType.DMA((2, 2, side - 1)),
        ],
        compiler_params=pltpu.CompilerParams(
            collective_id=2, has_side_effects=True, vmem_limit_bytes=60 * 1024 * 1024
        ),
    )(part, bias)

def on_device(
    dense,
    bottom_weight,
    bottom_bias,
    cross_blocks,
    cross_bias,
    cotangent,
    in_blocks,
    out_blocks,
    live_slots,
):
    groups = lax.axis_size("tensor")
    mine = lax.axis_index("tensor")
    row_count = dense.shape[0]
    local_width = bottom_weight.shape[1]
    per_device = local_width // BLK
    capacity = -(-SLOTS // groups)
    preact = jnp.dot(dense, bottom_weight, preferred_element_type=jnp.float32) + bottom_bias
    start = jax.nn.silu(preact).astype(jnp.bfloat16)
    start_wide = start.astype(jnp.float32)
    cot_wide = cotangent.astype(jnp.float32)
    grad_mixed = cot_wide * start_wide
    grad_mixed_low = grad_mixed.astype(jnp.bfloat16)
    alive = jnp.arange(SLOTS)[None, :] < live_slots[:, None]
    alive_mine = alive[mine]
    in_owner = in_blocks // per_device
    in_local = in_blocks % per_device
    out_owner = out_blocks // per_device
    out_local = out_blocks % per_device
    in_rank = slot_ranks(in_owner, alive)
    out_rank = slot_ranks(out_owner, alive)
    combo = jnp.concatenate([start, grad_mixed_low], axis=1)
    stack_a, stack_b = ring_gather(combo, "tensor", groups)
    step_a = lambda owner: (mine - owner) % groups
    step_b = lambda owner: (owner - mine) % groups
    tables = (
        step_a(in_owner[mine]),
        step_b(in_owner[mine]),
        in_local[mine],
        step_a(out_owner[mine]),
        step_b(out_owner[mine]),
        out_local[mine] + per_device,
        alive_mine.astype(jnp.int32),
    )
    weights = lax.all_gather(cross_blocks, "dp", axis=1, tiled=True)
    parts, back_parts, block_terms = slot_products(
        stack_a.reshape(groups, -1, 2 * local_width),
        stack_b.reshape(groups, -1, 2 * local_width),
        weights,
        tuple(t.astype(jnp.int32) for t in tables),
    )
    chosen_out, filled_out = post_table(
        out_owner[mine], out_rank[mine], alive_mine, groups, capacity
    )
    chosen_in, filled_in = post_table(in_owner[mine], in_rank[mine], alive_mine, groups, capacity)
    arrived_parts, arrived_back = exchange(
        pack_parts(parts, chosen_out, filled_out),
        pack_parts(back_parts, chosen_in, filled_in),
        groups,
    )
    mixed = (
        collect_parts(
            arrived_parts, out_owner, out_local, out_rank, alive, mine, capacity, per_device
        )
        + cross_bias
    )
    cross_out = (start_wide * mixed + start_wide).astype(jnp.bfloat16)
    grad_start = collect_parts(
        arrived_back, in_owner, in_local, in_rank, alive, mine, capacity, per_device
    )
    grad_blocks = lax.psum_scatter(block_terms, "dp", scatter_dimension=1, tiled=True).astype(
        jnp.float32
    )
    grad_start = grad_start + cot_wide * mixed + cot_wide
    sigma = jax.nn.sigmoid(preact)
    grad_pre = grad_start * sigma * (1.0 + preact * (1.0 - sigma))
    grad_pre_low = grad_pre.astype(jnp.bfloat16)
    taken = dense
    side = int(round(lax.axis_size("dp") ** 0.5))
    bias_rows = jnp.zeros((8, local_width), jnp.float32)
    bias_rows = bias_rows.at[0].set(jnp.sum(grad_pre, axis=0)).at[1].set(jnp.sum(grad_mixed, axis=0))
    grad_bottom, bias_sums = reduce_rows(group_outer(taken, grad_pre_low), bias_rows, side)
    grad_bias_bottom = bias_sums[0]
    grad_bias = bias_sums[1]
    return (cross_out, grad_bottom, grad_bias_bottom, grad_blocks, grad_bias)


def solution(mesh):
    return jax.shard_map(
        on_device,
        mesh=mesh,
        in_specs=(
            P("dp", None),
            P(None, "tensor"),
            P("tensor"),
            P("tensor", "dp", None),
            P("tensor"),
            P("dp", "tensor"),
            P(),
            P(),
            P(),
        ),
        out_specs=(
            P("dp", "tensor"),
            P("dp", "tensor"),
            P("tensor"),
            P("tensor", "dp", None),
            P("tensor"),
        ),
        check_vma=False,
    )
```

```python
import functools

import jax
import jax.numpy as jnp
from jax import lax
from jax.sharding import PartitionSpec as P
from jax.experimental import pallas as pl
from jax.experimental.pallas import tpu as pltpu

BLK = 512
SLOTS = 10
RING_CHUNKS = 6


def slot_ranks(owner, alive):
    order = jnp.arange(owner.shape[1])
    earlier = order[None, :] < order[:, None]
    same = (owner[:, :, None] == owner[:, None, :]) & alive[:, None, :] & earlier[None, :, :]
    return jnp.sum(same.astype(jnp.int32), axis=2)


def post_table(owner_mine, rank_mine, alive_mine, groups, capacity):
    slot_count = owner_mine.shape[0]
    match = (
        (owner_mine[None, None, :] == jnp.arange(groups)[:, None, None])
        & (rank_mine[None, None, :] == jnp.arange(capacity)[None, :, None])
        & alive_mine[None, None, :]
    )
    chosen = jnp.sum(match.astype(jnp.int32) * jnp.arange(slot_count)[None, None, :], axis=2)
    filled = jnp.any(match, axis=2)
    return (chosen, filled)


def pack_parts(parts, chosen, filled):
    picked = jnp.take(parts, chosen.reshape(-1), axis=0) * filled.reshape(-1)[:, None, None].astype(
        parts.dtype
    )
    return picked.reshape(chosen.shape[0], chosen.shape[1] * parts.shape[1], parts.shape[2])


def collect_parts(received, owner, local, rank, alive, target, capacity, per_device):
    groups, span_rows, block_width = received.shape
    row_count = span_rows // capacity
    match = ((owner == target) & alive)[:, :, None] & (
        rank[:, :, None] == jnp.arange(capacity)[None, None, :]
    )
    matches = match[:, :, :, None] & (
        local[:, :, None, None] == jnp.arange(per_device)[None, None, None, :]
    )
    onehot = (
        jnp.sum(matches.astype(jnp.int32), axis=1)
        .reshape(groups * capacity, per_device)
        .astype(jnp.bfloat16)
    )
    flattened = received.reshape(groups * capacity, row_count, block_width)
    summed = jnp.einsum("irb,il->rlb", flattened, onehot, preferred_element_type=jnp.float32)
    return summed.reshape(row_count, per_device * block_width)

def ring_kernel(n, top, bottom, out_a, out_b, own_sem, send_sem, recv_sem):
    me = lax.axis_index("tensor")
    row = lax.axis_index("dp")
    right = lax.rem(me + 1, n)
    left = lax.rem(me + n - 1, n)
    mesh_ids = pl.DeviceIdType.MESH
    barrier = pltpu.get_barrier_semaphore()
    for neighbour in (left, right):
        pl.semaphore_signal(barrier, inc=1, device_id=(row, neighbour), device_id_type=mesh_ids)
    pl.semaphore_wait(barrier, 2)
    own_a = pltpu.make_async_copy(top, out_a.at[0], own_sem.at[0])
    own_b = pltpu.make_async_copy(bottom, out_b.at[0], own_sem.at[1])
    own_a.start()
    own_b.start()

    chunks = send_sem.shape[2]
    rows = top.shape[0] // chunks

    def piece(ref, c):
        return ref.at[pl.ds(c * rows, rows)]

    def link(out, side, step, c, target, src=None):
        return pltpu.make_async_remote_copy(
            src_ref=piece(out.at[step] if src is None else src, c),
            dst_ref=piece(out.at[step], c),
            send_sem=send_sem.at[side, step, c],
            recv_sem=recv_sem.at[side, step, c],
            device_id=(row, target),
            device_id_type=mesh_ids,
        )

    sends = []
    for step in range(1, n):
        for c in range(chunks):
            if step == 1:
                src_a, src_b = top, bottom
            else:
                link(out_a, 0, step - 1, c, right).wait_recv()
                link(out_b, 1, step - 1, c, left).wait_recv()
                src_a, src_b = out_a.at[step - 1], out_b.at[step - 1]
            copy_a = link(out_a, 0, step, c, right, src_a)
            copy_b = link(out_b, 1, step, c, left, src_b)
            copy_a.start()
            copy_b.start()
            sends += [copy_a, copy_b]
    for c in range(chunks):
        link(out_a, 0, n - 1, c, right).wait_recv()
        link(out_b, 1, n - 1, c, left).wait_recv()
    for copy in sends:
        copy.wait_send()
    own_a.wait()
    own_b.wait()


def ring_gather(x, axis, n):
    half = x.shape[0] // 2
    shape = jax.ShapeDtypeStruct((n, half, x.shape[1]), x.dtype)
    anywhere = pl.BlockSpec(memory_space=pl.ANY)
    return pl.pallas_call(
        functools.partial(ring_kernel, n),
        out_shape=[shape, shape],
        in_specs=[anywhere, anywhere],
        out_specs=[anywhere, anywhere],
        scratch_shapes=[
            pltpu.SemaphoreType.DMA((2,)),
            pltpu.SemaphoreType.DMA((2, n, RING_CHUNKS)),
            pltpu.SemaphoreType.DMA((2, n, RING_CHUNKS)),
        ],
        compiler_params=pltpu.CompilerParams(collective_id=0, has_side_effects=True),
    )(x[:half], x[half:])


def exchange_kernel(n, first, second, out_first, out_second, own_sem, send_sem, recv_sem):
    me = lax.axis_index("tensor")
    row = lax.axis_index("dp")
    mesh_ids = pl.DeviceIdType.MESH
    barrier = pltpu.get_barrier_semaphore()
    for offset in range(1, n):
        peer = lax.rem(me + offset, n)
        pl.semaphore_signal(barrier, inc=1, device_id=(row, peer), device_id_type=mesh_ids)
    pl.semaphore_wait(barrier, n - 1)
    pairs = ((first, out_first), (second, out_second))
    own = [
        pltpu.make_async_copy(src.at[me], dst.at[me], own_sem.at[side])
        for side, (src, dst) in enumerate(pairs)
    ]
    for copy in own:
        copy.start()

    def link(side, peer, slot):
        src, dst = pairs[side]
        return pltpu.make_async_remote_copy(
            src_ref=src.at[peer],
            dst_ref=dst.at[slot],
            send_sem=send_sem.at[side, peer],
            recv_sem=recv_sem.at[side, slot],
            device_id=(row, peer),
            device_id_type=mesh_ids,
        )

    sends = []
    for offset in (1, n - 1, 2, n - 2, 3, n - 3, 4)[: n - 1]:
        peer = lax.rem(me + offset, n)
        for side in range(2):
            copy = link(side, peer, me)
            copy.start()
            sends.append(copy)
    for offset in range(1, n):
        source = lax.rem(me + offset, n)
        for side in range(2):
            link(side, source, source).wait_recv()
    for copy in sends:
        copy.wait_send()
    for copy in own:
        copy.wait()


def exchange(first, second, n):
    anywhere = pl.BlockSpec(memory_space=pl.ANY)
    return pl.pallas_call(
        functools.partial(exchange_kernel, n),
        out_shape=[
            jax.ShapeDtypeStruct(first.shape, first.dtype),
            jax.ShapeDtypeStruct(second.shape, second.dtype),
        ],
        in_specs=[anywhere, anywhere],
        out_specs=[anywhere, anywhere],
        scratch_shapes=[
            pltpu.SemaphoreType.DMA((2,)),
            pltpu.SemaphoreType.DMA((2, n)),
            pltpu.SemaphoreType.DMA((2, n)),
        ],
        compiler_params=pltpu.CompilerParams(collective_id=1, has_side_effects=True),
    )(first, second)


def take_blocks(stack_a, stack_b, owner, local, me, n):
    steps, half, width = stack_a.shape
    blocks_a = stack_a.reshape(steps, half, width // BLK, BLK)
    blocks_b = stack_b.reshape(steps, half, width // BLK, BLK)
    step_a = (me - owner) % n
    step_b = (owner - me) % n
    top = blocks_a[step_a, :, local, :]
    bottom = blocks_b[step_b, :, local, :]
    return jnp.concatenate([top, bottom], axis=1)


def slot_kernel(sa_i, sb_i, bi, sa_o, sb_o, bo, live, fa, fb, ua, ub, w, part_ref, back_ref, term_ref):
    k = pl.program_id(0)
    on = live[k] > 0
    half = fa.shape[1]
    wk = w[0]
    top_in, bottom_in = fa[0], fb[0]
    top_up, bottom_up = ua[0], ub[0]
    nt = (((1,), (1,)), ((), ()))
    tn = (((0,), (0,)), ((), ()))
    for rows, src in ((slice(0, half), top_in), (slice(half, 2 * half), bottom_in)):
        value = jnp.dot(src, wk, preferred_element_type=jnp.float32)
        part_ref[0, rows, :] = jnp.where(on, value, 0.0).astype(part_ref.dtype)
    for rows, src in ((slice(0, half), top_up), (slice(half, 2 * half), bottom_up)):
        value = lax.dot_general(src, wk, nt, preferred_element_type=jnp.float32)
        back_ref[0, rows, :] = jnp.where(on, value, 0.0).astype(back_ref.dtype)
    term = lax.dot_general(top_in, top_up, tn, preferred_element_type=jnp.float32)
    term = term + lax.dot_general(bottom_in, bottom_up, tn, preferred_element_type=jnp.float32)
    term_ref[0] = jnp.where(on, term, 0.0).astype(term_ref.dtype)


def slot_products(stack_a, stack_b, weights, tables):
    slots, size, _ = weights.shape
    steps, half, width = stack_a.shape
    rows = 2 * half

    def block(step_ref, blk_ref):
        return pl.BlockSpec(
            (1, half, BLK), lambda k, *t: (t[step_ref][k], 0, t[blk_ref][k])
        )

    grid_spec = pltpu.PrefetchScalarGridSpec(
        num_scalar_prefetch=len(tables),
        grid=(slots,),
        in_specs=[
            block(0, 2),
            block(1, 2),
            block(3, 5),
            block(4, 5),
            pl.BlockSpec((1, size, size), lambda k, *t: (k, 0, 0)),
        ],
        out_specs=[
            pl.BlockSpec((1, rows, BLK), lambda k, *t: (k, 0, 0)),
            pl.BlockSpec((1, rows, BLK), lambda k, *t: (k, 0, 0)),
            pl.BlockSpec((1, size, size), lambda k, *t: (k, 0, 0)),
        ],
    )
    return pl.pallas_call(
        slot_kernel,
        grid_spec=grid_spec,
        out_shape=[
            jax.ShapeDtypeStruct((slots, rows, BLK), jnp.bfloat16),
            jax.ShapeDtypeStruct((slots, rows, BLK), jnp.bfloat16),
            jax.ShapeDtypeStruct((slots, size, size), jnp.bfloat16),
        ],
        cost_estimate=pl.CostEstimate(
            flops=6 * slots * rows * size * size,
            bytes_accessed=slots * (4 * rows * BLK + 2 * size * size) * 2,
            transcendentals=0,
        ),
    )(*tables, stack_a, stack_b, stack_a, stack_b, weights)


def outer_kernel(left, right, out):
    out[...] = lax.dot_general(
        left[...], right[...], (((0,), (0,)), ((), ())), preferred_element_type=jnp.float32
    ).astype(out.dtype)


def group_outer(left, right, tile_m=512, tile_n=1024):
    rows, m = left.shape
    n = right.shape[1]
    return pl.pallas_call(
        outer_kernel,
        grid=(m // tile_m, n // tile_n),
        in_specs=[
            pl.BlockSpec((rows, tile_m), lambda i, j: (0, i)),
            pl.BlockSpec((rows, tile_n), lambda i, j: (0, j)),
        ],
        out_specs=pl.BlockSpec((tile_m, tile_n), lambda i, j: (i, j)),
        out_shape=jax.ShapeDtypeStruct((m, n), jnp.bfloat16),
        cost_estimate=pl.CostEstimate(
            flops=2 * rows * m * n, bytes_accessed=2 * (rows * (m + n) + m * n), transcendentals=0
        ),
    )(left, right)


def reduce_kernel(side, part, bias, out, bias_out, send1, recv1, acc1, send2, recv2, sems1, sems2,
                  bsend1, brecv1, bacc1, bsend2, brecv2, bsems1, bsems2):
    core = lax.axis_index("tensor") % 2
    me = lax.axis_index("dp")
    column = lax.axis_index("tensor")
    hi, lo = me // side, me % side
    p1 = (1 - core) * hi + core * lo
    p2 = (1 - core) * lo + core * hi
    mesh_ids = pl.DeviceIdType.MESH
    half = part.shape[3] // 2
    halves = (pl.ds(0, half), pl.ds(half, half))

    def device(q1, q2):
        q1, q2 = q1 % side, q2 % side
        return (1 - core) * (q1 * side + q2) + core * (q2 * side + q1)

    ring1 = (device(p1 + 1, p2), device(p1 - 1, p2))
    ring2 = (device(p1, p2 + 1), device(p1, p2 - 1))
    barrier = pltpu.get_barrier_semaphore()
    for target in ring1 + ring2:
        pl.semaphore_signal(barrier, inc=1, device_id=(target, column), device_id_type=mesh_ids)
    pl.semaphore_wait(barrier, 4)

    def link(send, recv, sems, d, step, target):
        return pltpu.make_async_remote_copy(
            src_ref=send.at[d, step],
            dst_ref=recv.at[d, step],
            send_sem=sems.at[0, d, step],
            recv_sem=sems.at[1, d, step],
            device_id=(target, column),
            device_id_type=mesh_ids,
        )

    def own1(k, d):
        lead = part[k, :, :, halves[d]]
        cross = part[:, k, :, halves[d]]
        return jnp.where(core == 0, lead, cross).astype(jnp.float32)

    def own2(k, d):
        return acc1[k, :, halves[d]]

    def store1(total, d):
        acc1[:, :, halves[d]] = total

    def store2(total, d):
        out[:, halves[d]] = total

    def bias1(k, d):
        return bias[:, halves[d]]

    def bias2(k, d):
        return bacc1[:, halves[d]]

    def bstore1(total, d):
        bacc1[:, halves[d]] = total

    def bstore2(total, d):
        bias_out[:, halves[d]] = total

    stages = (
        (ring1, p1, ((send1, recv1, sems1, own1, store1), (bsend1, brecv1, bsems1, bias1, bstore1))),
        (ring2, p2, ((send2, recv2, sems2, own2, store2), (bsend2, brecv2, bsems2, bias2, bstore2))),
    )
    sends = []
    for ring, pos, channels in stages:
        for step in range(side - 1):
            for d, sign in ((0, 1), (1, -1)):
                k = (pos - sign * (1 + step)) % side
                for send, recv, sems, own, _ in channels:
                    value = own(k, d)
                    if step > 0:
                        link(send, recv, sems, d, step - 1, ring[d]).wait_recv()
                        value = value + recv[d, step - 1].astype(jnp.float32)
                    send[d, step] = value.astype(send.dtype)
                    copy = link(send, recv, sems, d, step, ring[d])
                    copy.start()
                    sends.append(copy)
        for d in range(2):
            for send, recv, sems, own, store in channels:
                link(send, recv, sems, d, side - 2, ring[d]).wait_recv()
                store(own(pos, d) + recv[d, side - 2].astype(jnp.float32), d)
    for copy in sends:
        copy.wait_send()


def reduce_rows(part, bias, side):
    chunk, width = part.shape[0] // (side * side), part.shape[1]
    part = part.reshape(side, side, chunk, width)
    rows = bias.shape[0]
    vmem = pl.BlockSpec(memory_space=pltpu.VMEM)
    return pl.pallas_call(
        functools.partial(reduce_kernel, side),
        out_shape=[
            jax.ShapeDtypeStruct((chunk, width), jnp.float32),
            jax.ShapeDtypeStruct((rows, width), jnp.float32),
        ],
        in_specs=[vmem, vmem],
        out_specs=[vmem, vmem],
        scratch_shapes=[
            pltpu.VMEM((2, side - 1, side, chunk, width // 2), jnp.bfloat16),
            pltpu.VMEM((2, side - 1, side, chunk, width // 2), jnp.bfloat16),
            pltpu.VMEM((side, chunk, width), jnp.float32),
            pltpu.VMEM((2, side - 1, chunk, width // 2), jnp.bfloat16),
            pltpu.VMEM((2, side - 1, chunk, width // 2), jnp.bfloat16),
            pltpu.SemaphoreType.DMA((2, 2, side - 1)),
            pltpu.SemaphoreType.DMA((2, 2, side - 1)),
            pltpu.VMEM((2, side - 1, rows, width // 2), jnp.float32),
            pltpu.VMEM((2, side - 1, rows, width // 2), jnp.float32),
            pltpu.VMEM((rows, width), jnp.float32),
            pltpu.VMEM((2, side - 1, rows, width // 2), jnp.float32),
            pltpu.VMEM((2, side - 1, rows, width // 2), jnp.float32),
            pltpu.SemaphoreType.DMA((2, 2, side - 1)),
            pltpu.SemaphoreType.DMA((2, 2, side - 1)),
        ],
        compiler_params=pltpu.CompilerParams(
            collective_id=2, has_side_effects=True, vmem_limit_bytes=60 * 1024 * 1024
        ),
    )(part, bias)

def on_device(
    dense,
    bottom_weight,
    bottom_bias,
    cross_blocks,
    cross_bias,
    cotangent,
    in_blocks,
    out_blocks,
    live_slots,
):
    groups = lax.axis_size("tensor")
    mine = lax.axis_index("tensor")
    row_count = dense.shape[0]
    local_width = bottom_weight.shape[1]
    per_device = local_width // BLK
    capacity = -(-SLOTS // groups)
    preact = jnp.dot(dense, bottom_weight, preferred_element_type=jnp.float32) + bottom_bias
    start = jax.nn.silu(preact).astype(jnp.bfloat16)
    start_wide = start.astype(jnp.float32)
    cot_wide = cotangent.astype(jnp.float32)
    grad_mixed = cot_wide * start_wide
    grad_mixed_low = grad_mixed.astype(jnp.bfloat16)
    alive = jnp.arange(SLOTS)[None, :] < live_slots[:, None]
    alive_mine = alive[mine]
    in_owner = in_blocks // per_device
    in_local = in_blocks % per_device
    out_owner = out_blocks // per_device
    out_local = out_blocks % per_device
    in_rank = slot_ranks(in_owner, alive)
    out_rank = slot_ranks(out_owner, alive)
    combo = jnp.concatenate([start, grad_mixed_low], axis=1)
    stack_a, stack_b = ring_gather(combo, "tensor", groups)
    step_a = lambda owner: (mine - owner) % groups
    step_b = lambda owner: (owner - mine) % groups
    tables = (
        step_a(in_owner[mine]),
        step_b(in_owner[mine]),
        in_local[mine],
        step_a(out_owner[mine]),
        step_b(out_owner[mine]),
        out_local[mine] + per_device,
        alive_mine.astype(jnp.int32),
    )
    weights = lax.all_gather(cross_blocks, "dp", axis=1, tiled=True)
    parts, back_parts, block_terms = slot_products(
        stack_a.reshape(groups, -1, 2 * local_width),
        stack_b.reshape(groups, -1, 2 * local_width),
        weights,
        tuple(t.astype(jnp.int32) for t in tables),
    )
    chosen_out, filled_out = post_table(
        out_owner[mine], out_rank[mine], alive_mine, groups, capacity
    )
    chosen_in, filled_in = post_table(in_owner[mine], in_rank[mine], alive_mine, groups, capacity)
    arrived_parts, arrived_back = exchange(
        pack_parts(parts, chosen_out, filled_out),
        pack_parts(back_parts, chosen_in, filled_in),
        groups,
    )
    mixed = (
        collect_parts(
            arrived_parts, out_owner, out_local, out_rank, alive, mine, capacity, per_device
        )
        + cross_bias
    )
    cross_out = (start_wide * mixed + start_wide).astype(jnp.bfloat16)
    grad_start = collect_parts(
        arrived_back, in_owner, in_local, in_rank, alive, mine, capacity, per_device
    )
    grad_blocks = lax.psum_scatter(block_terms, "dp", scatter_dimension=1, tiled=True).astype(
        jnp.float32
    )
    grad_start = grad_start + cot_wide * mixed + cot_wide
    sigma = jax.nn.sigmoid(preact)
    grad_pre = grad_start * sigma * (1.0 + preact * (1.0 - sigma))
    grad_pre_low = grad_pre.astype(jnp.bfloat16)
    taken = dense
    side = int(round(lax.axis_size("dp") ** 0.5))
    bias_rows = jnp.zeros((8, local_width), jnp.float32)
    bias_rows = bias_rows.at[0].set(jnp.sum(grad_pre, axis=0)).at[1].set(jnp.sum(grad_mixed, axis=0))
    grad_bottom, bias_sums = reduce_rows(group_outer(taken, grad_pre_low), bias_rows, side)
    grad_bias_bottom = bias_sums[0]
    grad_bias = bias_sums[1]
    return (cross_out, grad_bottom, grad_bias_bottom, grad_blocks, grad_bias)


def solution(mesh):
    return jax.shard_map(
        on_device,
        mesh=mesh,
        in_specs=(
            P("dp", None),
            P(None, "tensor"),
            P("tensor"),
            P("tensor", "dp", None),
            P("tensor"),
            P("dp", "tensor"),
            P(),
            P(),
            P(),
        ),
        out_specs=(
            P("dp", "tensor"),
            P("dp", "tensor"),
            P("tensor"),
            P("tensor", "dp", None),
            P("tensor"),
        ),
        check_vma=False,
    )
```

```python
import functools

import jax
import jax.numpy as jnp
from jax import lax
from jax.sharding import PartitionSpec as P
from jax.experimental import pallas as pl
from jax.experimental.pallas import tpu as pltpu

BLK = 512
SLOTS = 10
RING_CHUNKS = 4


def slot_ranks(owner, alive):
    order = jnp.arange(owner.shape[1])
    earlier = order[None, :] < order[:, None]
    same = (owner[:, :, None] == owner[:, None, :]) & alive[:, None, :] & earlier[None, :, :]
    return jnp.sum(same.astype(jnp.int32), axis=2)


def post_table(owner_mine, rank_mine, alive_mine, groups, capacity):
    slot_count = owner_mine.shape[0]
    match = (
        (owner_mine[None, None, :] == jnp.arange(groups)[:, None, None])
        & (rank_mine[None, None, :] == jnp.arange(capacity)[None, :, None])
        & alive_mine[None, None, :]
    )
    chosen = jnp.sum(match.astype(jnp.int32) * jnp.arange(slot_count)[None, None, :], axis=2)
    filled = jnp.any(match, axis=2)
    return (chosen, filled)


def pack_parts(parts, chosen, filled):
    picked = jnp.take(parts, chosen.reshape(-1), axis=0)
    return picked.reshape(chosen.shape[0], chosen.shape[1] * parts.shape[1], parts.shape[2])


def collect_parts(received, owner, local, rank, alive, target, capacity, per_device):
    groups, span_rows, block_width = received.shape
    row_count = span_rows // capacity
    match = ((owner == target) & alive)[:, :, None] & (
        rank[:, :, None] == jnp.arange(capacity)[None, None, :]
    )
    matches = match[:, :, :, None] & (
        local[:, :, None, None] == jnp.arange(per_device)[None, None, None, :]
    )
    onehot = (
        jnp.sum(matches.astype(jnp.int32), axis=1)
        .reshape(groups * capacity, per_device)
        .astype(jnp.bfloat16)
    )
    flattened = received.reshape(groups * capacity, row_count, block_width)
    summed = jnp.einsum("irb,il->rlb", flattened, onehot, preferred_element_type=jnp.float32)
    return summed.reshape(row_count, per_device * block_width)

def ring_kernel(n, top, bottom, out_a, out_b, own_sem, send_sem, recv_sem):
    me = lax.axis_index("tensor")
    row = lax.axis_index("dp")
    right = lax.rem(me + 1, n)
    left = lax.rem(me + n - 1, n)
    mesh_ids = pl.DeviceIdType.MESH
    barrier = pltpu.get_barrier_semaphore()
    for neighbour in (left, right):
        pl.semaphore_signal(barrier, inc=1, device_id=(row, neighbour), device_id_type=mesh_ids)
    pl.semaphore_wait(barrier, 2)
    own_a = pltpu.make_async_copy(top, out_a.at[0], own_sem.at[0])
    own_b = pltpu.make_async_copy(bottom, out_b.at[0], own_sem.at[1])
    own_a.start()
    own_b.start()

    chunks = send_sem.shape[2]
    rows = top.shape[0] // chunks

    def piece(ref, c):
        return ref.at[pl.ds(c * rows, rows)]

    def link(out, side, step, c, target, src=None):
        return pltpu.make_async_remote_copy(
            src_ref=piece(out.at[step] if src is None else src, c),
            dst_ref=piece(out.at[step], c),
            send_sem=send_sem.at[side, step, c],
            recv_sem=recv_sem.at[side, step, c],
            device_id=(row, target),
            device_id_type=mesh_ids,
        )

    sends = []
    for step in range(1, n):
        for c in range(chunks):
            if step == 1:
                src_a, src_b = top, bottom
            else:
                link(out_a, 0, step - 1, c, right).wait_recv()
                link(out_b, 1, step - 1, c, left).wait_recv()
                src_a, src_b = out_a.at[step - 1], out_b.at[step - 1]
            copy_a = link(out_a, 0, step, c, right, src_a)
            copy_b = link(out_b, 1, step, c, left, src_b)
            copy_a.start()
            copy_b.start()
            sends += [copy_a, copy_b]
    for c in range(chunks):
        link(out_a, 0, n - 1, c, right).wait_recv()
        link(out_b, 1, n - 1, c, left).wait_recv()
    for copy in sends:
        copy.wait_send()
    own_a.wait()
    own_b.wait()


def ring_gather(x, axis, n):
    half = x.shape[0] // 2
    shape = jax.ShapeDtypeStruct((n, half, x.shape[1]), x.dtype)
    anywhere = pl.BlockSpec(memory_space=pl.ANY)
    return pl.pallas_call(
        functools.partial(ring_kernel, n),
        out_shape=[shape, shape],
        in_specs=[anywhere, anywhere],
        out_specs=[anywhere, anywhere],
        scratch_shapes=[
            pltpu.SemaphoreType.DMA((2,)),
            pltpu.SemaphoreType.DMA((2, n, RING_CHUNKS)),
            pltpu.SemaphoreType.DMA((2, n, RING_CHUNKS)),
        ],
        compiler_params=pltpu.CompilerParams(collective_id=0, has_side_effects=True),
    )(x[:half], x[half:])


def exchange_kernel(n, first, second, out_first, out_second, own_sem, send_sem, recv_sem):
    me = lax.axis_index("tensor")
    row = lax.axis_index("dp")
    mesh_ids = pl.DeviceIdType.MESH
    barrier = pltpu.get_barrier_semaphore()
    for offset in range(1, n):
        peer = lax.rem(me + offset, n)
        pl.semaphore_signal(barrier, inc=1, device_id=(row, peer), device_id_type=mesh_ids)
    pl.semaphore_wait(barrier, n - 1)
    pairs = ((first, out_first), (second, out_second))
    own = [
        pltpu.make_async_copy(src.at[me], dst.at[me], own_sem.at[side])
        for side, (src, dst) in enumerate(pairs)
    ]
    for copy in own:
        copy.start()

    def link(side, peer, slot):
        src, dst = pairs[side]
        return pltpu.make_async_remote_copy(
            src_ref=src.at[peer],
            dst_ref=dst.at[slot],
            send_sem=send_sem.at[side, peer],
            recv_sem=recv_sem.at[side, slot],
            device_id=(row, peer),
            device_id_type=mesh_ids,
        )

    sends = []
    for offset in (1, n - 1, 2, n - 2, 3, n - 3, 4)[: n - 1]:
        peer = lax.rem(me + offset, n)
        for side in range(2):
            copy = link(side, peer, me)
            copy.start()
            sends.append(copy)
    for offset in range(1, n):
        source = lax.rem(me + offset, n)
        for side in range(2):
            link(side, source, source).wait_recv()
    for copy in sends:
        copy.wait_send()
    for copy in own:
        copy.wait()


def exchange(first, second, n):
    anywhere = pl.BlockSpec(memory_space=pl.ANY)
    return pl.pallas_call(
        functools.partial(exchange_kernel, n),
        out_shape=[
            jax.ShapeDtypeStruct(first.shape, first.dtype),
            jax.ShapeDtypeStruct(second.shape, second.dtype),
        ],
        in_specs=[anywhere, anywhere],
        out_specs=[anywhere, anywhere],
        scratch_shapes=[
            pltpu.SemaphoreType.DMA((2,)),
            pltpu.SemaphoreType.DMA((2, n)),
            pltpu.SemaphoreType.DMA((2, n)),
        ],
        compiler_params=pltpu.CompilerParams(collective_id=1, has_side_effects=True),
    )(first, second)


def take_blocks(stack_a, stack_b, owner, local, me, n):
    steps, half, width = stack_a.shape
    blocks_a = stack_a.reshape(steps, half, width // BLK, BLK)
    blocks_b = stack_b.reshape(steps, half, width // BLK, BLK)
    step_a = (me - owner) % n
    step_b = (owner - me) % n
    top = blocks_a[step_a, :, local, :]
    bottom = blocks_b[step_b, :, local, :]
    return jnp.concatenate([top, bottom], axis=1)


def slot_kernel(sa_i, sb_i, bi, sa_o, sb_o, bo, live, fa, fb, ua, ub, w, part_ref, back_ref, term_ref):
    k = pl.program_id(0)
    on = live[k] > 0
    half = fa.shape[1]
    wk = w[0]
    top_in, bottom_in = fa[0], fb[0]
    top_up, bottom_up = ua[0], ub[0]
    nt = (((1,), (1,)), ((), ()))
    tn = (((0,), (0,)), ((), ()))
    for rows, src in ((slice(0, half), top_in), (slice(half, 2 * half), bottom_in)):
        value = jnp.dot(src, wk, preferred_element_type=jnp.float32)
        part_ref[0, rows, :] = jnp.where(on, value, 0.0).astype(part_ref.dtype)
    for rows, src in ((slice(0, half), top_up), (slice(half, 2 * half), bottom_up)):
        value = lax.dot_general(src, wk, nt, preferred_element_type=jnp.float32)
        back_ref[0, rows, :] = jnp.where(on, value, 0.0).astype(back_ref.dtype)
    term = lax.dot_general(top_in, top_up, tn, preferred_element_type=jnp.float32)
    term = term + lax.dot_general(bottom_in, bottom_up, tn, preferred_element_type=jnp.float32)
    term_ref[0] = jnp.where(on, term, 0.0).astype(term_ref.dtype)


def slot_products(stack_a, stack_b, weights, tables):
    slots, size, _ = weights.shape
    steps, half, width = stack_a.shape
    rows = 2 * half

    def block(step_ref, blk_ref):
        return pl.BlockSpec(
            (1, half, BLK), lambda k, *t: (t[step_ref][k], 0, t[blk_ref][k])
        )

    grid_spec = pltpu.PrefetchScalarGridSpec(
        num_scalar_prefetch=len(tables),
        grid=(slots,),
        in_specs=[
            block(0, 2),
            block(1, 2),
            block(3, 5),
            block(4, 5),
            pl.BlockSpec((1, size, size), lambda k, *t: (k, 0, 0)),
        ],
        out_specs=[
            pl.BlockSpec((1, rows, BLK), lambda k, *t: (k, 0, 0)),
            pl.BlockSpec((1, rows, BLK), lambda k, *t: (k, 0, 0)),
            pl.BlockSpec((1, size, size), lambda k, *t: (k, 0, 0)),
        ],
    )
    return pl.pallas_call(
        slot_kernel,
        grid_spec=grid_spec,
        out_shape=[
            jax.ShapeDtypeStruct((slots, rows, BLK), jnp.bfloat16),
            jax.ShapeDtypeStruct((slots, rows, BLK), jnp.bfloat16),
            jax.ShapeDtypeStruct((slots, size, size), jnp.bfloat16),
        ],
        cost_estimate=pl.CostEstimate(
            flops=6 * slots * rows * size * size,
            bytes_accessed=slots * (4 * rows * BLK + 2 * size * size) * 2,
            transcendentals=0,
        ),
    )(*tables, stack_a, stack_b, stack_a, stack_b, weights)


def outer_kernel(left, right, out):
    out[...] = lax.dot_general(
        left[...], right[...], (((0,), (0,)), ((), ())), preferred_element_type=jnp.float32
    ).astype(out.dtype)


def group_outer(left, right, tile_m=512, tile_n=1024):
    rows, m = left.shape
    n = right.shape[1]
    return pl.pallas_call(
        outer_kernel,
        grid=(m // tile_m, n // tile_n),
        in_specs=[
            pl.BlockSpec((rows, tile_m), lambda i, j: (0, i)),
            pl.BlockSpec((rows, tile_n), lambda i, j: (0, j)),
        ],
        out_specs=pl.BlockSpec((tile_m, tile_n), lambda i, j: (i, j)),
        out_shape=jax.ShapeDtypeStruct((m, n), jnp.bfloat16),
        cost_estimate=pl.CostEstimate(
            flops=2 * rows * m * n, bytes_accessed=2 * (rows * (m + n) + m * n), transcendentals=0
        ),
    )(left, right)


def reduce_kernel(side, part, bias, out, bias_out, send1, recv1, acc1, send2, recv2, sems1, sems2,
                  bsend1, brecv1, bacc1, bsend2, brecv2, bsems1, bsems2):
    core = lax.axis_index("tensor") % 2
    me = lax.axis_index("dp")
    column = lax.axis_index("tensor")
    hi, lo = me // side, me % side
    p1 = (1 - core) * hi + core * lo
    p2 = (1 - core) * lo + core * hi
    mesh_ids = pl.DeviceIdType.MESH
    half = part.shape[3] // 2
    halves = (pl.ds(0, half), pl.ds(half, half))

    def device(q1, q2):
        q1, q2 = q1 % side, q2 % side
        return (1 - core) * (q1 * side + q2) + core * (q2 * side + q1)

    ring1 = (device(p1 + 1, p2), device(p1 - 1, p2))
    ring2 = (device(p1, p2 + 1), device(p1, p2 - 1))
    barrier = pltpu.get_barrier_semaphore()
    for target in ring1 + ring2:
        pl.semaphore_signal(barrier, inc=1, device_id=(target, column), device_id_type=mesh_ids)
    pl.semaphore_wait(barrier, 4)

    def link(send, recv, sems, d, step, target):
        return pltpu.make_async_remote_copy(
            src_ref=send.at[d, step],
            dst_ref=recv.at[d, step],
            send_sem=sems.at[0, d, step],
            recv_sem=sems.at[1, d, step],
            device_id=(target, column),
            device_id_type=mesh_ids,
        )

    def own1(k, d):
        lead = part[k, :, :, halves[d]]
        cross = part[:, k, :, halves[d]]
        return jnp.where(core == 0, lead, cross).astype(jnp.float32)

    def own2(k, d):
        return acc1[k, :, halves[d]]

    def store1(total, d):
        acc1[:, :, halves[d]] = total

    def store2(total, d):
        out[:, halves[d]] = total

    def bias1(k, d):
        return bias[:, halves[d]]

    def bias2(k, d):
        return bacc1[:, halves[d]]

    def bstore1(total, d):
        bacc1[:, halves[d]] = total

    def bstore2(total, d):
        bias_out[:, halves[d]] = total

    stages = (
        (ring1, p1, ((send1, recv1, sems1, own1, store1), (bsend1, brecv1, bsems1, bias1, bstore1))),
        (ring2, p2, ((send2, recv2, sems2, own2, store2), (bsend2, brecv2, bsems2, bias2, bstore2))),
    )
    sends = []
    for ring, pos, channels in stages:
        for step in range(side - 1):
            for d, sign in ((0, 1), (1, -1)):
                k = (pos - sign * (1 + step)) % side
                for send, recv, sems, own, _ in channels:
                    value = own(k, d)
                    if step > 0:
                        link(send, recv, sems, d, step - 1, ring[d]).wait_recv()
                        value = value + recv[d, step - 1].astype(jnp.float32)
                    send[d, step] = value.astype(send.dtype)
                    copy = link(send, recv, sems, d, step, ring[d])
                    copy.start()
                    sends.append(copy)
        for d in range(2):
            for send, recv, sems, own, store in channels:
                link(send, recv, sems, d, side - 2, ring[d]).wait_recv()
                store(own(pos, d) + recv[d, side - 2].astype(jnp.float32), d)
    for copy in sends:
        copy.wait_send()


def reduce_rows(part, bias, side):
    chunk, width = part.shape[0] // (side * side), part.shape[1]
    part = part.reshape(side, side, chunk, width)
    rows = bias.shape[0]
    vmem = pl.BlockSpec(memory_space=pltpu.VMEM)
    return pl.pallas_call(
        functools.partial(reduce_kernel, side),
        out_shape=[
            jax.ShapeDtypeStruct((chunk, width), jnp.float32),
            jax.ShapeDtypeStruct((rows, width), jnp.float32),
        ],
        in_specs=[vmem, vmem],
        out_specs=[vmem, vmem],
        scratch_shapes=[
            pltpu.VMEM((2, side - 1, side, chunk, width // 2), jnp.bfloat16),
            pltpu.VMEM((2, side - 1, side, chunk, width // 2), jnp.bfloat16),
            pltpu.VMEM((side, chunk, width), jnp.float32),
            pltpu.VMEM((2, side - 1, chunk, width // 2), jnp.bfloat16),
            pltpu.VMEM((2, side - 1, chunk, width // 2), jnp.bfloat16),
            pltpu.SemaphoreType.DMA((2, 2, side - 1)),
            pltpu.SemaphoreType.DMA((2, 2, side - 1)),
            pltpu.VMEM((2, side - 1, rows, width // 2), jnp.float32),
            pltpu.VMEM((2, side - 1, rows, width // 2), jnp.float32),
            pltpu.VMEM((rows, width), jnp.float32),
            pltpu.VMEM((2, side - 1, rows, width // 2), jnp.float32),
            pltpu.VMEM((2, side - 1, rows, width // 2), jnp.float32),
            pltpu.SemaphoreType.DMA((2, 2, side - 1)),
            pltpu.SemaphoreType.DMA((2, 2, side - 1)),
        ],
        compiler_params=pltpu.CompilerParams(
            collective_id=2, has_side_effects=True, vmem_limit_bytes=60 * 1024 * 1024
        ),
    )(part, bias)

def on_device(
    dense,
    bottom_weight,
    bottom_bias,
    cross_blocks,
    cross_bias,
    cotangent,
    in_blocks,
    out_blocks,
    live_slots,
):
    groups = lax.axis_size("tensor")
    mine = lax.axis_index("tensor")
    row_count = dense.shape[0]
    local_width = bottom_weight.shape[1]
    per_device = local_width // BLK
    capacity = -(-SLOTS // groups)
    preact = jnp.dot(dense, bottom_weight, preferred_element_type=jnp.float32) + bottom_bias
    start = jax.nn.silu(preact).astype(jnp.bfloat16)
    start_wide = start.astype(jnp.float32)
    cot_wide = cotangent.astype(jnp.float32)
    grad_mixed = cot_wide * start_wide
    grad_mixed_low = grad_mixed.astype(jnp.bfloat16)
    alive = jnp.arange(SLOTS)[None, :] < live_slots[:, None]
    alive_mine = alive[mine]
    in_owner = in_blocks // per_device
    in_local = in_blocks % per_device
    out_owner = out_blocks // per_device
    out_local = out_blocks % per_device
    in_rank = slot_ranks(in_owner, alive)
    out_rank = slot_ranks(out_owner, alive)
    combo = jnp.concatenate([start, grad_mixed_low], axis=1)
    stack_a, stack_b = ring_gather(combo, "tensor", groups)
    step_a = lambda owner: (mine - owner) % groups
    step_b = lambda owner: (owner - mine) % groups
    tables = (
        step_a(in_owner[mine]),
        step_b(in_owner[mine]),
        in_local[mine],
        step_a(out_owner[mine]),
        step_b(out_owner[mine]),
        out_local[mine] + per_device,
        alive_mine.astype(jnp.int32),
    )
    weights = lax.all_gather(cross_blocks, "dp", axis=1, tiled=True)
    parts, back_parts, block_terms = slot_products(
        stack_a.reshape(groups, -1, 2 * local_width),
        stack_b.reshape(groups, -1, 2 * local_width),
        weights,
        tuple(t.astype(jnp.int32) for t in tables),
    )
    chosen_out, filled_out = post_table(
        out_owner[mine], out_rank[mine], alive_mine, groups, capacity
    )
    chosen_in, filled_in = post_table(in_owner[mine], in_rank[mine], alive_mine, groups, capacity)
    arrived_parts, arrived_back = exchange(
        pack_parts(parts, chosen_out, filled_out),
        pack_parts(back_parts, chosen_in, filled_in),
        groups,
    )
    mixed = (
        collect_parts(
            arrived_parts, out_owner, out_local, out_rank, alive, mine, capacity, per_device
        )
        + cross_bias
    )
    cross_out = (start_wide * mixed + start_wide).astype(jnp.bfloat16)
    grad_start = collect_parts(
        arrived_back, in_owner, in_local, in_rank, alive, mine, capacity, per_device
    )
    grad_blocks = lax.psum_scatter(block_terms, "dp", scatter_dimension=1, tiled=True).astype(
        jnp.float32
    )
    grad_start = grad_start + cot_wide * mixed + cot_wide
    sigma = jax.nn.sigmoid(preact)
    grad_pre = grad_start * sigma * (1.0 + preact * (1.0 - sigma))
    grad_pre_low = grad_pre.astype(jnp.bfloat16)
    taken = dense
    side = int(round(lax.axis_size("dp") ** 0.5))
    bias_rows = jnp.zeros((8, local_width), jnp.float32)
    bias_rows = bias_rows.at[0].set(jnp.sum(grad_pre, axis=0)).at[1].set(jnp.sum(grad_mixed, axis=0))
    grad_bottom, bias_sums = reduce_rows(group_outer(taken, grad_pre_low), bias_rows, side)
    grad_bias_bottom = bias_sums[0]
    grad_bias = bias_sums[1]
    return (cross_out, grad_bottom, grad_bias_bottom, grad_blocks, grad_bias)


def solution(mesh):
    return jax.shard_map(
        on_device,
        mesh=mesh,
        in_specs=(
            P("dp", None),
            P(None, "tensor"),
            P("tensor"),
            P("tensor", "dp", None),
            P("tensor"),
            P("dp", "tensor"),
            P(),
            P(),
            P(),
        ),
        out_specs=(
            P("dp", "tensor"),
            P("dp", "tensor"),
            P("tensor"),
            P("tensor", "dp", None),
            P("tensor"),
        ),
        check_vma=False,
    )
```

```python
import functools

import jax
import jax.numpy as jnp
from jax import lax
from jax.sharding import PartitionSpec as P
from jax.experimental import pallas as pl
from jax.experimental.pallas import tpu as pltpu

BLK = 512
SLOTS = 10
RING_CHUNKS = 4


def slot_ranks(owner, alive):
    order = jnp.arange(owner.shape[1])
    earlier = order[None, :] < order[:, None]
    same = (owner[:, :, None] == owner[:, None, :]) & alive[:, None, :] & earlier[None, :, :]
    return jnp.sum(same.astype(jnp.int32), axis=2)


def post_table(owner_mine, rank_mine, alive_mine, groups, capacity):
    slot_count = owner_mine.shape[0]
    match = (
        (owner_mine[None, None, :] == jnp.arange(groups)[:, None, None])
        & (rank_mine[None, None, :] == jnp.arange(capacity)[None, :, None])
        & alive_mine[None, None, :]
    )
    chosen = jnp.sum(match.astype(jnp.int32) * jnp.arange(slot_count)[None, None, :], axis=2)
    filled = jnp.any(match, axis=2)
    return (chosen, filled)


def pack_parts(parts, chosen, filled):
    picked = jnp.take(parts, chosen.reshape(-1), axis=0)
    return picked.reshape(chosen.shape[0], chosen.shape[1] * parts.shape[1], parts.shape[2])


def collect_parts(received, owner, local, rank, alive, target, capacity, per_device):
    groups, span_rows, block_width = received.shape
    row_count = span_rows // capacity
    match = ((owner == target) & alive)[:, :, None] & (
        rank[:, :, None] == jnp.arange(capacity)[None, None, :]
    )
    matches = match[:, :, :, None] & (
        local[:, :, None, None] == jnp.arange(per_device)[None, None, None, :]
    )
    onehot = (
        jnp.sum(matches.astype(jnp.int32), axis=1)
        .reshape(groups * capacity, per_device)
        .astype(jnp.bfloat16)
    )
    flattened = received.reshape(groups * capacity, row_count, block_width)
    summed = jnp.einsum("irb,il->rlb", flattened, onehot, preferred_element_type=jnp.float32)
    return summed.reshape(row_count, per_device * block_width)

def ring_kernel(n, top, bottom, out_a, out_b, own_sem, send_sem, recv_sem):
    me = lax.axis_index("tensor")
    row = lax.axis_index("dp")
    right = lax.rem(me + 1, n)
    left = lax.rem(me + n - 1, n)
    mesh_ids = pl.DeviceIdType.MESH
    barrier = pltpu.get_barrier_semaphore()
    for neighbour in (left, right):
        pl.semaphore_signal(barrier, inc=1, device_id=(row, neighbour), device_id_type=mesh_ids)
    pl.semaphore_wait(barrier, 2)
    own_a = pltpu.make_async_copy(top, out_a.at[0], own_sem.at[0])
    own_b = pltpu.make_async_copy(bottom, out_b.at[0], own_sem.at[1])
    own_a.start()
    own_b.start()

    chunks = send_sem.shape[2]
    rows = top.shape[0] // chunks

    def piece(ref, c):
        return ref.at[pl.ds(c * rows, rows)]

    def link(out, side, step, c, target, src=None):
        return pltpu.make_async_remote_copy(
            src_ref=piece(out.at[step] if src is None else src, c),
            dst_ref=piece(out.at[step], c),
            send_sem=send_sem.at[side, step, c],
            recv_sem=recv_sem.at[side, step, c],
            device_id=(row, target),
            device_id_type=mesh_ids,
        )

    sends = []
    for step in range(1, n):
        for c in range(chunks):
            if step == 1:
                src_a, src_b = top, bottom
            else:
                link(out_a, 0, step - 1, c, right).wait_recv()
                link(out_b, 1, step - 1, c, left).wait_recv()
                src_a, src_b = out_a.at[step - 1], out_b.at[step - 1]
            copy_a = link(out_a, 0, step, c, right, src_a)
            copy_b = link(out_b, 1, step, c, left, src_b)
            copy_a.start()
            copy_b.start()
            sends += [copy_a, copy_b]
    for c in range(chunks):
        link(out_a, 0, n - 1, c, right).wait_recv()
        link(out_b, 1, n - 1, c, left).wait_recv()
    for copy in sends:
        copy.wait_send()
    own_a.wait()
    own_b.wait()


def ring_gather(x, axis, n):
    half = x.shape[0] // 2
    shape = jax.ShapeDtypeStruct((n, half, x.shape[1]), x.dtype)
    anywhere = pl.BlockSpec(memory_space=pl.ANY)
    return pl.pallas_call(
        functools.partial(ring_kernel, n),
        out_shape=[shape, shape],
        in_specs=[anywhere, anywhere],
        out_specs=[anywhere, anywhere],
        scratch_shapes=[
            pltpu.SemaphoreType.DMA((2,)),
            pltpu.SemaphoreType.DMA((2, n, RING_CHUNKS)),
            pltpu.SemaphoreType.DMA((2, n, RING_CHUNKS)),
        ],
        compiler_params=pltpu.CompilerParams(collective_id=0, has_side_effects=True),
    )(x[:half], x[half:])


def exchange_kernel(n, first, second, out_first, out_second, own_sem, send_sem, recv_sem):
    me = lax.axis_index("tensor")
    row = lax.axis_index("dp")
    mesh_ids = pl.DeviceIdType.MESH
    barrier = pltpu.get_barrier_semaphore()
    for offset in range(1, n):
        peer = lax.rem(me + offset, n)
        pl.semaphore_signal(barrier, inc=1, device_id=(row, peer), device_id_type=mesh_ids)
    pl.semaphore_wait(barrier, n - 1)
    pairs = ((first, out_first), (second, out_second))
    own = [
        pltpu.make_async_copy(src.at[me], dst.at[me], own_sem.at[side])
        for side, (src, dst) in enumerate(pairs)
    ]
    for copy in own:
        copy.start()

    def link(side, peer, slot):
        src, dst = pairs[side]
        return pltpu.make_async_remote_copy(
            src_ref=src.at[peer],
            dst_ref=dst.at[slot],
            send_sem=send_sem.at[side, peer],
            recv_sem=recv_sem.at[side, slot],
            device_id=(row, peer),
            device_id_type=mesh_ids,
        )

    sends = []
    for offset in (1, n - 1, 2, n - 2, 3, n - 3, 4)[: n - 1]:
        peer = lax.rem(me + offset, n)
        for side in range(2):
            copy = link(side, peer, me)
            copy.start()
            sends.append(copy)
    for offset in range(1, n):
        source = lax.rem(me + offset, n)
        for side in range(2):
            link(side, source, source).wait_recv()
    for copy in sends:
        copy.wait_send()
    for copy in own:
        copy.wait()


def exchange(first, second, n):
    anywhere = pl.BlockSpec(memory_space=pl.ANY)
    return pl.pallas_call(
        functools.partial(exchange_kernel, n),
        out_shape=[
            jax.ShapeDtypeStruct(first.shape, first.dtype),
            jax.ShapeDtypeStruct(second.shape, second.dtype),
        ],
        in_specs=[anywhere, anywhere],
        out_specs=[anywhere, anywhere],
        scratch_shapes=[
            pltpu.SemaphoreType.DMA((2,)),
            pltpu.SemaphoreType.DMA((2, n)),
            pltpu.SemaphoreType.DMA((2, n)),
        ],
        compiler_params=pltpu.CompilerParams(collective_id=1, has_side_effects=True),
    )(first, second)


def take_blocks(stack_a, stack_b, owner, local, me, n):
    steps, half, width = stack_a.shape
    blocks_a = stack_a.reshape(steps, half, width // BLK, BLK)
    blocks_b = stack_b.reshape(steps, half, width // BLK, BLK)
    step_a = (me - owner) % n
    step_b = (owner - me) % n
    top = blocks_a[step_a, :, local, :]
    bottom = blocks_b[step_b, :, local, :]
    return jnp.concatenate([top, bottom], axis=1)


def slot_kernel(sa_i, sb_i, bi, sa_o, sb_o, bo, live, fa, fb, ua, ub, w, part_ref, back_ref, term_ref):
    k = pl.program_id(0)
    on = live[k] > 0
    half = fa.shape[1]
    wk = w[0]
    top_in, bottom_in = fa[0], fb[0]
    top_up, bottom_up = ua[0], ub[0]
    nt = (((1,), (1,)), ((), ()))
    tn = (((0,), (0,)), ((), ()))
    for rows, src in ((slice(0, half), top_in), (slice(half, 2 * half), bottom_in)):
        value = jnp.dot(src, wk, preferred_element_type=jnp.float32)
        part_ref[0, rows, :] = jnp.where(on, value, 0.0).astype(part_ref.dtype)
    for rows, src in ((slice(0, half), top_up), (slice(half, 2 * half), bottom_up)):
        value = lax.dot_general(src, wk, nt, preferred_element_type=jnp.float32)
        back_ref[0, rows, :] = jnp.where(on, value, 0.0).astype(back_ref.dtype)
    term = lax.dot_general(top_in, top_up, tn, preferred_element_type=jnp.float32)
    term = term + lax.dot_general(bottom_in, bottom_up, tn, preferred_element_type=jnp.float32)
    term_ref[0] = jnp.where(on, term, 0.0).astype(term_ref.dtype)


def slot_products(stack_a, stack_b, weights, tables):
    slots, size, _ = weights.shape
    steps, half, width = stack_a.shape
    rows = 2 * half

    def block(step_ref, blk_ref):
        return pl.BlockSpec(
            (1, half, BLK), lambda k, *t: (t[step_ref][k], 0, t[blk_ref][k])
        )

    grid_spec = pltpu.PrefetchScalarGridSpec(
        num_scalar_prefetch=len(tables),
        grid=(slots,),
        in_specs=[
            block(0, 2),
            block(1, 2),
            block(3, 5),
            block(4, 5),
            pl.BlockSpec((1, size, size), lambda k, *t: (k, 0, 0)),
        ],
        out_specs=[
            pl.BlockSpec((1, rows, BLK), lambda k, *t: (k, 0, 0)),
            pl.BlockSpec((1, rows, BLK), lambda k, *t: (k, 0, 0)),
            pl.BlockSpec((1, size, size), lambda k, *t: (k, 0, 0)),
        ],
    )
    return pl.pallas_call(
        slot_kernel,
        grid_spec=grid_spec,
        out_shape=[
            jax.ShapeDtypeStruct((slots, rows, BLK), jnp.bfloat16),
            jax.ShapeDtypeStruct((slots, rows, BLK), jnp.bfloat16),
            jax.ShapeDtypeStruct((slots, size, size), jnp.bfloat16),
        ],
        cost_estimate=pl.CostEstimate(
            flops=6 * slots * rows * size * size,
            bytes_accessed=slots * (4 * rows * BLK + 2 * size * size) * 2,
            transcendentals=0,
        ),
    )(*tables, stack_a, stack_b, stack_a, stack_b, weights)


def outer_kernel(left, right, out):
    out[...] = lax.dot_general(
        left[...], right[...], (((0,), (0,)), ((), ())), preferred_element_type=jnp.float32
    ).astype(out.dtype)


def group_outer(left, right, tile_m=512, tile_n=1024):
    rows, m = left.shape
    n = right.shape[1]
    return pl.pallas_call(
        outer_kernel,
        grid=(m // tile_m, n // tile_n),
        in_specs=[
            pl.BlockSpec((rows, tile_m), lambda i, j: (0, i)),
            pl.BlockSpec((rows, tile_n), lambda i, j: (0, j)),
        ],
        out_specs=pl.BlockSpec((tile_m, tile_n), lambda i, j: (i, j)),
        out_shape=jax.ShapeDtypeStruct((m, n), jnp.bfloat16),
        cost_estimate=pl.CostEstimate(
            flops=2 * rows * m * n, bytes_accessed=2 * (rows * (m + n) + m * n), transcendentals=0
        ),
    )(left, right)


def reduce_kernel(side, part, bias, out, bias_out, send1, recv1, acc1, send2, recv2, sems1, sems2,
                  bsend1, brecv1, bacc1, bsend2, brecv2, bsems1, bsems2):
    core = lax.axis_index("tensor") % 2
    me = lax.axis_index("dp")
    column = lax.axis_index("tensor")
    hi, lo = me // side, me % side
    p1 = (1 - core) * hi + core * lo
    p2 = (1 - core) * lo + core * hi
    mesh_ids = pl.DeviceIdType.MESH
    half = part.shape[3] // 2
    halves = (pl.ds(0, half), pl.ds(half, half))

    def device(q1, q2):
        q1, q2 = q1 % side, q2 % side
        return (1 - core) * (q1 * side + q2) + core * (q2 * side + q1)

    ring1 = (device(p1 + 1, p2), device(p1 - 1, p2))
    ring2 = (device(p1, p2 + 1), device(p1, p2 - 1))
    barrier = pltpu.get_barrier_semaphore()
    for target in ring1 + ring2:
        pl.semaphore_signal(barrier, inc=1, device_id=(target, column), device_id_type=mesh_ids)
    pl.semaphore_wait(barrier, 4)

    def link(send, recv, sems, d, step, target):
        return pltpu.make_async_remote_copy(
            src_ref=send.at[d, step],
            dst_ref=recv.at[d, step],
            send_sem=sems.at[0, d, step],
            recv_sem=sems.at[1, d, step],
            device_id=(target, column),
            device_id_type=mesh_ids,
        )

    def own1(k, d):
        lead = part[k, :, :, halves[d]]
        cross = part[:, k, :, halves[d]]
        return jnp.where(core == 0, lead, cross).astype(jnp.float32)

    def own2(k, d):
        return acc1[k, :, halves[d]]

    def store1(total, d):
        acc1[:, :, halves[d]] = total

    def store2(total, d):
        out[:, halves[d]] = total

    def bias1(k, d):
        return bias[:, halves[d]]

    def bias2(k, d):
        return bacc1[:, halves[d]]

    def bstore1(total, d):
        bacc1[:, halves[d]] = total

    def bstore2(total, d):
        bias_out[:, halves[d]] = total

    stages = (
        (ring1, p1, ((send1, recv1, sems1, own1, store1), (bsend1, brecv1, bsems1, bias1, bstore1))),
        (ring2, p2, ((send2, recv2, sems2, own2, store2), (bsend2, brecv2, bsems2, bias2, bstore2))),
    )
    sends = []
    for ring, pos, channels in stages:
        for step in range(side - 1):
            for d, sign in ((0, 1), (1, -1)):
                k = (pos - sign * (1 + step)) % side
                for send, recv, sems, own, _ in channels:
                    value = own(k, d)
                    if step > 0:
                        link(send, recv, sems, d, step - 1, ring[d]).wait_recv()
                        value = value + recv[d, step - 1].astype(jnp.float32)
                    send[d, step] = value.astype(send.dtype)
                    copy = link(send, recv, sems, d, step, ring[d])
                    copy.start()
                    sends.append(copy)
        for d in range(2):
            for send, recv, sems, own, store in channels:
                link(send, recv, sems, d, side - 2, ring[d]).wait_recv()
                store(own(pos, d) + recv[d, side - 2].astype(jnp.float32), d)
    for copy in sends:
        copy.wait_send()


def reduce_rows(part, bias, side):
    chunk, width = part.shape[0] // (side * side), part.shape[1]
    part = part.reshape(side, side, chunk, width)
    rows = bias.shape[0]
    vmem = pl.BlockSpec(memory_space=pltpu.VMEM)
    return pl.pallas_call(
        functools.partial(reduce_kernel, side),
        out_shape=[
            jax.ShapeDtypeStruct((chunk, width), jnp.float32),
            jax.ShapeDtypeStruct((rows, width), jnp.float32),
        ],
        in_specs=[vmem, vmem],
        out_specs=[vmem, vmem],
        scratch_shapes=[
            pltpu.VMEM((2, side - 1, side, chunk, width // 2), jnp.bfloat16),
            pltpu.VMEM((2, side - 1, side, chunk, width // 2), jnp.bfloat16),
            pltpu.VMEM((side, chunk, width), jnp.float32),
            pltpu.VMEM((2, side - 1, chunk, width // 2), jnp.bfloat16),
            pltpu.VMEM((2, side - 1, chunk, width // 2), jnp.bfloat16),
            pltpu.SemaphoreType.DMA((2, 2, side - 1)),
            pltpu.SemaphoreType.DMA((2, 2, side - 1)),
            pltpu.VMEM((2, side - 1, rows, width // 2), jnp.float32),
            pltpu.VMEM((2, side - 1, rows, width // 2), jnp.float32),
            pltpu.VMEM((rows, width), jnp.float32),
            pltpu.VMEM((2, side - 1, rows, width // 2), jnp.float32),
            pltpu.VMEM((2, side - 1, rows, width // 2), jnp.float32),
            pltpu.SemaphoreType.DMA((2, 2, side - 1)),
            pltpu.SemaphoreType.DMA((2, 2, side - 1)),
        ],
        compiler_params=pltpu.CompilerParams(
            collective_id=2, has_side_effects=True, vmem_limit_bytes=60 * 1024 * 1024
        ),
    )(part, bias)

def on_device(
    dense,
    bottom_weight,
    bottom_bias,
    cross_blocks,
    cross_bias,
    cotangent,
    in_blocks,
    out_blocks,
    live_slots,
):
    groups = lax.axis_size("tensor")
    mine = lax.axis_index("tensor")
    row_count = dense.shape[0]
    local_width = bottom_weight.shape[1]
    per_device = local_width // BLK
    capacity = -(-SLOTS // groups)
    preact = jnp.dot(dense, bottom_weight, preferred_element_type=jnp.float32) + bottom_bias
    start = jax.nn.silu(preact).astype(jnp.bfloat16)
    start_wide = start.astype(jnp.float32)
    cot_wide = cotangent.astype(jnp.float32)
    grad_mixed = cot_wide * start_wide
    grad_mixed_low = grad_mixed.astype(jnp.bfloat16)
    alive = jnp.arange(SLOTS)[None, :] < live_slots[:, None]
    alive_mine = alive[mine]
    in_owner = in_blocks // per_device
    in_local = in_blocks % per_device
    out_owner = out_blocks // per_device
    out_local = out_blocks % per_device
    in_rank = slot_ranks(in_owner, alive)
    out_rank = slot_ranks(out_owner, alive)
    combo = jnp.concatenate([start, grad_mixed_low], axis=1)
    stack_a, stack_b = ring_gather(combo, "tensor", groups)
    step_a = lambda owner: (mine - owner) % groups
    step_b = lambda owner: (owner - mine) % groups
    tables = (
        step_a(in_owner[mine]),
        step_b(in_owner[mine]),
        in_local[mine],
        step_a(out_owner[mine]),
        step_b(out_owner[mine]),
        out_local[mine] + per_device,
        alive_mine.astype(jnp.int32),
    )
    weights = lax.all_gather(cross_blocks, "dp", axis=1, tiled=True)
    parts, back_parts, block_terms = slot_products(
        stack_a.reshape(groups, -1, 2 * local_width),
        stack_b.reshape(groups, -1, 2 * local_width),
        weights,
        tuple(t.astype(jnp.int32) for t in tables),
    )
    chosen_out, filled_out = post_table(
        out_owner[mine], out_rank[mine], alive_mine, groups, capacity
    )
    chosen_in, filled_in = post_table(in_owner[mine], in_rank[mine], alive_mine, groups, capacity)
    arrived_parts, arrived_back = exchange(
        pack_parts(parts, chosen_out, filled_out),
        pack_parts(back_parts, chosen_in, filled_in),
        groups,
    )
    mixed = (
        collect_parts(
            arrived_parts, out_owner, out_local, out_rank, alive, mine, capacity, per_device
        )
        + cross_bias
    )
    cross_out = (start_wide * mixed + start_wide).astype(jnp.bfloat16)
    grad_start = collect_parts(
        arrived_back, in_owner, in_local, in_rank, alive, mine, capacity, per_device
    )
    grad_blocks = lax.psum_scatter(
        block_terms.astype(jnp.float32), "dp", scatter_dimension=1, tiled=True
    )
    grad_start = grad_start + cot_wide * mixed + cot_wide
    sigma = jax.nn.sigmoid(preact)
    grad_pre = grad_start * sigma * (1.0 + preact * (1.0 - sigma))
    grad_pre_low = grad_pre.astype(jnp.bfloat16)
    taken = dense
    side = int(round(lax.axis_size("dp") ** 0.5))
    bias_rows = jnp.zeros((8, local_width), jnp.float32)
    bias_rows = bias_rows.at[0].set(jnp.sum(grad_pre, axis=0)).at[1].set(jnp.sum(grad_mixed, axis=0))
    grad_bottom, bias_sums = reduce_rows(group_outer(taken, grad_pre_low), bias_rows, side)
    grad_bias_bottom = bias_sums[0]
    grad_bias = bias_sums[1]
    return (cross_out, grad_bottom, grad_bias_bottom, grad_blocks, grad_bias)


def solution(mesh):
    return jax.shard_map(
        on_device,
        mesh=mesh,
        in_specs=(
            P("dp", None),
            P(None, "tensor"),
            P("tensor"),
            P("tensor", "dp", None),
            P("tensor"),
            P("dp", "tensor"),
            P(),
            P(),
            P(),
        ),
        out_specs=(
            P("dp", "tensor"),
            P("dp", "tensor"),
            P("tensor"),
            P("tensor", "dp", None),
            P("tensor"),
        ),
        check_vma=False,
    )
```

```python
import functools

import jax
import jax.numpy as jnp
from jax import lax
from jax.sharding import PartitionSpec as P
from jax.experimental import pallas as pl
from jax.experimental.pallas import tpu as pltpu

BLK = 512
SLOTS = 10
RING_CHUNKS = 4


def slot_ranks(owner, alive):
    order = jnp.arange(owner.shape[1])
    earlier = order[None, :] < order[:, None]
    same = (owner[:, :, None] == owner[:, None, :]) & alive[:, None, :] & earlier[None, :, :]
    return jnp.sum(same.astype(jnp.int32), axis=2)


def post_table(owner_mine, rank_mine, alive_mine, groups, capacity):
    slot_count = owner_mine.shape[0]
    match = (
        (owner_mine[None, None, :] == jnp.arange(groups)[:, None, None])
        & (rank_mine[None, None, :] == jnp.arange(capacity)[None, :, None])
        & alive_mine[None, None, :]
    )
    chosen = jnp.sum(match.astype(jnp.int32) * jnp.arange(slot_count)[None, None, :], axis=2)
    filled = jnp.any(match, axis=2)
    return (chosen, filled)


def pack_parts(parts, chosen, filled):
    picked = jnp.take(parts, chosen.reshape(-1), axis=0)
    return picked.reshape(chosen.shape[0], chosen.shape[1] * parts.shape[1], parts.shape[2])


def collect_parts(received, owner, local, rank, alive, target, capacity, per_device):
    groups, span_rows, block_width = received.shape
    row_count = span_rows // capacity
    match = ((owner == target) & alive)[:, :, None] & (
        rank[:, :, None] == jnp.arange(capacity)[None, None, :]
    )
    matches = match[:, :, :, None] & (
        local[:, :, None, None] == jnp.arange(per_device)[None, None, None, :]
    )
    onehot = (
        jnp.sum(matches.astype(jnp.int32), axis=1)
        .reshape(groups * capacity, per_device)
        .astype(jnp.bfloat16)
    )
    flattened = received.reshape(groups * capacity, row_count, block_width)
    summed = jnp.einsum("irb,il->rlb", flattened, onehot, preferred_element_type=jnp.float32)
    return summed.reshape(row_count, per_device * block_width)

def ring_kernel(n, top, bottom, out_a, out_b, own_sem, send_sem, recv_sem):
    me = lax.axis_index("tensor")
    row = lax.axis_index("dp")
    right = lax.rem(me + 1, n)
    left = lax.rem(me + n - 1, n)
    mesh_ids = pl.DeviceIdType.MESH
    barrier = pltpu.get_barrier_semaphore()
    for neighbour in (left, right):
        pl.semaphore_signal(barrier, inc=1, device_id=(row, neighbour), device_id_type=mesh_ids)
    pl.semaphore_wait(barrier, 2)
    own_a = pltpu.make_async_copy(top, out_a.at[0], own_sem.at[0])
    own_b = pltpu.make_async_copy(bottom, out_b.at[0], own_sem.at[1])
    own_a.start()
    own_b.start()

    chunks = send_sem.shape[2]
    rows = top.shape[0] // chunks

    def piece(ref, c):
        return ref.at[pl.ds(c * rows, rows)]

    def link(out, side, step, c, target, src=None):
        return pltpu.make_async_remote_copy(
            src_ref=piece(out.at[step] if src is None else src, c),
            dst_ref=piece(out.at[step], c),
            send_sem=send_sem.at[side, step, c],
            recv_sem=recv_sem.at[side, step, c],
            device_id=(row, target),
            device_id_type=mesh_ids,
        )

    sends = []
    for step in range(1, n):
        for c in range(chunks):
            if step == 1:
                src_a, src_b = top, bottom
            else:
                link(out_a, 0, step - 1, c, right).wait_recv()
                link(out_b, 1, step - 1, c, left).wait_recv()
                src_a, src_b = out_a.at[step - 1], out_b.at[step - 1]
            copy_a = link(out_a, 0, step, c, right, src_a)
            copy_b = link(out_b, 1, step, c, left, src_b)
            copy_a.start()
            copy_b.start()
            sends += [copy_a, copy_b]
    for c in range(chunks):
        link(out_a, 0, n - 1, c, right).wait_recv()
        link(out_b, 1, n - 1, c, left).wait_recv()
    for copy in sends:
        copy.wait_send()
    own_a.wait()
    own_b.wait()


def ring_gather(x, axis, n):
    half = x.shape[0] // 2
    shape = jax.ShapeDtypeStruct((n, half, x.shape[1]), x.dtype)
    anywhere = pl.BlockSpec(memory_space=pl.ANY)
    return pl.pallas_call(
        functools.partial(ring_kernel, n),
        out_shape=[shape, shape],
        in_specs=[anywhere, anywhere],
        out_specs=[anywhere, anywhere],
        scratch_shapes=[
            pltpu.SemaphoreType.DMA((2,)),
            pltpu.SemaphoreType.DMA((2, n, RING_CHUNKS)),
            pltpu.SemaphoreType.DMA((2, n, RING_CHUNKS)),
        ],
        compiler_params=pltpu.CompilerParams(collective_id=0, has_side_effects=True),
    )(x[:half], x[half:])


def exchange_kernel(n, first, second, out_first, out_second, own_sem, send_sem, recv_sem):
    me = lax.axis_index("tensor")
    row = lax.axis_index("dp")
    mesh_ids = pl.DeviceIdType.MESH
    barrier = pltpu.get_barrier_semaphore()
    for offset in range(1, n):
        peer = lax.rem(me + offset, n)
        pl.semaphore_signal(barrier, inc=1, device_id=(row, peer), device_id_type=mesh_ids)
    pl.semaphore_wait(barrier, n - 1)
    pairs = ((first, out_first), (second, out_second))
    own = [
        pltpu.make_async_copy(src.at[me], dst.at[me], own_sem.at[side])
        for side, (src, dst) in enumerate(pairs)
    ]
    for copy in own:
        copy.start()

    def link(side, peer, slot):
        src, dst = pairs[side]
        return pltpu.make_async_remote_copy(
            src_ref=src.at[peer],
            dst_ref=dst.at[slot],
            send_sem=send_sem.at[side, peer],
            recv_sem=recv_sem.at[side, slot],
            device_id=(row, peer),
            device_id_type=mesh_ids,
        )

    sends = []
    for offset in (1, n - 1, 2, n - 2, 3, n - 3, 4)[: n - 1]:
        peer = lax.rem(me + offset, n)
        for side in range(2):
            copy = link(side, peer, me)
            copy.start()
            sends.append(copy)
    for offset in range(1, n):
        source = lax.rem(me + offset, n)
        for side in range(2):
            link(side, source, source).wait_recv()
    for copy in sends:
        copy.wait_send()
    for copy in own:
        copy.wait()


def exchange(first, second, n):
    anywhere = pl.BlockSpec(memory_space=pl.ANY)
    return pl.pallas_call(
        functools.partial(exchange_kernel, n),
        out_shape=[
            jax.ShapeDtypeStruct(first.shape, first.dtype),
            jax.ShapeDtypeStruct(second.shape, second.dtype),
        ],
        in_specs=[anywhere, anywhere],
        out_specs=[anywhere, anywhere],
        scratch_shapes=[
            pltpu.SemaphoreType.DMA((2,)),
            pltpu.SemaphoreType.DMA((2, n)),
            pltpu.SemaphoreType.DMA((2, n)),
        ],
        compiler_params=pltpu.CompilerParams(collective_id=1, has_side_effects=True),
    )(first, second)


def take_blocks(stack_a, stack_b, owner, local, me, n):
    steps, half, width = stack_a.shape
    blocks_a = stack_a.reshape(steps, half, width // BLK, BLK)
    blocks_b = stack_b.reshape(steps, half, width // BLK, BLK)
    step_a = (me - owner) % n
    step_b = (owner - me) % n
    top = blocks_a[step_a, :, local, :]
    bottom = blocks_b[step_b, :, local, :]
    return jnp.concatenate([top, bottom], axis=1)


def slot_kernel(sa_i, sb_i, bi, sa_o, sb_o, bo, live, fa, fb, ua, ub, w, part_ref, back_ref, term_ref):
    k = pl.program_id(0)
    on = live[k] > 0
    half = fa.shape[1]
    wk = w[0]
    top_in, bottom_in = fa[0], fb[0]
    top_up, bottom_up = ua[0], ub[0]
    nt = (((1,), (1,)), ((), ()))
    tn = (((0,), (0,)), ((), ()))
    for rows, src in ((slice(0, half), top_in), (slice(half, 2 * half), bottom_in)):
        value = jnp.dot(src, wk, preferred_element_type=jnp.float32)
        part_ref[0, rows, :] = jnp.where(on, value, 0.0).astype(part_ref.dtype)
    for rows, src in ((slice(0, half), top_up), (slice(half, 2 * half), bottom_up)):
        value = lax.dot_general(src, wk, nt, preferred_element_type=jnp.float32)
        back_ref[0, rows, :] = jnp.where(on, value, 0.0).astype(back_ref.dtype)
    term = lax.dot_general(top_in, top_up, tn, preferred_element_type=jnp.float32)
    term = term + lax.dot_general(bottom_in, bottom_up, tn, preferred_element_type=jnp.float32)
    term_ref[0] = jnp.where(on, term, 0.0).astype(term_ref.dtype)


def slot_products(stack_a, stack_b, weights, tables):
    slots, size, _ = weights.shape
    steps, half, width = stack_a.shape
    rows = 2 * half

    def block(step_ref, blk_ref):
        return pl.BlockSpec(
            (1, half, BLK), lambda k, *t: (t[step_ref][k], 0, t[blk_ref][k])
        )

    grid_spec = pltpu.PrefetchScalarGridSpec(
        num_scalar_prefetch=len(tables),
        grid=(slots,),
        in_specs=[
            block(0, 2),
            block(1, 2),
            block(3, 5),
            block(4, 5),
            pl.BlockSpec((1, size, size), lambda k, *t: (k, 0, 0)),
        ],
        out_specs=[
            pl.BlockSpec((1, rows, BLK), lambda k, *t: (k, 0, 0)),
            pl.BlockSpec((1, rows, BLK), lambda k, *t: (k, 0, 0)),
            pl.BlockSpec((1, size, size), lambda k, *t: (k, 0, 0)),
        ],
    )
    return pl.pallas_call(
        slot_kernel,
        grid_spec=grid_spec,
        out_shape=[
            jax.ShapeDtypeStruct((slots, rows, BLK), jnp.bfloat16),
            jax.ShapeDtypeStruct((slots, rows, BLK), jnp.bfloat16),
            jax.ShapeDtypeStruct((slots, size, size), jnp.bfloat16),
        ],
        cost_estimate=pl.CostEstimate(
            flops=6 * slots * rows * size * size,
            bytes_accessed=slots * (4 * rows * BLK + 2 * size * size) * 2,
            transcendentals=0,
        ),
    )(*tables, stack_a, stack_b, stack_a, stack_b, weights)


def outer_kernel(left, right, out):
    out[...] = lax.dot_general(
        left[...], right[...], (((0,), (0,)), ((), ())), preferred_element_type=jnp.float32
    ).astype(out.dtype)


def group_outer(left, right, tile_m=512, tile_n=2048):
    rows, m = left.shape
    n = right.shape[1]
    return pl.pallas_call(
        outer_kernel,
        grid=(m // tile_m, n // tile_n),
        in_specs=[
            pl.BlockSpec((rows, tile_m), lambda i, j: (0, i)),
            pl.BlockSpec((rows, tile_n), lambda i, j: (0, j)),
        ],
        out_specs=pl.BlockSpec((tile_m, tile_n), lambda i, j: (i, j)),
        out_shape=jax.ShapeDtypeStruct((m, n), jnp.bfloat16),
        cost_estimate=pl.CostEstimate(
            flops=2 * rows * m * n, bytes_accessed=2 * (rows * (m + n) + m * n), transcendentals=0
        ),
    )(left, right)


def reduce_kernel(side, part, bias, out, bias_out, send1, recv1, acc1, send2, recv2, sems1, sems2,
                  bsend1, brecv1, bacc1, bsend2, brecv2, bsems1, bsems2):
    core = lax.axis_index("tensor") % 2
    me = lax.axis_index("dp")
    column = lax.axis_index("tensor")
    hi, lo = me // side, me % side
    p1 = (1 - core) * hi + core * lo
    p2 = (1 - core) * lo + core * hi
    mesh_ids = pl.DeviceIdType.MESH
    half = part.shape[3] // 2
    halves = (pl.ds(0, half), pl.ds(half, half))

    def device(q1, q2):
        q1, q2 = q1 % side, q2 % side
        return (1 - core) * (q1 * side + q2) + core * (q2 * side + q1)

    ring1 = (device(p1 + 1, p2), device(p1 - 1, p2))
    ring2 = (device(p1, p2 + 1), device(p1, p2 - 1))
    barrier = pltpu.get_barrier_semaphore()
    for target in ring1 + ring2:
        pl.semaphore_signal(barrier, inc=1, device_id=(target, column), device_id_type=mesh_ids)
    pl.semaphore_wait(barrier, 4)

    def link(send, recv, sems, d, step, target):
        return pltpu.make_async_remote_copy(
            src_ref=send.at[d, step],
            dst_ref=recv.at[d, step],
            send_sem=sems.at[0, d, step],
            recv_sem=sems.at[1, d, step],
            device_id=(target, column),
            device_id_type=mesh_ids,
        )

    def own1(k, d):
        lead = part[k, :, :, halves[d]]
        cross = part[:, k, :, halves[d]]
        return jnp.where(core == 0, lead, cross).astype(jnp.float32)

    def own2(k, d):
        return acc1[k, :, halves[d]]

    def store1(total, d):
        acc1[:, :, halves[d]] = total

    def store2(total, d):
        out[:, halves[d]] = total

    def bias1(k, d):
        return bias[:, halves[d]]

    def bias2(k, d):
        return bacc1[:, halves[d]]

    def bstore1(total, d):
        bacc1[:, halves[d]] = total

    def bstore2(total, d):
        bias_out[:, halves[d]] = total

    stages = (
        (ring1, p1, ((send1, recv1, sems1, own1, store1), (bsend1, brecv1, bsems1, bias1, bstore1))),
        (ring2, p2, ((send2, recv2, sems2, own2, store2), (bsend2, brecv2, bsems2, bias2, bstore2))),
    )
    sends = []
    for ring, pos, channels in stages:
        for step in range(side - 1):
            for d, sign in ((0, 1), (1, -1)):
                k = (pos - sign * (1 + step)) % side
                for send, recv, sems, own, _ in channels:
                    value = own(k, d)
                    if step > 0:
                        link(send, recv, sems, d, step - 1, ring[d]).wait_recv()
                        value = value + recv[d, step - 1].astype(jnp.float32)
                    send[d, step] = value.astype(send.dtype)
                    copy = link(send, recv, sems, d, step, ring[d])
                    copy.start()
                    sends.append(copy)
        for d in range(2):
            for send, recv, sems, own, store in channels:
                link(send, recv, sems, d, side - 2, ring[d]).wait_recv()
                store(own(pos, d) + recv[d, side - 2].astype(jnp.float32), d)
    for copy in sends:
        copy.wait_send()


def reduce_rows(part, bias, side):
    chunk, width = part.shape[0] // (side * side), part.shape[1]
    part = part.reshape(side, side, chunk, width)
    rows = bias.shape[0]
    vmem = pl.BlockSpec(memory_space=pltpu.VMEM)
    return pl.pallas_call(
        functools.partial(reduce_kernel, side),
        out_shape=[
            jax.ShapeDtypeStruct((chunk, width), jnp.float32),
            jax.ShapeDtypeStruct((rows, width), jnp.float32),
        ],
        in_specs=[vmem, vmem],
        out_specs=[vmem, vmem],
        scratch_shapes=[
            pltpu.VMEM((2, side - 1, side, chunk, width // 2), jnp.bfloat16),
            pltpu.VMEM((2, side - 1, side, chunk, width // 2), jnp.bfloat16),
            pltpu.VMEM((side, chunk, width), jnp.float32),
            pltpu.VMEM((2, side - 1, chunk, width // 2), jnp.bfloat16),
            pltpu.VMEM((2, side - 1, chunk, width // 2), jnp.bfloat16),
            pltpu.SemaphoreType.DMA((2, 2, side - 1)),
            pltpu.SemaphoreType.DMA((2, 2, side - 1)),
            pltpu.VMEM((2, side - 1, rows, width // 2), jnp.float32),
            pltpu.VMEM((2, side - 1, rows, width // 2), jnp.float32),
            pltpu.VMEM((rows, width), jnp.float32),
            pltpu.VMEM((2, side - 1, rows, width // 2), jnp.float32),
            pltpu.VMEM((2, side - 1, rows, width // 2), jnp.float32),
            pltpu.SemaphoreType.DMA((2, 2, side - 1)),
            pltpu.SemaphoreType.DMA((2, 2, side - 1)),
        ],
        compiler_params=pltpu.CompilerParams(
            collective_id=2, has_side_effects=True, vmem_limit_bytes=60 * 1024 * 1024
        ),
    )(part, bias)

def on_device(
    dense,
    bottom_weight,
    bottom_bias,
    cross_blocks,
    cross_bias,
    cotangent,
    in_blocks,
    out_blocks,
    live_slots,
):
    groups = lax.axis_size("tensor")
    mine = lax.axis_index("tensor")
    row_count = dense.shape[0]
    local_width = bottom_weight.shape[1]
    per_device = local_width // BLK
    capacity = -(-SLOTS // groups)
    preact = jnp.dot(dense, bottom_weight, preferred_element_type=jnp.float32) + bottom_bias
    start = jax.nn.silu(preact).astype(jnp.bfloat16)
    start_wide = start.astype(jnp.float32)
    cot_wide = cotangent.astype(jnp.float32)
    grad_mixed = cot_wide * start_wide
    grad_mixed_low = grad_mixed.astype(jnp.bfloat16)
    alive = jnp.arange(SLOTS)[None, :] < live_slots[:, None]
    alive_mine = alive[mine]
    in_owner = in_blocks // per_device
    in_local = in_blocks % per_device
    out_owner = out_blocks // per_device
    out_local = out_blocks % per_device
    in_rank = slot_ranks(in_owner, alive)
    out_rank = slot_ranks(out_owner, alive)
    combo = jnp.concatenate([start, grad_mixed_low], axis=1)
    stack_a, stack_b = ring_gather(combo, "tensor", groups)
    step_a = lambda owner: (mine - owner) % groups
    step_b = lambda owner: (owner - mine) % groups
    tables = (
        step_a(in_owner[mine]),
        step_b(in_owner[mine]),
        in_local[mine],
        step_a(out_owner[mine]),
        step_b(out_owner[mine]),
        out_local[mine] + per_device,
        alive_mine.astype(jnp.int32),
    )
    weights = lax.all_gather(cross_blocks, "dp", axis=1, tiled=True)
    parts, back_parts, block_terms = slot_products(
        stack_a.reshape(groups, -1, 2 * local_width),
        stack_b.reshape(groups, -1, 2 * local_width),
        weights,
        tuple(t.astype(jnp.int32) for t in tables),
    )
    chosen_out, filled_out = post_table(
        out_owner[mine], out_rank[mine], alive_mine, groups, capacity
    )
    chosen_in, filled_in = post_table(in_owner[mine], in_rank[mine], alive_mine, groups, capacity)
    arrived_parts, arrived_back = exchange(
        pack_parts(parts, chosen_out, filled_out),
        pack_parts(back_parts, chosen_in, filled_in),
        groups,
    )
    mixed = (
        collect_parts(
            arrived_parts, out_owner, out_local, out_rank, alive, mine, capacity, per_device
        )
        + cross_bias
    )
    cross_out = (start_wide * mixed + start_wide).astype(jnp.bfloat16)
    grad_start = collect_parts(
        arrived_back, in_owner, in_local, in_rank, alive, mine, capacity, per_device
    )
    grad_blocks = lax.psum_scatter(block_terms, "dp", scatter_dimension=1, tiled=True).astype(
        jnp.float32
    )
    grad_start = grad_start + cot_wide * mixed + cot_wide
    sigma = jax.nn.sigmoid(preact)
    grad_pre = grad_start * sigma * (1.0 + preact * (1.0 - sigma))
    grad_pre_low = grad_pre.astype(jnp.bfloat16)
    taken = dense
    side = int(round(lax.axis_size("dp") ** 0.5))
    bias_rows = jnp.zeros((8, local_width), jnp.float32)
    bias_rows = bias_rows.at[0].set(jnp.sum(grad_pre, axis=0)).at[1].set(jnp.sum(grad_mixed, axis=0))
    grad_bottom, bias_sums = reduce_rows(group_outer(taken, grad_pre_low), bias_rows, side)
    grad_bias_bottom = bias_sums[0]
    grad_bias = bias_sums[1]
    return (cross_out, grad_bottom, grad_bias_bottom, grad_blocks, grad_bias)


def solution(mesh):
    return jax.shard_map(
        on_device,
        mesh=mesh,
        in_specs=(
            P("dp", None),
            P(None, "tensor"),
            P("tensor"),
            P("tensor", "dp", None),
            P("tensor"),
            P("dp", "tensor"),
            P(),
            P(),
            P(),
        ),
        out_specs=(
            P("dp", "tensor"),
            P("dp", "tensor"),
            P("tensor"),
            P("tensor", "dp", None),
            P("tensor"),
        ),
        check_vma=False,
    )
```

```python
import functools

import jax
import jax.numpy as jnp
from jax import lax
from jax.sharding import PartitionSpec as P
from jax.experimental import pallas as pl
from jax.experimental.pallas import tpu as pltpu

BLK = 512
SLOTS = 10
RING_CHUNKS = 4


def slot_ranks(owner, alive):
    order = jnp.arange(owner.shape[1])
    earlier = order[None, :] < order[:, None]
    same = (owner[:, :, None] == owner[:, None, :]) & alive[:, None, :] & earlier[None, :, :]
    return jnp.sum(same.astype(jnp.int32), axis=2)


def post_table(owner_mine, rank_mine, alive_mine, groups, capacity):
    slot_count = owner_mine.shape[0]
    match = (
        (owner_mine[None, None, :] == jnp.arange(groups)[:, None, None])
        & (rank_mine[None, None, :] == jnp.arange(capacity)[None, :, None])
        & alive_mine[None, None, :]
    )
    chosen = jnp.sum(match.astype(jnp.int32) * jnp.arange(slot_count)[None, None, :], axis=2)
    filled = jnp.any(match, axis=2)
    return (chosen, filled)


def pack_parts(parts, chosen, filled):
    picked = jnp.take(parts, chosen.reshape(-1), axis=0)
    return picked.reshape(chosen.shape[0], chosen.shape[1] * parts.shape[1], parts.shape[2])


def collect_parts(received, owner, local, rank, alive, target, capacity, per_device):
    groups, span_rows, block_width = received.shape
    row_count = span_rows // capacity
    match = ((owner == target) & alive)[:, :, None] & (
        rank[:, :, None] == jnp.arange(capacity)[None, None, :]
    )
    matches = match[:, :, :, None] & (
        local[:, :, None, None] == jnp.arange(per_device)[None, None, None, :]
    )
    onehot = (
        jnp.sum(matches.astype(jnp.int32), axis=1)
        .reshape(groups * capacity, per_device)
        .astype(jnp.bfloat16)
    )
    flattened = received.reshape(groups * capacity, row_count, block_width)
    summed = jnp.einsum("irb,il->rlb", flattened, onehot, preferred_element_type=jnp.float32)
    return summed.reshape(row_count, per_device * block_width)

def ring_kernel(n, top, bottom, out_a, out_b, own_sem, send_sem, recv_sem):
    me = lax.axis_index("tensor")
    row = lax.axis_index("dp")
    right = lax.rem(me + 1, n)
    left = lax.rem(me + n - 1, n)
    mesh_ids = pl.DeviceIdType.MESH
    barrier = pltpu.get_barrier_semaphore()
    for neighbour in (left, right):
        pl.semaphore_signal(barrier, inc=1, device_id=(row, neighbour), device_id_type=mesh_ids)
    pl.semaphore_wait(barrier, 2)
    own_a = pltpu.make_async_copy(top, out_a.at[0], own_sem.at[0])
    own_b = pltpu.make_async_copy(bottom, out_b.at[0], own_sem.at[1])
    own_a.start()
    own_b.start()

    chunks = send_sem.shape[2]
    rows = top.shape[0] // chunks

    def piece(ref, c):
        return ref.at[pl.ds(c * rows, rows)]

    def link(out, side, step, c, target, src=None):
        return pltpu.make_async_remote_copy(
            src_ref=piece(out.at[step] if src is None else src, c),
            dst_ref=piece(out.at[step], c),
            send_sem=send_sem.at[side, step, c],
            recv_sem=recv_sem.at[side, step, c],
            device_id=(row, target),
            device_id_type=mesh_ids,
        )

    sends = []
    for step in range(1, n):
        for c in range(chunks):
            if step == 1:
                src_a, src_b = top, bottom
            else:
                link(out_a, 0, step - 1, c, right).wait_recv()
                link(out_b, 1, step - 1, c, left).wait_recv()
                src_a, src_b = out_a.at[step - 1], out_b.at[step - 1]
            copy_a = link(out_a, 0, step, c, right, src_a)
            copy_b = link(out_b, 1, step, c, left, src_b)
            copy_a.start()
            copy_b.start()
            sends += [copy_a, copy_b]
    for c in range(chunks):
        link(out_a, 0, n - 1, c, right).wait_recv()
        link(out_b, 1, n - 1, c, left).wait_recv()
    for copy in sends:
        copy.wait_send()
    own_a.wait()
    own_b.wait()


def ring_gather(x, axis, n):
    half = x.shape[0] // 2
    shape = jax.ShapeDtypeStruct((n, half, x.shape[1]), x.dtype)
    anywhere = pl.BlockSpec(memory_space=pl.ANY)
    return pl.pallas_call(
        functools.partial(ring_kernel, n),
        out_shape=[shape, shape],
        in_specs=[anywhere, anywhere],
        out_specs=[anywhere, anywhere],
        scratch_shapes=[
            pltpu.SemaphoreType.DMA((2,)),
            pltpu.SemaphoreType.DMA((2, n, RING_CHUNKS)),
            pltpu.SemaphoreType.DMA((2, n, RING_CHUNKS)),
        ],
        compiler_params=pltpu.CompilerParams(collective_id=0, has_side_effects=True),
    )(x[:half], x[half:])


def exchange_kernel(n, first, second, out_first, out_second, own_sem, send_sem, recv_sem):
    me = lax.axis_index("tensor")
    row = lax.axis_index("dp")
    mesh_ids = pl.DeviceIdType.MESH
    barrier = pltpu.get_barrier_semaphore()
    for offset in range(1, n):
        peer = lax.rem(me + offset, n)
        pl.semaphore_signal(barrier, inc=1, device_id=(row, peer), device_id_type=mesh_ids)
    pl.semaphore_wait(barrier, n - 1)
    pairs = ((first, out_first), (second, out_second))
    own = [
        pltpu.make_async_copy(src.at[me], dst.at[me], own_sem.at[side])
        for side, (src, dst) in enumerate(pairs)
    ]
    for copy in own:
        copy.start()

    def link(side, peer, slot):
        src, dst = pairs[side]
        return pltpu.make_async_remote_copy(
            src_ref=src.at[peer],
            dst_ref=dst.at[slot],
            send_sem=send_sem.at[side, peer],
            recv_sem=recv_sem.at[side, slot],
            device_id=(row, peer),
            device_id_type=mesh_ids,
        )

    sends = []
    for offset in (1, n - 1, 2, n - 2, 3, n - 3, 4)[: n - 1]:
        peer = lax.rem(me + offset, n)
        for side in range(2):
            copy = link(side, peer, me)
            copy.start()
            sends.append(copy)
    for offset in range(1, n):
        source = lax.rem(me + offset, n)
        for side in range(2):
            link(side, source, source).wait_recv()
    for copy in sends:
        copy.wait_send()
    for copy in own:
        copy.wait()


def exchange(first, second, n):
    anywhere = pl.BlockSpec(memory_space=pl.ANY)
    return pl.pallas_call(
        functools.partial(exchange_kernel, n),
        out_shape=[
            jax.ShapeDtypeStruct(first.shape, first.dtype),
            jax.ShapeDtypeStruct(second.shape, second.dtype),
        ],
        in_specs=[anywhere, anywhere],
        out_specs=[anywhere, anywhere],
        scratch_shapes=[
            pltpu.SemaphoreType.DMA((2,)),
            pltpu.SemaphoreType.DMA((2, n)),
            pltpu.SemaphoreType.DMA((2, n)),
        ],
        compiler_params=pltpu.CompilerParams(collective_id=1, has_side_effects=True),
    )(first, second)


def take_blocks(stack_a, stack_b, owner, local, me, n):
    steps, half, width = stack_a.shape
    blocks_a = stack_a.reshape(steps, half, width // BLK, BLK)
    blocks_b = stack_b.reshape(steps, half, width // BLK, BLK)
    step_a = (me - owner) % n
    step_b = (owner - me) % n
    top = blocks_a[step_a, :, local, :]
    bottom = blocks_b[step_b, :, local, :]
    return jnp.concatenate([top, bottom], axis=1)


def slot_kernel(sa_i, sb_i, bi, sa_o, sb_o, bo, live, fa, fb, ua, ub, w, part_ref, back_ref, term_ref):
    k = pl.program_id(0)
    on = live[k] > 0
    half = fa.shape[1]
    wk = w[0]
    top_in, bottom_in = fa[0], fb[0]
    top_up, bottom_up = ua[0], ub[0]
    nt = (((1,), (1,)), ((), ()))
    tn = (((0,), (0,)), ((), ()))
    for rows, src in ((slice(0, half), top_in), (slice(half, 2 * half), bottom_in)):
        value = jnp.dot(src, wk, preferred_element_type=jnp.float32)
        part_ref[0, rows, :] = jnp.where(on, value, 0.0).astype(part_ref.dtype)
    for rows, src in ((slice(0, half), top_up), (slice(half, 2 * half), bottom_up)):
        value = lax.dot_general(src, wk, nt, preferred_element_type=jnp.float32)
        back_ref[0, rows, :] = jnp.where(on, value, 0.0).astype(back_ref.dtype)
    term = lax.dot_general(top_in, top_up, tn, preferred_element_type=jnp.float32)
    term = term + lax.dot_general(bottom_in, bottom_up, tn, preferred_element_type=jnp.float32)
    term_ref[0] = jnp.where(on, term, 0.0).astype(term_ref.dtype)


def slot_products(stack_a, stack_b, weights, tables):
    slots, size, _ = weights.shape
    steps, half, width = stack_a.shape
    rows = 2 * half

    def block(step_ref, blk_ref):
        return pl.BlockSpec(
            (1, half, BLK), lambda k, *t: (t[step_ref][k], 0, t[blk_ref][k])
        )

    grid_spec = pltpu.PrefetchScalarGridSpec(
        num_scalar_prefetch=len(tables),
        grid=(slots,),
        in_specs=[
            block(0, 2),
            block(1, 2),
            block(3, 5),
            block(4, 5),
            pl.BlockSpec((1, size, size), lambda k, *t: (k, 0, 0)),
        ],
        out_specs=[
            pl.BlockSpec((1, rows, BLK), lambda k, *t: (k, 0, 0)),
            pl.BlockSpec((1, rows, BLK), lambda k, *t: (k, 0, 0)),
            pl.BlockSpec((1, size, size), lambda k, *t: (k, 0, 0)),
        ],
    )
    return pl.pallas_call(
        slot_kernel,
        grid_spec=grid_spec,
        out_shape=[
            jax.ShapeDtypeStruct((slots, rows, BLK), jnp.bfloat16),
            jax.ShapeDtypeStruct((slots, rows, BLK), jnp.bfloat16),
            jax.ShapeDtypeStruct((slots, size, size), jnp.bfloat16),
        ],
        cost_estimate=pl.CostEstimate(
            flops=6 * slots * rows * size * size,
            bytes_accessed=slots * (4 * rows * BLK + 2 * size * size) * 2,
            transcendentals=0,
        ),
    )(*tables, stack_a, stack_b, stack_a, stack_b, weights)


def outer_kernel(left, right, out):
    out[...] = lax.dot_general(
        left[...], right[...], (((0,), (0,)), ((), ())), preferred_element_type=jnp.float32
    ).astype(out.dtype)


def group_outer(left, right, tile_m=1024, tile_n=2048):
    rows, m = left.shape
    n = right.shape[1]
    return pl.pallas_call(
        outer_kernel,
        grid=(m // tile_m, n // tile_n),
        in_specs=[
            pl.BlockSpec((rows, tile_m), lambda i, j: (0, i)),
            pl.BlockSpec((rows, tile_n), lambda i, j: (0, j)),
        ],
        out_specs=pl.BlockSpec((tile_m, tile_n), lambda i, j: (i, j)),
        out_shape=jax.ShapeDtypeStruct((m, n), jnp.bfloat16),
        cost_estimate=pl.CostEstimate(
            flops=2 * rows * m * n, bytes_accessed=2 * (rows * (m + n) + m * n), transcendentals=0
        ),
    )(left, right)


def reduce_kernel(side, part, bias, out, bias_out, send1, recv1, acc1, send2, recv2, sems1, sems2,
                  bsend1, brecv1, bacc1, bsend2, brecv2, bsems1, bsems2):
    core = lax.axis_index("tensor") % 2
    me = lax.axis_index("dp")
    column = lax.axis_index("tensor")
    hi, lo = me // side, me % side
    p1 = (1 - core) * hi + core * lo
    p2 = (1 - core) * lo + core * hi
    mesh_ids = pl.DeviceIdType.MESH
    half = part.shape[3] // 2
    halves = (pl.ds(0, half), pl.ds(half, half))

    def device(q1, q2):
        q1, q2 = q1 % side, q2 % side
        return (1 - core) * (q1 * side + q2) + core * (q2 * side + q1)

    ring1 = (device(p1 + 1, p2), device(p1 - 1, p2))
    ring2 = (device(p1, p2 + 1), device(p1, p2 - 1))
    barrier = pltpu.get_barrier_semaphore()
    for target in ring1 + ring2:
        pl.semaphore_signal(barrier, inc=1, device_id=(target, column), device_id_type=mesh_ids)
    pl.semaphore_wait(barrier, 4)

    def link(send, recv, sems, d, step, target):
        return pltpu.make_async_remote_copy(
            src_ref=send.at[d, step],
            dst_ref=recv.at[d, step],
            send_sem=sems.at[0, d, step],
            recv_sem=sems.at[1, d, step],
            device_id=(target, column),
            device_id_type=mesh_ids,
        )

    def own1(k, d):
        lead = part[k, :, :, halves[d]]
        cross = part[:, k, :, halves[d]]
        return jnp.where(core == 0, lead, cross).astype(jnp.float32)

    def own2(k, d):
        return acc1[k, :, halves[d]]

    def store1(total, d):
        acc1[:, :, halves[d]] = total

    def store2(total, d):
        out[:, halves[d]] = total

    def bias1(k, d):
        return bias[:, halves[d]]

    def bias2(k, d):
        return bacc1[:, halves[d]]

    def bstore1(total, d):
        bacc1[:, halves[d]] = total

    def bstore2(total, d):
        bias_out[:, halves[d]] = total

    stages = (
        (ring1, p1, ((send1, recv1, sems1, own1, store1), (bsend1, brecv1, bsems1, bias1, bstore1))),
        (ring2, p2, ((send2, recv2, sems2, own2, store2), (bsend2, brecv2, bsems2, bias2, bstore2))),
    )
    sends = []
    for ring, pos, channels in stages:
        for step in range(side - 1):
            for d, sign in ((0, 1), (1, -1)):
                k = (pos - sign * (1 + step)) % side
                for send, recv, sems, own, _ in channels:
                    value = own(k, d)
                    if step > 0:
                        link(send, recv, sems, d, step - 1, ring[d]).wait_recv()
                        value = value + recv[d, step - 1].astype(jnp.float32)
                    send[d, step] = value.astype(send.dtype)
                    copy = link(send, recv, sems, d, step, ring[d])
                    copy.start()
                    sends.append(copy)
        for d in range(2):
            for send, recv, sems, own, store in channels:
                link(send, recv, sems, d, side - 2, ring[d]).wait_recv()
                store(own(pos, d) + recv[d, side - 2].astype(jnp.float32), d)
    for copy in sends:
        copy.wait_send()


def reduce_rows(part, bias, side):
    chunk, width = part.shape[0] // (side * side), part.shape[1]
    part = part.reshape(side, side, chunk, width)
    rows = bias.shape[0]
    vmem = pl.BlockSpec(memory_space=pltpu.VMEM)
    return pl.pallas_call(
        functools.partial(reduce_kernel, side),
        out_shape=[
            jax.ShapeDtypeStruct((chunk, width), jnp.float32),
            jax.ShapeDtypeStruct((rows, width), jnp.float32),
        ],
        in_specs=[vmem, vmem],
        out_specs=[vmem, vmem],
        scratch_shapes=[
            pltpu.VMEM((2, side - 1, side, chunk, width // 2), jnp.bfloat16),
            pltpu.VMEM((2, side - 1, side, chunk, width // 2), jnp.bfloat16),
            pltpu.VMEM((side, chunk, width), jnp.float32),
            pltpu.VMEM((2, side - 1, chunk, width // 2), jnp.bfloat16),
            pltpu.VMEM((2, side - 1, chunk, width // 2), jnp.bfloat16),
            pltpu.SemaphoreType.DMA((2, 2, side - 1)),
            pltpu.SemaphoreType.DMA((2, 2, side - 1)),
            pltpu.VMEM((2, side - 1, rows, width // 2), jnp.float32),
            pltpu.VMEM((2, side - 1, rows, width // 2), jnp.float32),
            pltpu.VMEM((rows, width), jnp.float32),
            pltpu.VMEM((2, side - 1, rows, width // 2), jnp.float32),
            pltpu.VMEM((2, side - 1, rows, width // 2), jnp.float32),
            pltpu.SemaphoreType.DMA((2, 2, side - 1)),
            pltpu.SemaphoreType.DMA((2, 2, side - 1)),
        ],
        compiler_params=pltpu.CompilerParams(
            collective_id=2, has_side_effects=True, vmem_limit_bytes=60 * 1024 * 1024
        ),
    )(part, bias)

def on_device(
    dense,
    bottom_weight,
    bottom_bias,
    cross_blocks,
    cross_bias,
    cotangent,
    in_blocks,
    out_blocks,
    live_slots,
):
    groups = lax.axis_size("tensor")
    mine = lax.axis_index("tensor")
    row_count = dense.shape[0]
    local_width = bottom_weight.shape[1]
    per_device = local_width // BLK
    capacity = -(-SLOTS // groups)
    preact = jnp.dot(dense, bottom_weight, preferred_element_type=jnp.float32) + bottom_bias
    start = jax.nn.silu(preact).astype(jnp.bfloat16)
    start_wide = start.astype(jnp.float32)
    cot_wide = cotangent.astype(jnp.float32)
    grad_mixed = cot_wide * start_wide
    grad_mixed_low = grad_mixed.astype(jnp.bfloat16)
    alive = jnp.arange(SLOTS)[None, :] < live_slots[:, None]
    alive_mine = alive[mine]
    in_owner = in_blocks // per_device
    in_local = in_blocks % per_device
    out_owner = out_blocks // per_device
    out_local = out_blocks % per_device
    in_rank = slot_ranks(in_owner, alive)
    out_rank = slot_ranks(out_owner, alive)
    combo = jnp.concatenate([start, grad_mixed_low], axis=1)
    stack_a, stack_b = ring_gather(combo, "tensor", groups)
    step_a = lambda owner: (mine - owner) % groups
    step_b = lambda owner: (owner - mine) % groups
    tables = (
        step_a(in_owner[mine]),
        step_b(in_owner[mine]),
        in_local[mine],
        step_a(out_owner[mine]),
        step_b(out_owner[mine]),
        out_local[mine] + per_device,
        alive_mine.astype(jnp.int32),
    )
    weights = lax.all_gather(cross_blocks, "dp", axis=1, tiled=True)
    parts, back_parts, block_terms = slot_products(
        stack_a.reshape(groups, -1, 2 * local_width),
        stack_b.reshape(groups, -1, 2 * local_width),
        weights,
        tuple(t.astype(jnp.int32) for t in tables),
    )
    chosen_out, filled_out = post_table(
        out_owner[mine], out_rank[mine], alive_mine, groups, capacity
    )
    chosen_in, filled_in = post_table(in_owner[mine], in_rank[mine], alive_mine, groups, capacity)
    arrived_parts, arrived_back = exchange(
        pack_parts(parts, chosen_out, filled_out),
        pack_parts(back_parts, chosen_in, filled_in),
        groups,
    )
    mixed = (
        collect_parts(
            arrived_parts, out_owner, out_local, out_rank, alive, mine, capacity, per_device
        )
        + cross_bias
    )
    cross_out = (start_wide * mixed + start_wide).astype(jnp.bfloat16)
    grad_start = collect_parts(
        arrived_back, in_owner, in_local, in_rank, alive, mine, capacity, per_device
    )
    grad_blocks = lax.psum_scatter(block_terms, "dp", scatter_dimension=1, tiled=True).astype(
        jnp.float32
    )
    grad_start = grad_start + cot_wide * mixed + cot_wide
    sigma = jax.nn.sigmoid(preact)
    grad_pre = grad_start * sigma * (1.0 + preact * (1.0 - sigma))
    grad_pre_low = grad_pre.astype(jnp.bfloat16)
    taken = dense
    side = int(round(lax.axis_size("dp") ** 0.5))
    bias_rows = jnp.zeros((8, local_width), jnp.float32)
    bias_rows = bias_rows.at[0].set(jnp.sum(grad_pre, axis=0)).at[1].set(jnp.sum(grad_mixed, axis=0))
    grad_bottom, bias_sums = reduce_rows(group_outer(taken, grad_pre_low), bias_rows, side)
    grad_bias_bottom = bias_sums[0]
    grad_bias = bias_sums[1]
    return (cross_out, grad_bottom, grad_bias_bottom, grad_blocks, grad_bias)


def solution(mesh):
    return jax.shard_map(
        on_device,
        mesh=mesh,
        in_specs=(
            P("dp", None),
            P(None, "tensor"),
            P("tensor"),
            P("tensor", "dp", None),
            P("tensor"),
            P("dp", "tensor"),
            P(),
            P(),
            P(),
        ),
        out_specs=(
            P("dp", "tensor"),
            P("dp", "tensor"),
            P("tensor"),
            P("tensor", "dp", None),
            P("tensor"),
        ),
        check_vma=False,
    )
```
